512 devices in a mesh: pair: 32 (over x, z_lo, core), row: 2 (over z_hi), col: 8 (over y).
Axes of the slice: x: 4, y: 8, z: 8 (z_hi: 2, z_lo: 4; z = z_hi * 4 + z_lo), core: 2. Of those that a mesh axis runs over, the one named last changes fastest.
Arguments:
- limbs: int32 [6, 16384, 2048], P(None, 'pair', ('row', 'col')), parts along dimension 1, may hold values from 0 to 65535
Outputs:
- products: float32 [3, 16384, 2048], P(None, 'pair', ('row', 'col')), parts along dimension 1
The draws below stay inside these ranges and needn't reach their ends.
There are 32 independent parts, one for each index of `pair`. The reference program is written for one: setup_inputs(seed, part) draws one part's arguments, and reference() takes and returns one part's arrays. A program takes and returns all parts, laid end to end along the dimension named above; each array names one. Nothing has to cross between parts.
All inputs are finite; a program needn't handle non-finite values.
Results may differ from the reference program's by a relative error of at most 0.00007.
Values sent between devices are 32-bit elements; how exact they have to be, the bound alone decides.
No kernel may reach another device: no remote copies, remote signals or barrier semaphores. Data moves between devices by JAX's collectives and lax.ppermute only.
A program may use at most 64 MiB of HBM per device.

```python
import math
import jax
import jax.numpy as jnp

ROWS = 512
COLS = 2048


def place_ends(array, rng, least, top_value):
    longest = array.shape.index(max(array.shape))
    spots = []
    for shift in (0, 1):
        where = [jax.random.randint(jax.random.fold_in(rng, axis), (), 0, length) for axis, length in enumerate(array.shape)]
        where[longest] = (where[longest] + shift) % array.shape[longest]
        spots.append(tuple(where))
    return array.at[spots[0]].set(least).at[spots[1]].set(top_value)


def setup_inputs(seed: int = 0, part: int = 0) -> dict:
    splits = jax.random.split(jax.random.key(seed), 2)
    own_keys = jax.random.split(jax.random.fold_in(splits[1], part), 2)
    return {
        "limbs": place_ends(jax.random.randint(own_keys[0], (6, ROWS, COLS), 0, 65536), jax.random.fold_in(own_keys[0], 1), 0, 65535).astype(jnp.int32),
    }


def reference(limbs):
    balanced = (limbs - 32768).astype(jnp.float32) / 32768.0
    count_all = balanced.shape[1] * balanced.shape[2]
    signal = balanced.reshape(6, count_all)
    positions = jnp.arange(count_all, dtype=jnp.int32).astype(jnp.float32)
    angles = positions * (math.pi / count_all)
    weight_cos = jnp.cos(angles)
    weight_sin = jnp.sin(angles)
    spectra = jnp.fft.fft(signal * (weight_cos - 1j * weight_sin), axis=1)
    combined = jnp.stack((spectra[0] * spectra[3], spectra[1] * spectra[4], spectra[2] * spectra[4] + spectra[0] * spectra[5]))
    restored = jnp.fft.ifft(combined, axis=1) * (weight_cos + 1j * weight_sin)
    products = jnp.real(restored) / math.sqrt(count_all)
    return products.reshape(3, balanced.shape[1], balanced.shape[2]).astype(jnp.float32)
```

```python
import math

import jax
import jax.numpy as jnp
from jax import lax
from jax.sharding import PartitionSpec as P

highest = lax.Precision.HIGHEST


def phases(multiple, period):
    angles = multiple.astype(jnp.float32) * (math.pi / period)
    return (jnp.cos(angles), -jnp.sin(angles))


def dft_table(length):
    indices = jnp.arange(length, dtype=jnp.int32)
    return phases(2 * (indices[:, None] * indices[None, :] % length), length)


def mixing(former, latter, formula):
    return jnp.einsum(formula, former, latter, precision=highest)


def multiply_pair(ar, ai, br, bi):
    return ar * br - ai * bi, ar * bi + ai * br


def body(limbs):
    groups = lax.axis_size(("row", "col"))
    number, height, narrow = limbs.shape
    breadth = narrow * groups
    limb_total = height * breadth
    half = height // 2
    local = half // groups
    device = lax.axis_index(("row", "col"))
    balanced = (limbs - 32768).astype(jnp.float32) / 32768.0

    half_index = jnp.arange(half, dtype=jnp.int32)
    row_index = jnp.arange(height, dtype=jnp.int32)
    row_cos, row_sin = phases(
        row_index[None, :] * (2 * half_index[:, None] + 1) % (2 * height), height
    )
    columns = device * narrow + jnp.arange(narrow, dtype=jnp.int32)
    turn_cos, turn_sin = phases(
        columns[None, :] * (2 * half_index[:, None] + 1) % (2 * limb_total), limb_total
    )

    real_rows = mixing(row_cos, balanced, "ja,iab->ijb")
    imag_rows = mixing(row_sin, balanced, "ja,iab->ijb")
    turned = jnp.stack(
        (
            real_rows * turn_cos - imag_rows * turn_sin,
            real_rows * turn_sin + imag_rows * turn_cos,
        )
    )
    send = turned.reshape(2, number, groups, local, narrow).transpose(2, 0, 1, 3, 4)
    received = lax.all_to_all(send, ("row", "col"), 0, 0, tiled=True)

    outer_cos, outer_sin = dft_table(groups)
    forward_block = jnp.stack(
        (
            jnp.stack((outer_cos, -outer_sin), -1),
            jnp.stack((outer_sin, outer_cos), -1),
        ),
        1,
    ).reshape(2 * groups, 2 * groups)
    mixed = jnp.dot(
        forward_block, received.reshape(2 * groups, -1), precision=highest
    ).reshape(groups, 2, number, local, narrow)
    outer_index = jnp.arange(groups, dtype=jnp.int32)
    inner_index = jnp.arange(narrow, dtype=jnp.int32)
    twist_cos, twist_sin = phases(
        2 * (outer_index[:, None] * inner_index[None, :] % breadth), breadth
    )
    twist_cos = twist_cos[:, None, None, :]
    twist_sin = twist_sin[:, None, None, :]
    mixed_re = mixed[:, 0]
    mixed_im = mixed[:, 1]
    turned_re = mixed_re * twist_cos - mixed_im * twist_sin
    turned_im = mixed_re * twist_sin + mixed_im * twist_cos
    inner_cos, inner_sin = dft_table(narrow)
    spec_re = mixing(turned_re, inner_cos, "kijq,qm->kijm") - mixing(
        turned_im, inner_sin, "kijq,qm->kijm"
    )
    spec_im = mixing(turned_re, inner_sin, "kijq,qm->kijm") + mixing(
        turned_im, inner_cos, "kijq,qm->kijm"
    )

    def spectrum(k):
        return spec_re[:, k], spec_im[:, k]

    first = multiply_pair(*spectrum(0), *spectrum(3))
    second = multiply_pair(*spectrum(1), *spectrum(4))
    third_a = multiply_pair(*spectrum(2), *spectrum(4))
    third_b = multiply_pair(*spectrum(0), *spectrum(5))
    comb_re = jnp.stack((first[0], second[0], third_a[0] + third_b[0]), axis=1)
    comb_im = jnp.stack((first[1], second[1], third_a[1] + third_b[1]), axis=1)

    back_re = mixing(comb_re, inner_cos, "kijm,qm->kijq") + mixing(
        comb_im, inner_sin, "kijm,qm->kijq"
    )
    back_im = mixing(comb_im, inner_cos, "kijm,qm->kijq") - mixing(
        comb_re, inner_sin, "kijm,qm->kijq"
    )
    untwist_re = back_re * twist_cos + back_im * twist_sin
    untwist_im = back_im * twist_cos - back_re * twist_sin
    inverse_block = jnp.stack(
        (
            jnp.stack((outer_cos, outer_sin), -1),
            jnp.stack((-outer_sin, outer_cos), -1),
        ),
        1,
    ).reshape(2 * groups, 2 * groups)
    outgoing = jnp.dot(
        inverse_block,
        jnp.stack((untwist_re, untwist_im), axis=1).reshape(2 * groups, -1),
        precision=highest,
    ).reshape(groups, 2, 3, local, narrow)
    pieces = lax.all_to_all(outgoing, ("row", "col"), 0, 0, tiled=True)

    turn_cos = turn_cos.reshape(groups, 1, local, narrow)
    turn_sin = turn_sin.reshape(groups, 1, local, narrow)
    real_part = pieces[:, 0] * turn_cos + pieces[:, 1] * turn_sin
    imag_part = pieces[:, 1] * turn_cos - pieces[:, 0] * turn_sin
    scale_factor = 2.0 / (limb_total * math.sqrt(limb_total))
    row_cos = row_cos.reshape(groups, local, height)
    row_sin = row_sin.reshape(groups, local, height)
    total = mixing(row_cos, real_part, "sja,sijb->iab") + mixing(
        row_sin, imag_part, "sja,sijb->iab"
    )
    return total * scale_factor


def solution(mesh):
    in_specs = (P(None, "pair", ("row", "col")),)
    out_specs = P(None, "pair", ("row", "col"))
    return jax.shard_map(body, mesh=mesh, in_specs=in_specs, out_specs=out_specs, check_vma=False)
```

```python
import math

import jax
import jax.numpy as jnp
from jax import lax
from jax.experimental import pallas as pl
from jax.experimental.pallas import tpu as pltpu
from jax.sharding import PartitionSpec as P

highest = lax.Precision.HIGHEST


def phases(multiple, period):
    angles = multiple.astype(jnp.float32) * (math.pi / period)
    return (jnp.cos(angles), -jnp.sin(angles))


def dft_table(length):
    indices = jnp.arange(length, dtype=jnp.int32)
    return phases(2 * (indices[:, None] * indices[None, :] % length), length)


def mixing(former, latter, formula):
    return jnp.einsum(formula, former, latter, precision=highest)


def multiply_pair(ar, ai, br, bi):
    return ar * br - ai * bi, ar * bi + ai * br


def row_kernel(limbs_ref, matrix_ref, turn_cos_ref, turn_sin_ref, out_ref):
    half = turn_cos_ref.shape[0]
    groups, _, _, local, narrow = out_ref.shape
    values = (limbs_ref[0] - 32768).astype(jnp.float32) * (1.0 / 32768.0)
    rows = jnp.dot(matrix_ref[...], values, precision=highest, preferred_element_type=jnp.float32)
    real_rows = rows[:half]
    imag_rows = rows[half:]
    turn_cos = turn_cos_ref[...]
    turn_sin = turn_sin_ref[...]
    out_ref[:, 0, 0] = (real_rows * turn_cos - imag_rows * turn_sin).reshape(groups, local, narrow)
    out_ref[:, 1, 0] = (real_rows * turn_sin + imag_rows * turn_cos).reshape(groups, local, narrow)


def row_stage(limbs, matrix, turn_cos, turn_sin, groups):
    number, height, narrow = limbs.shape
    half = turn_cos.shape[0]
    local = half // groups
    return pl.pallas_call(
        row_kernel,
        out_shape=jax.ShapeDtypeStruct((groups, 2, number, local, narrow), jnp.float32),
        grid=(number,),
        in_specs=[
            pl.BlockSpec((1, height, narrow), lambda i: (i, 0, 0)),
            pl.BlockSpec((2 * half, height), lambda i: (0, 0)),
            pl.BlockSpec((half, narrow), lambda i: (0, 0)),
            pl.BlockSpec((half, narrow), lambda i: (0, 0)),
        ],
        out_specs=pl.BlockSpec((groups, 2, 1, local, narrow), lambda i: (0, 0, i, 0, 0)),
        cost_estimate=pl.CostEstimate(
            flops=6 * 2 * 2 * half * height * narrow * number,
            transcendentals=0,
            bytes_accessed=4 * (3 * number * height * narrow + 2 * half * height),
        ),
    )(limbs, matrix, turn_cos, turn_sin)


def body(limbs):
    groups = lax.axis_size(("row", "col"))
    number, height, narrow = limbs.shape
    breadth = narrow * groups
    limb_total = height * breadth
    half = height // 2
    local = half // groups
    device = lax.axis_index(("row", "col"))

    half_index = jnp.arange(half, dtype=jnp.int32)
    row_index = jnp.arange(height, dtype=jnp.int32)
    row_cos, row_sin = phases(
        row_index[None, :] * (2 * half_index[:, None] + 1) % (2 * height), height
    )
    base_cos, base_sin = phases(device * narrow * (2 * half_index + 1), limb_total)
    lane_index = jnp.arange(narrow, dtype=jnp.int32)
    lane_cos, lane_sin = phases(lane_index[None, :] * (2 * half_index[:, None] + 1), limb_total)
    base_cos = base_cos[:, None]
    base_sin = base_sin[:, None]
    turn_cos = base_cos * lane_cos - base_sin * lane_sin
    turn_sin = base_cos * lane_sin + base_sin * lane_cos

    send = row_stage(limbs, jnp.concatenate((row_cos, row_sin), axis=0), turn_cos, turn_sin, groups)
    received = lax.all_to_all(send, ("row", "col"), 0, 0, tiled=True)

    outer_cos, outer_sin = dft_table(groups)
    forward_block = jnp.stack(
        (
            jnp.stack((outer_cos, -outer_sin), -1),
            jnp.stack((outer_sin, outer_cos), -1),
        ),
        1,
    ).reshape(2 * groups, 2 * groups)
    mixed = jnp.dot(
        forward_block, received.reshape(2 * groups, -1), precision=highest
    ).reshape(groups, 2, number, local, narrow)
    outer_index = jnp.arange(groups, dtype=jnp.int32)
    inner_index = jnp.arange(narrow, dtype=jnp.int32)
    twist_cos, twist_sin = phases(
        2 * (outer_index[:, None] * inner_index[None, :] % breadth), breadth
    )
    twist_cos = twist_cos[:, None, None, :]
    twist_sin = twist_sin[:, None, None, :]
    mixed_re = mixed[:, 0]
    mixed_im = mixed[:, 1]
    turned_re = mixed_re * twist_cos - mixed_im * twist_sin
    turned_im = mixed_re * twist_sin + mixed_im * twist_cos
    inner_cos, inner_sin = dft_table(narrow)
    spec_re = mixing(turned_re, inner_cos, "kijq,qm->kijm") - mixing(
        turned_im, inner_sin, "kijq,qm->kijm"
    )
    spec_im = mixing(turned_re, inner_sin, "kijq,qm->kijm") + mixing(
        turned_im, inner_cos, "kijq,qm->kijm"
    )

    def spectrum(k):
        return spec_re[:, k], spec_im[:, k]

    first = multiply_pair(*spectrum(0), *spectrum(3))
    second = multiply_pair(*spectrum(1), *spectrum(4))
    third_a = multiply_pair(*spectrum(2), *spectrum(4))
    third_b = multiply_pair(*spectrum(0), *spectrum(5))
    comb_re = jnp.stack((first[0], second[0], third_a[0] + third_b[0]), axis=1)
    comb_im = jnp.stack((first[1], second[1], third_a[1] + third_b[1]), axis=1)

    back_re = mixing(comb_re, inner_cos, "kijm,qm->kijq") + mixing(
        comb_im, inner_sin, "kijm,qm->kijq"
    )
    back_im = mixing(comb_im, inner_cos, "kijm,qm->kijq") - mixing(
        comb_re, inner_sin, "kijm,qm->kijq"
    )
    untwist_re = back_re * twist_cos + back_im * twist_sin
    untwist_im = back_im * twist_cos - back_re * twist_sin
    inverse_block = jnp.stack(
        (
            jnp.stack((outer_cos, outer_sin), -1),
            jnp.stack((-outer_sin, outer_cos), -1),
        ),
        1,
    ).reshape(2 * groups, 2 * groups)
    outgoing = jnp.dot(
        inverse_block,
        jnp.stack((untwist_re, untwist_im), axis=1).reshape(2 * groups, -1),
        precision=highest,
    ).reshape(groups, 2, 3, local, narrow)
    pieces = lax.all_to_all(outgoing, ("row", "col"), 0, 0, tiled=True)

    turn_cos = turn_cos.reshape(groups, 1, local, narrow)
    turn_sin = turn_sin.reshape(groups, 1, local, narrow)
    real_part = pieces[:, 0] * turn_cos + pieces[:, 1] * turn_sin
    imag_part = pieces[:, 1] * turn_cos - pieces[:, 0] * turn_sin
    scale_factor = 2.0 / (limb_total * math.sqrt(limb_total))
    row_cos = row_cos.reshape(groups, local, height)
    row_sin = row_sin.reshape(groups, local, height)
    total = mixing(row_cos, real_part, "sja,sijb->iab") + mixing(
        row_sin, imag_part, "sja,sijb->iab"
    )
    return total * scale_factor


def solution(mesh):
    in_specs = (P(None, "pair", ("row", "col")),)
    out_specs = P(None, "pair", ("row", "col"))
    return jax.shard_map(body, mesh=mesh, in_specs=in_specs, out_specs=out_specs, check_vma=False)
```

```python
import math

import jax
import jax.numpy as jnp
import ml_dtypes
import numpy as np
from jax import lax
from jax.experimental import pallas as pl
from jax.experimental.pallas import tpu as pltpu
from jax.sharding import PartitionSpec as P

highest = lax.Precision.HIGHEST


def phases(multiple, period):
    angles = multiple.astype(jnp.float32) * (math.pi / period)
    return (jnp.cos(angles), -jnp.sin(angles))


def exact_phases(multiple, period):
    angles = np.asarray(multiple, dtype=np.float64) * (math.pi / period)
    return np.cos(angles), -np.sin(angles)


def constant(table):
    return jnp.asarray(np.asarray(table, dtype=np.float32))


def dft_table(length):
    indices = np.arange(length, dtype=np.int64)
    table_cos, table_sin = exact_phases(2 * (indices[:, None] * indices[None, :] % length), length)
    return constant(table_cos), constant(table_sin)


def split_bf16(table):
    first = table.astype(ml_dtypes.bfloat16)
    second = (table - first.astype(np.float64)).astype(ml_dtypes.bfloat16)
    return np.concatenate((first, second), axis=0)


def mixing(former, latter, formula):
    return jnp.einsum(formula, former, latter, precision=highest)


def multiply_pair(ar, ai, br, bi):
    return ar * br - ai * bi, ar * bi + ai * br


def row_kernel(limbs_ref, matrix_ref, turn_cos_ref, turn_sin_ref, out_ref):
    half = turn_cos_ref.shape[0]
    groups, _, _, local, narrow = out_ref.shape
    centred = limbs_ref[0] - jnp.int32(32768)
    upper = lax.shift_right_arithmetic(centred, jnp.int32(8))
    lower = centred - upper * jnp.int32(256)
    pieces = jnp.concatenate((upper, lower), axis=1).astype(jnp.float32).astype(jnp.bfloat16)
    products = jnp.dot(matrix_ref[...], pieces, preferred_element_type=jnp.float32)
    count = 2 * half
    narrow_in = pieces.shape[1] // 2
    upper_part = products[:count, :narrow_in] + products[count:, :narrow_in]
    lower_part = products[:count, narrow_in:] + products[count:, narrow_in:]
    rows = (upper_part * 256.0 + lower_part) * (1.0 / 32768.0)
    real_rows = rows[:half]
    imag_rows = rows[half:]
    turn_cos = turn_cos_ref[...]
    turn_sin = turn_sin_ref[...]
    out_ref[:, 0, 0] = (real_rows * turn_cos - imag_rows * turn_sin).reshape(groups, local, narrow)
    out_ref[:, 1, 0] = (real_rows * turn_sin + imag_rows * turn_cos).reshape(groups, local, narrow)


def row_stage(limbs, matrix, turn_cos, turn_sin, groups):
    number, height, narrow = limbs.shape
    half = turn_cos.shape[0]
    local = half // groups
    return pl.pallas_call(
        row_kernel,
        out_shape=jax.ShapeDtypeStruct((groups, 2, number, local, narrow), jnp.float32),
        grid=(number,),
        in_specs=[
            pl.BlockSpec((1, height, narrow), lambda i: (i, 0, 0)),
            pl.BlockSpec((4 * half, height), lambda i: (0, 0)),
            pl.BlockSpec((half, narrow), lambda i: (0, 0)),
            pl.BlockSpec((half, narrow), lambda i: (0, 0)),
        ],
        out_specs=pl.BlockSpec((groups, 2, 1, local, narrow), lambda i: (0, 0, i, 0, 0)),
        cost_estimate=pl.CostEstimate(
            flops=2 * 4 * half * height * 2 * narrow * number,
            transcendentals=0,
            bytes_accessed=4 * 3 * number * height * narrow + 2 * 4 * half * height,
        ),
    )(limbs, matrix, turn_cos, turn_sin)


def body(limbs):
    groups = lax.axis_size(("row", "col"))
    number, height, narrow = limbs.shape
    breadth = narrow * groups
    limb_total = height * breadth
    half = height // 2
    local = half // groups
    device = lax.axis_index(("row", "col"))

    half_index = np.arange(half, dtype=np.int64)
    row_index = np.arange(height, dtype=np.int64)
    row_cos_exact, row_sin_exact = exact_phases(
        row_index[None, :] * (2 * half_index[:, None] + 1) % (2 * height), height
    )
    row_matrix = jnp.asarray(split_bf16(np.concatenate((row_cos_exact, row_sin_exact), axis=0)))
    row_pieces = lax.optimization_barrier(row_matrix)
    row_float = row_pieces[: 2 * half].astype(jnp.float32) + row_pieces[2 * half :].astype(jnp.float32)
    row_cos = row_float[:half]
    row_sin = row_float[half:]
    base_cos, base_sin = phases(
        device * narrow * (2 * jnp.arange(half, dtype=jnp.int32) + 1), limb_total
    )
    lane_index = np.arange(narrow, dtype=np.int64)
    lane_cos, lane_sin = exact_phases(lane_index[None, :] * (2 * half_index[:, None] + 1), limb_total)
    lane_cos = constant(lane_cos)
    lane_sin = constant(lane_sin)
    base_cos = base_cos[:, None]
    base_sin = base_sin[:, None]
    turn_cos = base_cos * lane_cos - base_sin * lane_sin
    turn_sin = base_cos * lane_sin + base_sin * lane_cos

    send = row_stage(limbs, row_matrix, turn_cos, turn_sin, groups)
    received = lax.all_to_all(send, ("row", "col"), 0, 0, tiled=True)

    outer_cos, outer_sin = dft_table(groups)
    forward_block = jnp.stack(
        (
            jnp.stack((outer_cos, -outer_sin), -1),
            jnp.stack((outer_sin, outer_cos), -1),
        ),
        1,
    ).reshape(2 * groups, 2 * groups)
    mixed = jnp.dot(
        forward_block, received.reshape(2 * groups, -1), precision=highest
    ).reshape(groups, 2, number, local, narrow)
    outer_index = np.arange(groups, dtype=np.int64)
    inner_index = np.arange(narrow, dtype=np.int64)
    twist_cos, twist_sin = exact_phases(
        2 * (outer_index[:, None] * inner_index[None, :] % breadth), breadth
    )
    twist_cos = constant(twist_cos)[:, None, None, :]
    twist_sin = constant(twist_sin)[:, None, None, :]
    mixed_re = mixed[:, 0]
    mixed_im = mixed[:, 1]
    turned_re = mixed_re * twist_cos - mixed_im * twist_sin
    turned_im = mixed_re * twist_sin + mixed_im * twist_cos
    inner_cos, inner_sin = dft_table(narrow)
    spec_re = mixing(turned_re, inner_cos, "kijq,qm->kijm") - mixing(
        turned_im, inner_sin, "kijq,qm->kijm"
    )
    spec_im = mixing(turned_re, inner_sin, "kijq,qm->kijm") + mixing(
        turned_im, inner_cos, "kijq,qm->kijm"
    )

    def spectrum(k):
        return spec_re[:, k], spec_im[:, k]

    first = multiply_pair(*spectrum(0), *spectrum(3))
    second = multiply_pair(*spectrum(1), *spectrum(4))
    third_a = multiply_pair(*spectrum(2), *spectrum(4))
    third_b = multiply_pair(*spectrum(0), *spectrum(5))
    comb_re = jnp.stack((first[0], second[0], third_a[0] + third_b[0]), axis=1)
    comb_im = jnp.stack((first[1], second[1], third_a[1] + third_b[1]), axis=1)

    back_re = mixing(comb_re, inner_cos, "kijm,qm->kijq") + mixing(
        comb_im, inner_sin, "kijm,qm->kijq"
    )
    back_im = mixing(comb_im, inner_cos, "kijm,qm->kijq") - mixing(
        comb_re, inner_sin, "kijm,qm->kijq"
    )
    untwist_re = back_re * twist_cos + back_im * twist_sin
    untwist_im = back_im * twist_cos - back_re * twist_sin
    inverse_block = jnp.stack(
        (
            jnp.stack((outer_cos, outer_sin), -1),
            jnp.stack((-outer_sin, outer_cos), -1),
        ),
        1,
    ).reshape(2 * groups, 2 * groups)
    outgoing = jnp.dot(
        inverse_block,
        jnp.stack((untwist_re, untwist_im), axis=1).reshape(2 * groups, -1),
        precision=highest,
    ).reshape(groups, 2, 3, local, narrow)
    pieces = lax.all_to_all(outgoing, ("row", "col"), 0, 0, tiled=True)

    turn_cos = turn_cos.reshape(groups, 1, local, narrow)
    turn_sin = turn_sin.reshape(groups, 1, local, narrow)
    real_part = pieces[:, 0] * turn_cos + pieces[:, 1] * turn_sin
    imag_part = pieces[:, 1] * turn_cos - pieces[:, 0] * turn_sin
    scale_factor = 2.0 / (limb_total * math.sqrt(limb_total))
    row_cos = row_cos.reshape(groups, local, height)
    row_sin = row_sin.reshape(groups, local, height)
    total = mixing(row_cos, real_part, "sja,sijb->iab") + mixing(
        row_sin, imag_part, "sja,sijb->iab"
    )
    return total * scale_factor


def solution(mesh):
    in_specs = (P(None, "pair", ("row", "col")),)
    out_specs = P(None, "pair", ("row", "col"))
    return jax.shard_map(body, mesh=mesh, in_specs=in_specs, out_specs=out_specs, check_vma=False)
```

```python
import math

import jax
import jax.numpy as jnp
import ml_dtypes
import numpy as np
from jax import lax
from jax.experimental import pallas as pl
from jax.experimental.pallas import tpu as pltpu
from jax.sharding import PartitionSpec as P

highest = lax.Precision.HIGHEST


def phases(multiple, period):
    angles = multiple.astype(jnp.float32) * (math.pi / period)
    return (jnp.cos(angles), -jnp.sin(angles))


def exact_phases(multiple, period):
    angles = np.asarray(multiple, dtype=np.float64) * (math.pi / period)
    return np.cos(angles), -np.sin(angles)


def constant(table):
    return jnp.asarray(np.asarray(table, dtype=np.float32))


def dft_table(length):
    indices = np.arange(length, dtype=np.int64)
    table_cos, table_sin = exact_phases(2 * (indices[:, None] * indices[None, :] % length), length)
    return constant(table_cos), constant(table_sin)


def split_bf16(table):
    first = table.astype(ml_dtypes.bfloat16)
    second = (table - first.astype(np.float64)).astype(ml_dtypes.bfloat16)
    return np.concatenate((first, second), axis=0)


def mixing(former, latter, formula):
    return jnp.einsum(formula, former, latter, precision=highest)


def multiply_pair(ar, ai, br, bi):
    return ar * br - ai * bi, ar * bi + ai * br


def row_kernel(limbs_ref, matrix_ref, turn_cos_ref, turn_sin_ref, out_ref):
    half = turn_cos_ref.shape[0]
    groups, _, _, local, narrow = out_ref.shape
    centred = limbs_ref[0] - jnp.int32(32768)
    upper = lax.shift_right_arithmetic(centred, jnp.int32(8))
    lower = centred - upper * jnp.int32(256)
    pieces = jnp.concatenate((upper, lower), axis=1).astype(jnp.float32).astype(jnp.bfloat16)
    products = jnp.dot(matrix_ref[...], pieces, preferred_element_type=jnp.float32)
    count = 2 * half
    narrow_in = pieces.shape[1] // 2
    upper_part = products[:count, :narrow_in] + products[count:, :narrow_in]
    lower_part = products[:count, narrow_in:] + products[count:, narrow_in:]
    rows = (upper_part * 256.0 + lower_part) * (1.0 / 32768.0)
    real_rows = rows[:half]
    imag_rows = rows[half:]
    turn_cos = turn_cos_ref[...]
    turn_sin = turn_sin_ref[...]
    out_ref[:, 0, 0] = (real_rows * turn_cos - imag_rows * turn_sin).reshape(groups, local, narrow)
    out_ref[:, 1, 0] = (real_rows * turn_sin + imag_rows * turn_cos).reshape(groups, local, narrow)


def row_stage(limbs, matrix, turn_cos, turn_sin, groups):
    number, height, narrow = limbs.shape
    half = turn_cos.shape[0]
    local = half // groups
    return pl.pallas_call(
        row_kernel,
        out_shape=jax.ShapeDtypeStruct((groups, 2, number, local, narrow), jnp.float32),
        grid=(number,),
        in_specs=[
            pl.BlockSpec((1, height, narrow), lambda i: (i, 0, 0)),
            pl.BlockSpec((4 * half, height), lambda i: (0, 0)),
            pl.BlockSpec((half, narrow), lambda i: (0, 0)),
            pl.BlockSpec((half, narrow), lambda i: (0, 0)),
        ],
        out_specs=pl.BlockSpec((groups, 2, 1, local, narrow), lambda i: (0, 0, i, 0, 0)),
        cost_estimate=pl.CostEstimate(
            flops=2 * 4 * half * height * 2 * narrow * number,
            transcendentals=0,
            bytes_accessed=4 * 3 * number * height * narrow + 2 * 4 * half * height,
        ),
    )(limbs, matrix, turn_cos, turn_sin)


def fft16(real, imag, sign):
    def dft4(a, b, c, d):
        sum_ac = (a[0] + c[0], a[1] + c[1])
        dif_ac = (a[0] - c[0], a[1] - c[1])
        sum_bd = (b[0] + d[0], b[1] + d[1])
        dif_bd = (b[0] - d[0], b[1] - d[1])
        return (
            (sum_ac[0] + sum_bd[0], sum_ac[1] + sum_bd[1]),
            (dif_ac[0] - sign * dif_bd[1], dif_ac[1] + sign * dif_bd[0]),
            (sum_ac[0] - sum_bd[0], sum_ac[1] - sum_bd[1]),
            (dif_ac[0] + sign * dif_bd[1], dif_ac[1] - sign * dif_bd[0]),
        )

    values = list(zip(real, imag))
    stage = []
    for first in range(4):
        outs = dft4(*(values[4 * second + first] for second in range(4)))
        turned = []
        for low, (re, im) in enumerate(outs):
            if first * low == 0:
                turned.append((re, im))
                continue
            angle = sign * 2.0 * math.pi * first * low / 16.0
            cos_v, sin_v = math.cos(angle), math.sin(angle)
            turned.append((re * cos_v - im * sin_v, re * sin_v + im * cos_v))
        stage.append(turned)
    result = [None] * 16
    for low in range(4):
        outs = dft4(*(stage[first][low] for first in range(4)))
        for high in range(4):
            result[low + 4 * high] = outs[high]
    return [v[0] for v in result], [v[1] for v in result]


def column_kernel(in_ref, twist_cos_ref, twist_sin_ref, forward_ref, inverse_ref, out_ref, lifted_ref, mixed_ref):
    groups, _, number, local, narrow = in_ref.shape
    tile = 8
    for operand in range(number):
        for start in range(0, local, tile):
            rows = pl.ds(start, tile)
            real = [in_ref[p, 0, operand, rows, :] for p in range(groups)]
            imag = [in_ref[p, 1, operand, rows, :] for p in range(groups)]
            real, imag = fft16(real, imag, -1.0)
            for k in range(groups):
                cos_v = twist_cos_ref[k : k + 1, :]
                sin_v = twist_sin_ref[k : k + 1, :]
                lifted_ref[k, operand, rows, :narrow] = real[k] * cos_v - imag[k] * sin_v
                lifted_ref[k, operand, rows, narrow:] = real[k] * sin_v + imag[k] * cos_v
    spectra = jnp.dot(
        lifted_ref[...].reshape(groups * number * local, 2 * narrow),
        forward_ref[...],
        precision=highest,
        preferred_element_type=jnp.float32,
    ).reshape(groups, number, local, 2 * narrow)

    def spectrum(k):
        part = spectra[:, k]
        return part[..., :narrow], part[..., narrow:]

    first = multiply_pair(*spectrum(0), *spectrum(3))
    second = multiply_pair(*spectrum(1), *spectrum(4))
    third_a = multiply_pair(*spectrum(2), *spectrum(4))
    third_b = multiply_pair(*spectrum(0), *spectrum(5))
    combined = (first, second, (third_a[0] + third_b[0], third_a[1] + third_b[1]))
    for index, (re, im) in enumerate(combined):
        mixed_ref[:, index, :, :narrow] = re
        mixed_ref[:, index, :, narrow:] = im
    outputs = mixed_ref.shape[1]
    mixed_ref[...] = jnp.dot(
        mixed_ref[...].reshape(groups * outputs * local, 2 * narrow),
        inverse_ref[...],
        precision=highest,
        preferred_element_type=jnp.float32,
    ).reshape(groups, outputs, local, 2 * narrow)
    for operand in range(outputs):
        for start in range(0, local, tile):
            rows = pl.ds(start, tile)
            real = []
            imag = []
            for k in range(groups):
                re = mixed_ref[k, operand, rows, :narrow]
                im = mixed_ref[k, operand, rows, narrow:]
                cos_v = twist_cos_ref[k : k + 1, :]
                sin_v = twist_sin_ref[k : k + 1, :]
                real.append(re * cos_v + im * sin_v)
                imag.append(im * cos_v - re * sin_v)
            real, imag = fft16(real, imag, 1.0)
            for p in range(groups):
                out_ref[p, 0, operand, rows, :] = real[p]
                out_ref[p, 1, operand, rows, :] = imag[p]


def column_stage(received, twist_cos, twist_sin, forward, inverse):
    groups, _, number, local, narrow = received.shape
    outputs = 3
    rows = groups * local
    return pl.pallas_call(
        column_kernel,
        out_shape=jax.ShapeDtypeStruct((groups, 2, outputs, local, narrow), jnp.float32),
        scratch_shapes=[
            pltpu.VMEM((groups, number, local, 2 * narrow), jnp.float32),
            pltpu.VMEM((groups, outputs, local, 2 * narrow), jnp.float32),
        ],
        cost_estimate=pl.CostEstimate(
            flops=6 * 2 * rows * (number + outputs) * (2 * narrow) ** 2,
            transcendentals=0,
            bytes_accessed=4 * rows * narrow * 2 * (number + outputs),
        ),
    )(received, twist_cos, twist_sin, forward, inverse)


def body(limbs):
    groups = lax.axis_size(("row", "col"))
    number, height, narrow = limbs.shape
    breadth = narrow * groups
    limb_total = height * breadth
    half = height // 2
    local = half // groups
    device = lax.axis_index(("row", "col"))

    half_index = np.arange(half, dtype=np.int64)
    row_index = np.arange(height, dtype=np.int64)
    row_cos_exact, row_sin_exact = exact_phases(
        row_index[None, :] * (2 * half_index[:, None] + 1) % (2 * height), height
    )
    row_matrix = jnp.asarray(split_bf16(np.concatenate((row_cos_exact, row_sin_exact), axis=0)))
    row_pieces = lax.optimization_barrier(row_matrix)
    row_float = row_pieces[: 2 * half].astype(jnp.float32) + row_pieces[2 * half :].astype(jnp.float32)
    row_cos = row_float[:half]
    row_sin = row_float[half:]
    base_cos, base_sin = phases(
        device * narrow * (2 * jnp.arange(half, dtype=jnp.int32) + 1), limb_total
    )
    lane_index = np.arange(narrow, dtype=np.int64)
    lane_cos, lane_sin = exact_phases(lane_index[None, :] * (2 * half_index[:, None] + 1), limb_total)
    lane_cos = constant(lane_cos)
    lane_sin = constant(lane_sin)
    base_cos = base_cos[:, None]
    base_sin = base_sin[:, None]
    turn_cos = base_cos * lane_cos - base_sin * lane_sin
    turn_sin = base_cos * lane_sin + base_sin * lane_cos

    send = row_stage(limbs, row_matrix, turn_cos, turn_sin, groups)
    received = lax.all_to_all(send, ("row", "col"), 0, 0, tiled=True)

    outer_index = np.arange(groups, dtype=np.int64)
    inner_index = np.arange(narrow, dtype=np.int64)
    twist_cos, twist_sin = exact_phases(
        2 * (outer_index[:, None] * inner_index[None, :] % breadth), breadth
    )
    inner_cos, inner_sin = exact_phases(2 * (inner_index[:, None] * inner_index[None, :] % narrow), narrow)
    forward = np.block([[inner_cos, inner_sin], [-inner_sin, inner_cos]])
    inverse = np.block([[inner_cos, -inner_sin], [inner_sin, inner_cos]])
    outgoing = column_stage(
        received, constant(twist_cos), constant(twist_sin), constant(forward), constant(inverse)
    )
    pieces = lax.all_to_all(outgoing, ("row", "col"), 0, 0, tiled=True)

    turn_cos = turn_cos.reshape(groups, 1, local, narrow)
    turn_sin = turn_sin.reshape(groups, 1, local, narrow)
    real_part = pieces[:, 0] * turn_cos + pieces[:, 1] * turn_sin
    imag_part = pieces[:, 1] * turn_cos - pieces[:, 0] * turn_sin
    scale_factor = 2.0 / (limb_total * math.sqrt(limb_total))
    row_cos = row_cos.reshape(groups, local, height)
    row_sin = row_sin.reshape(groups, local, height)
    total = mixing(row_cos, real_part, "sja,sijb->iab") + mixing(
        row_sin, imag_part, "sja,sijb->iab"
    )
    return total * scale_factor


def solution(mesh):
    in_specs = (P(None, "pair", ("row", "col")),)
    out_specs = P(None, "pair", ("row", "col"))
    return jax.shard_map(body, mesh=mesh, in_specs=in_specs, out_specs=out_specs, check_vma=False)
```

```python
import functools
import math

import jax
import jax.numpy as jnp
import ml_dtypes
import numpy as np
from jax import lax
from jax.experimental import pallas as pl
from jax.experimental.pallas import tpu as pltpu
from jax.sharding import PartitionSpec as P

highest = lax.Precision.HIGHEST


def phases(multiple, period):
    angles = multiple.astype(jnp.float32) * (math.pi / period)
    return (jnp.cos(angles), -jnp.sin(angles))


def exact_phases(multiple, period):
    angles = np.asarray(multiple, dtype=np.float64) * (math.pi / period)
    return np.cos(angles), -np.sin(angles)


def constant(table):
    return jnp.asarray(np.asarray(table, dtype=np.float32))


def dft_table(length):
    indices = np.arange(length, dtype=np.int64)
    table_cos, table_sin = exact_phases(2 * (indices[:, None] * indices[None, :] % length), length)
    return constant(table_cos), constant(table_sin)


def split_bf16(table):
    first = table.astype(ml_dtypes.bfloat16)
    second = (table - first.astype(np.float64)).astype(ml_dtypes.bfloat16)
    return np.concatenate((first, second), axis=0)


def mixing(former, latter, formula):
    return jnp.einsum(formula, former, latter, precision=highest)


def multiply_pair(ar, ai, br, bi):
    return ar * br - ai * bi, ar * bi + ai * br


def row_kernel(limbs_ref, matrix_ref, base_cos_ref, base_sin_ref, lane_cos_ref, lane_sin_ref, out_ref):
    number = limbs_ref.shape[0]
    half = lane_cos_ref.shape[0]
    groups, _, _, local, narrow = out_ref.shape
    turn_cos, turn_sin = turn_tables(base_cos_ref, base_sin_ref, lane_cos_ref, lane_sin_ref)
    centred = [limbs_ref[i] - jnp.int32(32768) for i in range(number)]
    upper = [lax.shift_right_arithmetic(value, jnp.int32(8)) for value in centred]
    lower = [value - top * jnp.int32(256) for value, top in zip(centred, upper)]
    pieces = jnp.concatenate(upper + lower, axis=1).astype(jnp.float32).astype(jnp.bfloat16)
    products = jnp.dot(matrix_ref[...], pieces, preferred_element_type=jnp.float32)
    count = 2 * half
    width = number * narrow
    upper_part = products[:count, :width] + products[count:, :width]
    lower_part = products[:count, width:] + products[count:, width:]
    rows = (upper_part * 256.0 + lower_part) * (1.0 / 32768.0)
    for i in range(number):
        real_rows = rows[:half, i * narrow : (i + 1) * narrow]
        imag_rows = rows[half:, i * narrow : (i + 1) * narrow]
        out_ref[:, 0, i] = (real_rows * turn_cos - imag_rows * turn_sin).reshape(groups, local, narrow)
        out_ref[:, 1, i] = (real_rows * turn_sin + imag_rows * turn_cos).reshape(groups, local, narrow)


def turn_tables(base_cos_ref, base_sin_ref, lane_cos_ref, lane_sin_ref):
    base_cos = base_cos_ref[...]
    base_sin = base_sin_ref[...]
    lane_cos = lane_cos_ref[...]
    lane_sin = lane_sin_ref[...]
    return base_cos * lane_cos - base_sin * lane_sin, base_cos * lane_sin + base_sin * lane_cos


def row_stage(limbs, matrix, tables, groups):
    number, height, narrow = limbs.shape
    half = tables[2].shape[0]
    local = half // groups
    return pl.pallas_call(
        row_kernel,
        out_shape=jax.ShapeDtypeStruct((groups, 2, number, local, narrow), jnp.float32),
        cost_estimate=pl.CostEstimate(
            flops=2 * 4 * half * height * 2 * narrow * number,
            transcendentals=0,
            bytes_accessed=4 * 3 * number * height * narrow + 2 * 4 * half * height,
        ),
    )(limbs, matrix, *tables)


def final_kernel(pieces_ref, matrix_ref, base_cos_ref, base_sin_ref, lane_cos_ref, lane_sin_ref, out_ref, *, scale):
    groups, _, outputs, local, narrow = pieces_ref.shape
    half = groups * local
    turn_cos, turn_sin = turn_tables(base_cos_ref, base_sin_ref, lane_cos_ref, lane_sin_ref)
    turn_cos = turn_cos.reshape(groups, local, narrow)
    turn_sin = turn_sin.reshape(groups, local, narrow)
    columns = []
    for i in range(outputs):
        real = pieces_ref[:, 0, i]
        imag = pieces_ref[:, 1, i]
        untwisted = jnp.stack(
            (real * turn_cos + imag * turn_sin, imag * turn_cos - real * turn_sin), axis=1
        )
        columns.append(untwisted.reshape(2 * half, narrow))
    gathered = jnp.concatenate(columns, axis=1)
    first = gathered.astype(jnp.bfloat16)
    second = (gathered - first.astype(jnp.float32)).astype(jnp.bfloat16)
    products = jnp.dot(
        matrix_ref[...], jnp.concatenate((first, second), axis=1), preferred_element_type=jnp.float32
    )
    height = matrix_ref.shape[0] // 2
    width = outputs * narrow
    small = products[height:, width:] + products[height:, :width] + products[:height, width:]
    total = (small + products[:height, :width]) * scale
    for i in range(outputs):
        out_ref[i] = total[:, i * narrow : (i + 1) * narrow]


def final_stage(pieces, matrix, tables, scale):
    groups, _, outputs, local, narrow = pieces.shape
    height = matrix.shape[0] // 2
    return pl.pallas_call(
        functools.partial(final_kernel, scale=scale),
        out_shape=jax.ShapeDtypeStruct((outputs, height, narrow), jnp.float32),
        cost_estimate=pl.CostEstimate(
            flops=2 * 4 * height * height * 2 * outputs * narrow,
            transcendentals=0,
            bytes_accessed=4 * 3 * outputs * height * narrow + 2 * 2 * height * height,
        ),
    )(pieces, matrix, *tables)


def fft16(real, imag, sign):
    def dft4(a, b, c, d):
        sum_ac = (a[0] + c[0], a[1] + c[1])
        dif_ac = (a[0] - c[0], a[1] - c[1])
        sum_bd = (b[0] + d[0], b[1] + d[1])
        dif_bd = (b[0] - d[0], b[1] - d[1])
        return (
            (sum_ac[0] + sum_bd[0], sum_ac[1] + sum_bd[1]),
            (dif_ac[0] - sign * dif_bd[1], dif_ac[1] + sign * dif_bd[0]),
            (sum_ac[0] - sum_bd[0], sum_ac[1] - sum_bd[1]),
            (dif_ac[0] + sign * dif_bd[1], dif_ac[1] - sign * dif_bd[0]),
        )

    values = list(zip(real, imag))
    stage = []
    for first in range(4):
        outs = dft4(*(values[4 * second + first] for second in range(4)))
        turned = []
        for low, (re, im) in enumerate(outs):
            if first * low == 0:
                turned.append((re, im))
                continue
            angle = sign * 2.0 * math.pi * first * low / 16.0
            cos_v, sin_v = math.cos(angle), math.sin(angle)
            turned.append((re * cos_v - im * sin_v, re * sin_v + im * cos_v))
        stage.append(turned)
    result = [None] * 16
    for low in range(4):
        outs = dft4(*(stage[first][low] for first in range(4)))
        for high in range(4):
            result[low + 4 * high] = outs[high]
    return [v[0] for v in result], [v[1] for v in result]


def column_kernel(in_ref, twist_cos_ref, twist_sin_ref, forward_ref, inverse_ref, out_ref, lifted_ref, mixed_ref):
    groups, _, number, local, narrow = in_ref.shape
    tile = 8
    for operand in range(number):
        for start in range(0, local, tile):
            rows = pl.ds(start, tile)
            real = [in_ref[p, 0, operand, rows, :] for p in range(groups)]
            imag = [in_ref[p, 1, operand, rows, :] for p in range(groups)]
            real, imag = fft16(real, imag, -1.0)
            for k in range(groups):
                cos_v = twist_cos_ref[k : k + 1, :]
                sin_v = twist_sin_ref[k : k + 1, :]
                lifted_ref[k, operand, rows, :narrow] = real[k] * cos_v - imag[k] * sin_v
                lifted_ref[k, operand, rows, narrow:] = real[k] * sin_v + imag[k] * cos_v
    spectra = jnp.dot(
        lifted_ref[...].reshape(groups * number * local, 2 * narrow),
        forward_ref[...],
        precision=highest,
        preferred_element_type=jnp.float32,
    ).reshape(groups, number, local, 2 * narrow)

    def spectrum(k):
        part = spectra[:, k]
        return part[..., :narrow], part[..., narrow:]

    first = multiply_pair(*spectrum(0), *spectrum(3))
    second = multiply_pair(*spectrum(1), *spectrum(4))
    third_a = multiply_pair(*spectrum(2), *spectrum(4))
    third_b = multiply_pair(*spectrum(0), *spectrum(5))
    combined = (first, second, (third_a[0] + third_b[0], third_a[1] + third_b[1]))
    for index, (re, im) in enumerate(combined):
        mixed_ref[:, index, :, :narrow] = re
        mixed_ref[:, index, :, narrow:] = im
    outputs = mixed_ref.shape[1]
    mixed_ref[...] = jnp.dot(
        mixed_ref[...].reshape(groups * outputs * local, 2 * narrow),
        inverse_ref[...],
        precision=highest,
        preferred_element_type=jnp.float32,
    ).reshape(groups, outputs, local, 2 * narrow)
    for operand in range(outputs):
        for start in range(0, local, tile):
            rows = pl.ds(start, tile)
            real = []
            imag = []
            for k in range(groups):
                re = mixed_ref[k, operand, rows, :narrow]
                im = mixed_ref[k, operand, rows, narrow:]
                cos_v = twist_cos_ref[k : k + 1, :]
                sin_v = twist_sin_ref[k : k + 1, :]
                real.append(re * cos_v + im * sin_v)
                imag.append(im * cos_v - re * sin_v)
            real, imag = fft16(real, imag, 1.0)
            for p in range(groups):
                out_ref[p, 0, operand, rows, :] = real[p]
                out_ref[p, 1, operand, rows, :] = imag[p]


def column_stage(received, twist_cos, twist_sin, forward, inverse):
    groups, _, number, local, narrow = received.shape
    outputs = 3
    rows = groups * local
    return pl.pallas_call(
        column_kernel,
        out_shape=jax.ShapeDtypeStruct((groups, 2, outputs, local, narrow), jnp.float32),
        scratch_shapes=[
            pltpu.VMEM((groups, number, local, 2 * narrow), jnp.float32),
            pltpu.VMEM((groups, outputs, local, 2 * narrow), jnp.float32),
        ],
        cost_estimate=pl.CostEstimate(
            flops=6 * 2 * rows * (number + outputs) * (2 * narrow) ** 2,
            transcendentals=0,
            bytes_accessed=4 * rows * narrow * 2 * (number + outputs),
        ),
    )(received, twist_cos, twist_sin, forward, inverse)


def body(limbs):
    groups = lax.axis_size(("row", "col"))
    number, height, narrow = limbs.shape
    breadth = narrow * groups
    limb_total = height * breadth
    half = height // 2
    local = half // groups
    device = lax.axis_index(("row", "col"))

    half_index = np.arange(half, dtype=np.int64)
    row_index = np.arange(height, dtype=np.int64)
    row_cos_exact, row_sin_exact = exact_phases(
        row_index[None, :] * (2 * half_index[:, None] + 1) % (2 * height), height
    )
    row_matrix = jnp.asarray(split_bf16(np.concatenate((row_cos_exact, row_sin_exact), axis=0)))
    final_table = np.stack(
        (row_cos_exact.reshape(groups, local, height), row_sin_exact.reshape(groups, local, height)), axis=1
    ).reshape(2 * half, height)
    final_matrix = jnp.asarray(split_bf16(final_table.T))
    base_cos, base_sin = phases(
        device * narrow * (2 * jnp.arange(half, dtype=jnp.int32) + 1), limb_total
    )
    lane_index = np.arange(narrow, dtype=np.int64)
    lane_cos, lane_sin = exact_phases(lane_index[None, :] * (2 * half_index[:, None] + 1), limb_total)
    tables = (base_cos[:, None], base_sin[:, None], constant(lane_cos), constant(lane_sin))

    send = row_stage(limbs, row_matrix, tables, groups)
    received = lax.all_to_all(send, ("row", "col"), 0, 0, tiled=True)

    outer_index = np.arange(groups, dtype=np.int64)
    inner_index = np.arange(narrow, dtype=np.int64)
    twist_cos, twist_sin = exact_phases(
        2 * (outer_index[:, None] * inner_index[None, :] % breadth), breadth
    )
    inner_cos, inner_sin = exact_phases(2 * (inner_index[:, None] * inner_index[None, :] % narrow), narrow)
    forward = np.block([[inner_cos, inner_sin], [-inner_sin, inner_cos]])
    inverse = np.block([[inner_cos, -inner_sin], [inner_sin, inner_cos]])
    outgoing = column_stage(
        received, constant(twist_cos), constant(twist_sin), constant(forward), constant(inverse)
    )
    pieces = lax.all_to_all(outgoing, ("row", "col"), 0, 0, tiled=True)

    scale_factor = 2.0 / (limb_total * math.sqrt(limb_total))
    return final_stage(pieces, final_matrix, tables, scale_factor)


def solution(mesh):
    in_specs = (P(None, "pair", ("row", "col")),)
    out_specs = P(None, "pair", ("row", "col"))
    return jax.shard_map(body, mesh=mesh, in_specs=in_specs, out_specs=out_specs, check_vma=False)
```

```python
import functools
import math

import jax
import jax.numpy as jnp
import ml_dtypes
import numpy as np
from jax import lax
from jax.experimental import pallas as pl
from jax.experimental.pallas import tpu as pltpu
from jax.sharding import PartitionSpec as P

highest = lax.Precision.HIGHEST


def phases(multiple, period):
    angles = multiple.astype(jnp.float32) * (math.pi / period)
    return (jnp.cos(angles), -jnp.sin(angles))


def exact_phases(multiple, period):
    angles = np.asarray(multiple, dtype=np.float64) * (math.pi / period)
    return np.cos(angles), -np.sin(angles)


def constant(table):
    return jnp.asarray(np.asarray(table, dtype=np.float32))


def dft_table(length):
    indices = np.arange(length, dtype=np.int64)
    table_cos, table_sin = exact_phases(2 * (indices[:, None] * indices[None, :] % length), length)
    return constant(table_cos), constant(table_sin)


def split_bf16(table):
    first = table.astype(ml_dtypes.bfloat16)
    second = (table - first.astype(np.float64)).astype(ml_dtypes.bfloat16)
    return np.concatenate((first, second), axis=0)


def mixing(former, latter, formula):
    return jnp.einsum(formula, former, latter, precision=highest)


def multiply_pair(ar, ai, br, bi):
    return ar * br - ai * bi, ar * bi + ai * br


def row_kernel(limbs_ref, matrix_ref, base_cos_ref, base_sin_ref, lane_cos_ref, lane_sin_ref, out_ref):
    number = limbs_ref.shape[0]
    half = lane_cos_ref.shape[0]
    groups, _, _, local, narrow = out_ref.shape
    turn_cos, turn_sin = turn_tables(base_cos_ref, base_sin_ref, lane_cos_ref, lane_sin_ref)
    centred = [limbs_ref[i] - jnp.int32(32768) for i in range(number)]
    upper = [lax.shift_right_arithmetic(value, jnp.int32(8)) for value in centred]
    lower = [value - top * jnp.int32(256) for value, top in zip(centred, upper)]
    pieces = jnp.concatenate(upper + lower, axis=1).astype(jnp.float32).astype(jnp.bfloat16)
    products = jnp.dot(matrix_ref[...], pieces, preferred_element_type=jnp.float32)
    count = 2 * half
    width = number * narrow
    upper_part = products[:count, :width] + products[count:, :width]
    lower_part = products[:count, width:] + products[count:, width:]
    rows = (upper_part * 256.0 + lower_part) * (1.0 / 32768.0)
    for i in range(number):
        real_rows = rows[:half, i * narrow : (i + 1) * narrow]
        imag_rows = rows[half:, i * narrow : (i + 1) * narrow]
        out_ref[:, 0, i] = (real_rows * turn_cos - imag_rows * turn_sin).reshape(groups, local, narrow)
        out_ref[:, 1, i] = (real_rows * turn_sin + imag_rows * turn_cos).reshape(groups, local, narrow)


def turn_tables(base_cos_ref, base_sin_ref, lane_cos_ref, lane_sin_ref):
    base_cos = base_cos_ref[...]
    base_sin = base_sin_ref[...]
    lane_cos = lane_cos_ref[...]
    lane_sin = lane_sin_ref[...]
    return base_cos * lane_cos - base_sin * lane_sin, base_cos * lane_sin + base_sin * lane_cos


def row_stage(limbs, matrix, tables, groups):
    number, height, narrow = limbs.shape
    half = tables[2].shape[0]
    local = half // groups
    return pl.pallas_call(
        row_kernel,
        out_shape=jax.ShapeDtypeStruct((groups, 2, number, local, narrow), jnp.float32),
        cost_estimate=pl.CostEstimate(
            flops=2 * 4 * half * height * 2 * narrow * number,
            transcendentals=0,
            bytes_accessed=4 * 3 * number * height * narrow + 2 * 4 * half * height,
        ),
    )(limbs, matrix, *tables)


def final_kernel(pieces_ref, matrix_ref, base_cos_ref, base_sin_ref, lane_cos_ref, lane_sin_ref, out_ref, *, scale):
    groups, _, outputs, local, narrow = pieces_ref.shape
    half = groups * local
    turn_cos, turn_sin = turn_tables(base_cos_ref, base_sin_ref, lane_cos_ref, lane_sin_ref)
    turn_cos = turn_cos.reshape(groups, local, narrow)
    turn_sin = turn_sin.reshape(groups, local, narrow)
    columns = []
    for i in range(outputs):
        real = pieces_ref[:, 0, i]
        imag = pieces_ref[:, 1, i]
        untwisted = jnp.stack(
            (real * turn_cos + imag * turn_sin, imag * turn_cos - real * turn_sin), axis=1
        )
        columns.append(untwisted.reshape(2 * half, narrow))
    gathered = jnp.concatenate(columns, axis=1)
    first = gathered.astype(jnp.bfloat16)
    second = (gathered - first.astype(jnp.float32)).astype(jnp.bfloat16)
    products = jnp.dot(
        matrix_ref[...], jnp.concatenate((first, second), axis=1), preferred_element_type=jnp.float32
    )
    height = matrix_ref.shape[0] // 2
    width = outputs * narrow
    small = products[height:, width:] + products[height:, :width] + products[:height, width:]
    total = (small + products[:height, :width]) * scale
    for i in range(outputs):
        out_ref[i] = total[:, i * narrow : (i + 1) * narrow]


def final_stage(pieces, matrix, tables, scale):
    groups, _, outputs, local, narrow = pieces.shape
    height = matrix.shape[0] // 2
    return pl.pallas_call(
        functools.partial(final_kernel, scale=scale),
        out_shape=jax.ShapeDtypeStruct((outputs, height, narrow), jnp.float32),
        cost_estimate=pl.CostEstimate(
            flops=2 * 4 * height * height * 2 * outputs * narrow,
            transcendentals=0,
            bytes_accessed=4 * 3 * outputs * height * narrow + 2 * 2 * height * height,
        ),
    )(pieces, matrix, *tables)


def fft16(real, imag, sign):
    def dft4(a, b, c, d):
        sum_ac = (a[0] + c[0], a[1] + c[1])
        dif_ac = (a[0] - c[0], a[1] - c[1])
        sum_bd = (b[0] + d[0], b[1] + d[1])
        dif_bd = (b[0] - d[0], b[1] - d[1])
        return (
            (sum_ac[0] + sum_bd[0], sum_ac[1] + sum_bd[1]),
            (dif_ac[0] - sign * dif_bd[1], dif_ac[1] + sign * dif_bd[0]),
            (sum_ac[0] - sum_bd[0], sum_ac[1] - sum_bd[1]),
            (dif_ac[0] + sign * dif_bd[1], dif_ac[1] - sign * dif_bd[0]),
        )

    values = list(zip(real, imag))
    stage = []
    for first in range(4):
        outs = dft4(*(values[4 * second + first] for second in range(4)))
        turned = []
        for low, (re, im) in enumerate(outs):
            if first * low == 0:
                turned.append((re, im))
                continue
            angle = sign * 2.0 * math.pi * first * low / 16.0
            cos_v, sin_v = math.cos(angle), math.sin(angle)
            turned.append((re * cos_v - im * sin_v, re * sin_v + im * cos_v))
        stage.append(turned)
    result = [None] * 16
    for low in range(4):
        outs = dft4(*(stage[first][low] for first in range(4)))
        for high in range(4):
            result[low + 4 * high] = outs[high]
    return [v[0] for v in result], [v[1] for v in result]


def split_dot(values, matrix_ref):
    size = matrix_ref.shape[0] // 2
    first = values.astype(jnp.bfloat16)
    second = (values - first.astype(jnp.float32)).astype(jnp.bfloat16)
    major = matrix_ref[:size]
    minor = matrix_ref[size:]
    small = jnp.dot(second, major, preferred_element_type=jnp.float32) + jnp.dot(
        first, minor, preferred_element_type=jnp.float32
    )
    return small + jnp.dot(first, major, preferred_element_type=jnp.float32)


def column_kernel(in_ref, twist_cos_ref, twist_sin_ref, forward_ref, inverse_ref, out_ref, lifted_ref, mixed_ref):
    groups, _, number, local, narrow = in_ref.shape
    tile = 8
    for operand in range(number):
        for start in range(0, local, tile):
            rows = pl.ds(start, tile)
            real = [in_ref[p, 0, operand, rows, :] for p in range(groups)]
            imag = [in_ref[p, 1, operand, rows, :] for p in range(groups)]
            real, imag = fft16(real, imag, -1.0)
            for k in range(groups):
                cos_v = twist_cos_ref[k : k + 1, :]
                sin_v = twist_sin_ref[k : k + 1, :]
                lifted_ref[k, operand, rows, :narrow] = real[k] * cos_v - imag[k] * sin_v
                lifted_ref[k, operand, rows, narrow:] = real[k] * sin_v + imag[k] * cos_v
    spectra = split_dot(
        lifted_ref[...].reshape(groups * number * local, 2 * narrow), forward_ref
    ).reshape(groups, number, local, 2 * narrow)

    def spectrum(k):
        part = spectra[:, k]
        return part[..., :narrow], part[..., narrow:]

    first = multiply_pair(*spectrum(0), *spectrum(3))
    second = multiply_pair(*spectrum(1), *spectrum(4))
    third_a = multiply_pair(*spectrum(2), *spectrum(4))
    third_b = multiply_pair(*spectrum(0), *spectrum(5))
    combined = (first, second, (third_a[0] + third_b[0], third_a[1] + third_b[1]))
    for index, (re, im) in enumerate(combined):
        mixed_ref[:, index, :, :narrow] = re
        mixed_ref[:, index, :, narrow:] = im
    outputs = mixed_ref.shape[1]
    mixed_ref[...] = split_dot(
        mixed_ref[...].reshape(groups * outputs * local, 2 * narrow), inverse_ref
    ).reshape(groups, outputs, local, 2 * narrow)
    for operand in range(outputs):
        for start in range(0, local, tile):
            rows = pl.ds(start, tile)
            real = []
            imag = []
            for k in range(groups):
                re = mixed_ref[k, operand, rows, :narrow]
                im = mixed_ref[k, operand, rows, narrow:]
                cos_v = twist_cos_ref[k : k + 1, :]
                sin_v = twist_sin_ref[k : k + 1, :]
                real.append(re * cos_v + im * sin_v)
                imag.append(im * cos_v - re * sin_v)
            real, imag = fft16(real, imag, 1.0)
            for p in range(groups):
                out_ref[p, 0, operand, rows, :] = real[p]
                out_ref[p, 1, operand, rows, :] = imag[p]


def column_stage(received, twist_cos, twist_sin, forward, inverse):
    groups, _, number, local, narrow = received.shape
    outputs = 3
    rows = groups * local
    return pl.pallas_call(
        column_kernel,
        out_shape=jax.ShapeDtypeStruct((groups, 2, outputs, local, narrow), jnp.float32),
        scratch_shapes=[
            pltpu.VMEM((groups, number, local, 2 * narrow), jnp.float32),
            pltpu.VMEM((groups, outputs, local, 2 * narrow), jnp.float32),
        ],
        cost_estimate=pl.CostEstimate(
            flops=3 * 2 * rows * (number + outputs) * (2 * narrow) ** 2,
            transcendentals=0,
            bytes_accessed=4 * rows * narrow * 2 * (number + outputs),
        ),
    )(received, twist_cos, twist_sin, forward, inverse)


def body(limbs):
    groups = lax.axis_size(("row", "col"))
    number, height, narrow = limbs.shape
    breadth = narrow * groups
    limb_total = height * breadth
    half = height // 2
    local = half // groups
    device = lax.axis_index(("row", "col"))

    half_index = np.arange(half, dtype=np.int64)
    row_index = np.arange(height, dtype=np.int64)
    row_cos_exact, row_sin_exact = exact_phases(
        row_index[None, :] * (2 * half_index[:, None] + 1) % (2 * height), height
    )
    row_matrix = jnp.asarray(split_bf16(np.concatenate((row_cos_exact, row_sin_exact), axis=0)))
    final_table = np.stack(
        (row_cos_exact.reshape(groups, local, height), row_sin_exact.reshape(groups, local, height)), axis=1
    ).reshape(2 * half, height)
    final_matrix = jnp.asarray(split_bf16(final_table.T))
    device_index = np.arange(groups, dtype=np.int64)
    base_cos, base_sin = exact_phases(
        device_index[:, None] * narrow * (2 * half_index[None, :] + 1), limb_total
    )
    base_cos = lax.dynamic_index_in_dim(constant(base_cos), device, 0, keepdims=False)
    base_sin = lax.dynamic_index_in_dim(constant(base_sin), device, 0, keepdims=False)
    lane_index = np.arange(narrow, dtype=np.int64)
    lane_cos, lane_sin = exact_phases(lane_index[None, :] * (2 * half_index[:, None] + 1), limb_total)
    tables = (base_cos[:, None], base_sin[:, None], constant(lane_cos), constant(lane_sin))

    send = row_stage(limbs, row_matrix, tables, groups)
    received = lax.all_to_all(send, ("row", "col"), 0, 0, tiled=True)

    outer_index = np.arange(groups, dtype=np.int64)
    inner_index = np.arange(narrow, dtype=np.int64)
    twist_cos, twist_sin = exact_phases(
        2 * (outer_index[:, None] * inner_index[None, :] % breadth), breadth
    )
    inner_cos, inner_sin = exact_phases(2 * (inner_index[:, None] * inner_index[None, :] % narrow), narrow)
    forward = np.block([[inner_cos, inner_sin], [-inner_sin, inner_cos]])
    inverse = np.block([[inner_cos, -inner_sin], [inner_sin, inner_cos]])
    outgoing = column_stage(
        received,
        constant(twist_cos),
        constant(twist_sin),
        jnp.asarray(split_bf16(forward)),
        jnp.asarray(split_bf16(inverse)),
    )
    pieces = lax.all_to_all(outgoing, ("row", "col"), 0, 0, tiled=True)

    scale_factor = 2.0 / (limb_total * math.sqrt(limb_total))
    return final_stage(pieces, final_matrix, tables, scale_factor)


def solution(mesh):
    in_specs = (P(None, "pair", ("row", "col")),)
    out_specs = P(None, "pair", ("row", "col"))
    return jax.shard_map(body, mesh=mesh, in_specs=in_specs, out_specs=out_specs, check_vma=False)
```

```python
import functools
import math

import jax
import jax.numpy as jnp
import ml_dtypes
import numpy as np
from jax import lax
from jax.experimental import pallas as pl
from jax.experimental.pallas import tpu as pltpu
from jax.sharding import PartitionSpec as P

highest = lax.Precision.HIGHEST


def phases(multiple, period):
    angles = multiple.astype(jnp.float32) * (math.pi / period)
    return (jnp.cos(angles), -jnp.sin(angles))


def exact_phases(multiple, period):
    angles = np.asarray(multiple, dtype=np.float64) * (math.pi / period)
    return np.cos(angles), -np.sin(angles)


def constant(table):
    return jnp.asarray(np.asarray(table, dtype=np.float32))


def dft_table(length):
    indices = np.arange(length, dtype=np.int64)
    table_cos, table_sin = exact_phases(2 * (indices[:, None] * indices[None, :] % length), length)
    return constant(table_cos), constant(table_sin)


def split_bf16(table):
    first = table.astype(ml_dtypes.bfloat16)
    second = (table - first.astype(np.float64)).astype(ml_dtypes.bfloat16)
    return np.concatenate((first, second), axis=0)


def mixing(former, latter, formula):
    return jnp.einsum(formula, former, latter, precision=highest)


def multiply_pair(ar, ai, br, bi):
    return ar * br - ai * bi, ar * bi + ai * br


def row_kernel(limbs_ref, matrix_ref, turn_cos_ref, turn_sin_ref, out_ref):
    number = limbs_ref.shape[0]
    half = turn_cos_ref.shape[0]
    groups, _, _, local, narrow = out_ref.shape
    turn_cos, turn_sin = turn_tables(turn_cos_ref, turn_sin_ref)
    centred = [limbs_ref[i] - jnp.int32(32768) for i in range(number)]
    upper = [lax.shift_right_arithmetic(value, jnp.int32(8)) for value in centred]
    lower = [value - top * jnp.int32(256) for value, top in zip(centred, upper)]
    pieces = jnp.concatenate(upper + lower, axis=1).astype(jnp.float32).astype(jnp.bfloat16)
    products = jnp.dot(matrix_ref[...], pieces, preferred_element_type=jnp.float32)
    count = 2 * half
    width = number * narrow
    upper_part = products[:count, :width] + products[count:, :width]
    lower_part = products[:count, width:] + products[count:, width:]
    rows = (upper_part * 256.0 + lower_part) * (1.0 / 32768.0)
    for i in range(number):
        real_rows = rows[:half, i * narrow : (i + 1) * narrow]
        imag_rows = rows[half:, i * narrow : (i + 1) * narrow]
        out_ref[:, 0, i] = (real_rows * turn_cos - imag_rows * turn_sin).reshape(groups, local, narrow)
        out_ref[:, 1, i] = (real_rows * turn_sin + imag_rows * turn_cos).reshape(groups, local, narrow)


def turn_tables(turn_cos_ref, turn_sin_ref):
    return turn_cos_ref[...], turn_sin_ref[...]


def row_stage(limbs, matrix, tables, groups):
    number, height, narrow = limbs.shape
    half = tables[0].shape[0]
    local = half // groups
    return pl.pallas_call(
        row_kernel,
        out_shape=jax.ShapeDtypeStruct((groups, 2, number, local, narrow), jnp.float32),
        cost_estimate=pl.CostEstimate(
            flops=2 * 4 * half * height * 2 * narrow * number,
            transcendentals=0,
            bytes_accessed=4 * 3 * number * height * narrow + 2 * 4 * half * height,
        ),
    )(limbs, matrix, *tables)


def final_kernel(pieces_ref, matrix_ref, turn_cos_ref, turn_sin_ref, out_ref, *, scale):
    groups, _, outputs, local, narrow = pieces_ref.shape
    half = groups * local
    turn_cos, turn_sin = turn_tables(turn_cos_ref, turn_sin_ref)
    turn_cos = turn_cos.reshape(groups, local, narrow)
    turn_sin = turn_sin.reshape(groups, local, narrow)
    columns = []
    for i in range(outputs):
        real = pieces_ref[:, 0, i]
        imag = pieces_ref[:, 1, i]
        untwisted = jnp.concatenate(
            (
                (real * turn_cos + imag * turn_sin).reshape(half, narrow),
                (imag * turn_cos - real * turn_sin).reshape(half, narrow),
            ),
            axis=0,
        )
        columns.append(untwisted)
    gathered = jnp.concatenate(columns, axis=1)
    first = gathered.astype(jnp.bfloat16)
    second = (gathered - first.astype(jnp.float32)).astype(jnp.bfloat16)
    products = jnp.dot(
        matrix_ref[...], jnp.concatenate((first, second), axis=1), preferred_element_type=jnp.float32
    )
    height = matrix_ref.shape[0] // 2
    width = outputs * narrow
    small = products[height:, width:] + products[height:, :width] + products[:height, width:]
    total = (small + products[:height, :width]) * scale
    for i in range(outputs):
        out_ref[i] = total[:, i * narrow : (i + 1) * narrow]


def final_stage(pieces, matrix, tables, scale):
    groups, _, outputs, local, narrow = pieces.shape
    height = matrix.shape[0] // 2
    return pl.pallas_call(
        functools.partial(final_kernel, scale=scale),
        out_shape=jax.ShapeDtypeStruct((outputs, height, narrow), jnp.float32),
        cost_estimate=pl.CostEstimate(
            flops=2 * 4 * height * height * 2 * outputs * narrow,
            transcendentals=0,
            bytes_accessed=4 * 3 * outputs * height * narrow + 2 * 2 * height * height,
        ),
    )(pieces, matrix, *tables)


def fft16(real, imag, sign):
    def dft4(a, b, c, d):
        sum_ac = (a[0] + c[0], a[1] + c[1])
        dif_ac = (a[0] - c[0], a[1] - c[1])
        sum_bd = (b[0] + d[0], b[1] + d[1])
        dif_bd = (b[0] - d[0], b[1] - d[1])
        return (
            (sum_ac[0] + sum_bd[0], sum_ac[1] + sum_bd[1]),
            (dif_ac[0] - sign * dif_bd[1], dif_ac[1] + sign * dif_bd[0]),
            (sum_ac[0] - sum_bd[0], sum_ac[1] - sum_bd[1]),
            (dif_ac[0] + sign * dif_bd[1], dif_ac[1] - sign * dif_bd[0]),
        )

    values = list(zip(real, imag))
    stage = []
    for first in range(4):
        outs = dft4(*(values[4 * second + first] for second in range(4)))
        turned = []
        for low, (re, im) in enumerate(outs):
            if first * low == 0:
                turned.append((re, im))
                continue
            angle = sign * 2.0 * math.pi * first * low / 16.0
            cos_v, sin_v = math.cos(angle), math.sin(angle)
            turned.append((re * cos_v - im * sin_v, re * sin_v + im * cos_v))
        stage.append(turned)
    result = [None] * 16
    for low in range(4):
        outs = dft4(*(stage[first][low] for first in range(4)))
        for high in range(4):
            result[low + 4 * high] = outs[high]
    return [v[0] for v in result], [v[1] for v in result]


def split_dot(values, matrix_ref):
    size = matrix_ref.shape[0] // 2
    first = values.astype(jnp.bfloat16)
    second = (values - first.astype(jnp.float32)).astype(jnp.bfloat16)
    major = matrix_ref[:size]
    minor = matrix_ref[size:]
    small = jnp.dot(second, major, preferred_element_type=jnp.float32) + jnp.dot(
        first, minor, preferred_element_type=jnp.float32
    )
    return small + jnp.dot(first, major, preferred_element_type=jnp.float32)


def column_kernel(in_ref, twist_cos_ref, twist_sin_ref, forward_ref, inverse_ref, out_ref, lifted_ref, mixed_ref):
    groups, _, number, local, narrow = in_ref.shape
    tile = 8
    for operand in range(number):
        for start in range(0, local, tile):
            rows = pl.ds(start, tile)
            real = [in_ref[p, 0, operand, rows, :] for p in range(groups)]
            imag = [in_ref[p, 1, operand, rows, :] for p in range(groups)]
            real, imag = fft16(real, imag, -1.0)
            for k in range(groups):
                cos_v = twist_cos_ref[k : k + 1, :]
                sin_v = twist_sin_ref[k : k + 1, :]
                lifted_ref[k, operand, rows, :narrow] = real[k] * cos_v - imag[k] * sin_v
                lifted_ref[k, operand, rows, narrow:] = real[k] * sin_v + imag[k] * cos_v
    spectra = split_dot(
        lifted_ref[...].reshape(groups * number * local, 2 * narrow), forward_ref
    ).reshape(groups, number, local, 2 * narrow)

    def spectrum(k):
        part = spectra[:, k]
        return part[..., :narrow], part[..., narrow:]

    first = multiply_pair(*spectrum(0), *spectrum(3))
    second = multiply_pair(*spectrum(1), *spectrum(4))
    third_a = multiply_pair(*spectrum(2), *spectrum(4))
    third_b = multiply_pair(*spectrum(0), *spectrum(5))
    combined = (first, second, (third_a[0] + third_b[0], third_a[1] + third_b[1]))
    for index, (re, im) in enumerate(combined):
        mixed_ref[:, index, :, :narrow] = re
        mixed_ref[:, index, :, narrow:] = im
    outputs = mixed_ref.shape[1]
    mixed_ref[...] = split_dot(
        mixed_ref[...].reshape(groups * outputs * local, 2 * narrow), inverse_ref
    ).reshape(groups, outputs, local, 2 * narrow)
    for operand in range(outputs):
        for start in range(0, local, tile):
            rows = pl.ds(start, tile)
            real = []
            imag = []
            for k in range(groups):
                re = mixed_ref[k, operand, rows, :narrow]
                im = mixed_ref[k, operand, rows, narrow:]
                cos_v = twist_cos_ref[k : k + 1, :]
                sin_v = twist_sin_ref[k : k + 1, :]
                real.append(re * cos_v + im * sin_v)
                imag.append(im * cos_v - re * sin_v)
            real, imag = fft16(real, imag, 1.0)
            for p in range(groups):
                out_ref[p, 0, operand, rows, :] = real[p]
                out_ref[p, 1, operand, rows, :] = imag[p]


def column_stage(received, twist_cos, twist_sin, forward, inverse):
    groups, _, number, local, narrow = received.shape
    outputs = 3
    rows = groups * local
    return pl.pallas_call(
        column_kernel,
        out_shape=jax.ShapeDtypeStruct((groups, 2, outputs, local, narrow), jnp.float32),
        scratch_shapes=[
            pltpu.VMEM((groups, number, local, 2 * narrow), jnp.float32),
            pltpu.VMEM((groups, outputs, local, 2 * narrow), jnp.float32),
        ],
        cost_estimate=pl.CostEstimate(
            flops=3 * 2 * rows * (number + outputs) * (2 * narrow) ** 2,
            transcendentals=0,
            bytes_accessed=4 * rows * narrow * 2 * (number + outputs),
        ),
    )(received, twist_cos, twist_sin, forward, inverse)


def body(limbs):
    groups = lax.axis_size(("row", "col"))
    number, height, narrow = limbs.shape
    breadth = narrow * groups
    limb_total = height * breadth
    half = height // 2
    local = half // groups
    device = lax.axis_index(("row", "col"))

    half_index = np.arange(half, dtype=np.int64)
    row_index = np.arange(height, dtype=np.int64)
    row_cos_exact, row_sin_exact = exact_phases(
        row_index[None, :] * (2 * half_index[:, None] + 1) % (2 * height), height
    )
    row_matrix = jnp.asarray(split_bf16(np.concatenate((row_cos_exact, row_sin_exact), axis=0)))
    final_matrix = jnp.asarray(split_bf16(np.concatenate((row_cos_exact, row_sin_exact), axis=0).T))
    device_index = np.arange(groups, dtype=np.int64)
    base_cos, base_sin = exact_phases(
        device_index[:, None] * narrow * (2 * half_index[None, :] + 1), limb_total
    )
    base_cos = lax.dynamic_index_in_dim(constant(base_cos), device, 0, keepdims=False)[:, None]
    base_sin = lax.dynamic_index_in_dim(constant(base_sin), device, 0, keepdims=False)[:, None]
    lane_index = np.arange(narrow, dtype=np.int64)
    lane_cos, lane_sin = exact_phases(lane_index[None, :] * (2 * half_index[:, None] + 1), limb_total)
    lane_cos = constant(lane_cos)
    lane_sin = constant(lane_sin)
    tables = (
        base_cos * lane_cos - base_sin * lane_sin,
        base_cos * lane_sin + base_sin * lane_cos,
    )

    send = row_stage(limbs, row_matrix, tables, groups)
    received = lax.all_to_all(send, ("row", "col"), 0, 0, tiled=True)

    outer_index = np.arange(groups, dtype=np.int64)
    inner_index = np.arange(narrow, dtype=np.int64)
    twist_cos, twist_sin = exact_phases(
        2 * (outer_index[:, None] * inner_index[None, :] % breadth), breadth
    )
    inner_cos, inner_sin = exact_phases(2 * (inner_index[:, None] * inner_index[None, :] % narrow), narrow)
    forward = np.block([[inner_cos, inner_sin], [-inner_sin, inner_cos]])
    inverse = np.block([[inner_cos, -inner_sin], [inner_sin, inner_cos]])
    outgoing = column_stage(
        received,
        constant(twist_cos),
        constant(twist_sin),
        jnp.asarray(split_bf16(forward)),
        jnp.asarray(split_bf16(inverse)),
    )
    pieces = lax.all_to_all(outgoing, ("row", "col"), 0, 0, tiled=True)

    scale_factor = 2.0 / (limb_total * math.sqrt(limb_total))
    return final_stage(pieces, final_matrix, tables, scale_factor)


def solution(mesh):
    in_specs = (P(None, "pair", ("row", "col")),)
    out_specs = P(None, "pair", ("row", "col"))
    return jax.shard_map(body, mesh=mesh, in_specs=in_specs, out_specs=out_specs, check_vma=False)
```

```python
import functools
import math

import jax
import jax.numpy as jnp
import ml_dtypes
import numpy as np
from jax import lax
from jax.experimental import pallas as pl
from jax.experimental.pallas import tpu as pltpu
from jax.sharding import PartitionSpec as P

highest = lax.Precision.HIGHEST


def phases(multiple, period):
    angles = multiple.astype(jnp.float32) * (math.pi / period)
    return (jnp.cos(angles), -jnp.sin(angles))


def exact_phases(multiple, period):
    angles = np.asarray(multiple, dtype=np.float64) * (math.pi / period)
    return np.cos(angles), -np.sin(angles)


def constant(table):
    return jnp.asarray(np.asarray(table, dtype=np.float32))


def dft_table(length):
    indices = np.arange(length, dtype=np.int64)
    table_cos, table_sin = exact_phases(2 * (indices[:, None] * indices[None, :] % length), length)
    return constant(table_cos), constant(table_sin)


def split_bf16(table):
    first = table.astype(ml_dtypes.bfloat16)
    second = (table - first.astype(np.float64)).astype(ml_dtypes.bfloat16)
    return np.concatenate((first, second), axis=0)


def mixing(former, latter, formula):
    return jnp.einsum(formula, former, latter, precision=highest)


def multiply_pair(ar, ai, br, bi):
    return ar * br - ai * bi, ar * bi + ai * br


def row_kernel(limbs_ref, matrix_ref, turn_cos_ref, turn_sin_ref, out_ref):
    number = limbs_ref.shape[0]
    half = turn_cos_ref.shape[0]
    groups, _, _, local, narrow = out_ref.shape
    turn_cos, turn_sin = turn_tables(turn_cos_ref, turn_sin_ref)
    centred = [limbs_ref[i] - jnp.int32(32768) for i in range(number)]
    upper = [lax.shift_right_arithmetic(value, jnp.int32(8)) for value in centred]
    lower = [value - top * jnp.int32(256) for value, top in zip(centred, upper)]
    pieces = jnp.concatenate(upper + lower, axis=1).astype(jnp.float32).astype(jnp.bfloat16)
    products = jnp.dot(matrix_ref[...], pieces, preferred_element_type=jnp.float32)
    count = 2 * half
    width = number * narrow
    upper_part = products[:count, :width] + products[count:, :width]
    lower_part = products[:count, width:] + products[count:, width:]
    rows = (upper_part * 256.0 + lower_part) * (1.0 / 32768.0)
    for i in range(number):
        real_rows = rows[:half, i * narrow : (i + 1) * narrow]
        imag_rows = rows[half:, i * narrow : (i + 1) * narrow]
        out_ref[:, 0, i] = (real_rows * turn_cos - imag_rows * turn_sin).reshape(groups, local, narrow)
        out_ref[:, 1, i] = (real_rows * turn_sin + imag_rows * turn_cos).reshape(groups, local, narrow)


def turn_tables(turn_cos_ref, turn_sin_ref):
    return turn_cos_ref[...], turn_sin_ref[...]


def row_stage(limbs, matrix, tables, groups):
    number, height, narrow = limbs.shape
    half = tables[0].shape[0]
    local = half // groups
    return pl.pallas_call(
        row_kernel,
        out_shape=jax.ShapeDtypeStruct((groups, 2, number, local, narrow), jnp.float32),
        cost_estimate=pl.CostEstimate(
            flops=2 * 4 * half * height * 2 * narrow * number,
            transcendentals=0,
            bytes_accessed=4 * 3 * number * height * narrow + 2 * 4 * half * height,
        ),
    )(limbs, matrix, *tables)


def final_kernel(pieces_ref, matrix_ref, turn_cos_ref, turn_sin_ref, out_ref, *, scale):
    groups, _, outputs, local, narrow = pieces_ref.shape
    half = groups * local
    turn_cos, turn_sin = turn_tables(turn_cos_ref, turn_sin_ref)
    turn_cos = turn_cos.reshape(groups, local, narrow)
    turn_sin = turn_sin.reshape(groups, local, narrow)
    columns = []
    for i in range(outputs):
        real = pieces_ref[:, 0, i]
        imag = pieces_ref[:, 1, i]
        untwisted = jnp.concatenate(
            (
                (real * turn_cos + imag * turn_sin).reshape(half, narrow),
                (imag * turn_cos - real * turn_sin).reshape(half, narrow),
            ),
            axis=0,
        )
        columns.append(untwisted)
    gathered = jnp.concatenate(columns, axis=1)
    first = gathered.astype(jnp.bfloat16)
    second = (gathered - first.astype(jnp.float32)).astype(jnp.bfloat16)
    products = jnp.dot(
        matrix_ref[...], jnp.concatenate((first, second), axis=1), preferred_element_type=jnp.float32
    )
    height = matrix_ref.shape[0] // 2
    width = outputs * narrow
    small = products[height:, width:] + products[height:, :width] + products[:height, width:]
    total = (small + products[:height, :width]) * scale
    for i in range(outputs):
        out_ref[i] = total[:, i * narrow : (i + 1) * narrow]


def final_stage(pieces, matrix, tables, scale):
    groups, _, outputs, local, narrow = pieces.shape
    height = matrix.shape[0] // 2
    return pl.pallas_call(
        functools.partial(final_kernel, scale=scale),
        out_shape=jax.ShapeDtypeStruct((outputs, height, narrow), jnp.float32),
        cost_estimate=pl.CostEstimate(
            flops=2 * 4 * height * height * 2 * outputs * narrow,
            transcendentals=0,
            bytes_accessed=4 * 3 * outputs * height * narrow + 2 * 2 * height * height,
        ),
    )(pieces, matrix, *tables)


def fft16(real, imag, sign):
    def dft4(a, b, c, d):
        sum_ac = (a[0] + c[0], a[1] + c[1])
        dif_ac = (a[0] - c[0], a[1] - c[1])
        sum_bd = (b[0] + d[0], b[1] + d[1])
        dif_bd = (b[0] - d[0], b[1] - d[1])
        return (
            (sum_ac[0] + sum_bd[0], sum_ac[1] + sum_bd[1]),
            (dif_ac[0] - sign * dif_bd[1], dif_ac[1] + sign * dif_bd[0]),
            (sum_ac[0] - sum_bd[0], sum_ac[1] - sum_bd[1]),
            (dif_ac[0] + sign * dif_bd[1], dif_ac[1] - sign * dif_bd[0]),
        )

    values = list(zip(real, imag))
    stage = []
    for first in range(4):
        outs = dft4(*(values[4 * second + first] for second in range(4)))
        turned = []
        for low, (re, im) in enumerate(outs):
            if first * low == 0:
                turned.append((re, im))
                continue
            angle = sign * 2.0 * math.pi * first * low / 16.0
            cos_v, sin_v = math.cos(angle), math.sin(angle)
            turned.append((re * cos_v - im * sin_v, re * sin_v + im * cos_v))
        stage.append(turned)
    result = [None] * 16
    for low in range(4):
        outs = dft4(*(stage[first][low] for first in range(4)))
        for high in range(4):
            result[low + 4 * high] = outs[high]
    return [v[0] for v in result], [v[1] for v in result]


def split_dot(values, matrix_ref):
    size = matrix_ref.shape[0] // 2
    first = values.astype(jnp.bfloat16)
    second = (values - first.astype(jnp.float32)).astype(jnp.bfloat16)
    major = matrix_ref[:size]
    minor = matrix_ref[size:]
    small = jnp.dot(second, major, preferred_element_type=jnp.float32) + jnp.dot(
        first, minor, preferred_element_type=jnp.float32
    )
    return small + jnp.dot(first, major, preferred_element_type=jnp.float32)


def column_kernel(in_ref, twist_cos_ref, twist_sin_ref, forward_ref, inverse_ref, out_ref, lifted_ref, mixed_ref):
    groups, _, number, local, narrow = in_ref.shape
    tile = 8
    for operand in range(number):
        for start in range(0, local, tile):
            rows = pl.ds(start, tile)
            real = [in_ref[p, 0, operand, rows, :] for p in range(groups)]
            imag = [in_ref[p, 1, operand, rows, :] for p in range(groups)]
            real, imag = fft16(real, imag, -1.0)
            for k in range(groups):
                cos_v = twist_cos_ref[k : k + 1, :]
                sin_v = twist_sin_ref[k : k + 1, :]
                lifted_ref[k, operand, rows, :narrow] = real[k] * cos_v - imag[k] * sin_v
                lifted_ref[k, operand, rows, narrow:] = real[k] * sin_v + imag[k] * cos_v
    spectra = split_dot(
        lifted_ref[...].reshape(groups * number * local, 2 * narrow), forward_ref
    ).reshape(groups, number, local, 2 * narrow)

    def spectrum(k):
        part = spectra[:, k]
        return part[..., :narrow], part[..., narrow:]

    first = multiply_pair(*spectrum(0), *spectrum(3))
    second = multiply_pair(*spectrum(1), *spectrum(4))
    third_a = multiply_pair(*spectrum(2), *spectrum(4))
    third_b = multiply_pair(*spectrum(0), *spectrum(5))
    combined = (first, second, (third_a[0] + third_b[0], third_a[1] + third_b[1]))
    for index, (re, im) in enumerate(combined):
        mixed_ref[:, index, :, :narrow] = re
        mixed_ref[:, index, :, narrow:] = im
    outputs = mixed_ref.shape[1]
    mixed_ref[...] = split_dot(
        mixed_ref[...].reshape(groups * outputs * local, 2 * narrow), inverse_ref
    ).reshape(groups, outputs, local, 2 * narrow)
    for operand in range(outputs):
        for start in range(0, local, tile):
            rows = pl.ds(start, tile)
            real = []
            imag = []
            for k in range(groups):
                re = mixed_ref[k, operand, rows, :narrow]
                im = mixed_ref[k, operand, rows, narrow:]
                cos_v = twist_cos_ref[k : k + 1, :]
                sin_v = twist_sin_ref[k : k + 1, :]
                real.append(re * cos_v + im * sin_v)
                imag.append(im * cos_v - re * sin_v)
            real, imag = fft16(real, imag, 1.0)
            for p in range(groups):
                out_ref[p, 0, operand, rows, :] = real[p]
                out_ref[p, 1, operand, rows, :] = imag[p]


def column_stage(received, twist_cos, twist_sin, forward, inverse):
    groups, _, number, local, narrow = received.shape
    outputs = 3
    rows = groups * local
    return pl.pallas_call(
        column_kernel,
        out_shape=jax.ShapeDtypeStruct((groups, 2, outputs, local, narrow), jnp.float32),
        scratch_shapes=[
            pltpu.VMEM((groups, number, local, 2 * narrow), jnp.float32),
            pltpu.VMEM((groups, outputs, local, 2 * narrow), jnp.float32),
        ],
        cost_estimate=pl.CostEstimate(
            flops=3 * 2 * rows * (number + outputs) * (2 * narrow) ** 2,
            transcendentals=0,
            bytes_accessed=4 * rows * narrow * 2 * (number + outputs),
        ),
    )(received, twist_cos, twist_sin, forward, inverse)


def body(limbs):
    groups = lax.axis_size(("row", "col"))
    number, height, narrow = limbs.shape
    breadth = narrow * groups
    limb_total = height * breadth
    half = height // 2
    local = half // groups
    device = lax.axis_index(("row", "col"))

    half_index = np.arange(half, dtype=np.int64)
    row_index = np.arange(height, dtype=np.int64)
    row_cos_exact, row_sin_exact = exact_phases(
        row_index[None, :] * (2 * half_index[:, None] + 1) % (2 * height), height
    )
    row_matrix = jnp.asarray(split_bf16(np.concatenate((row_cos_exact, row_sin_exact), axis=0)))
    final_matrix = jnp.asarray(split_bf16(np.concatenate((row_cos_exact, row_sin_exact), axis=0).T))
    device_index = np.arange(groups, dtype=np.int64)
    base_cos, base_sin = exact_phases(
        device_index[:, None] * narrow * (2 * half_index[None, :] + 1), limb_total
    )
    chooser = (
        lax.broadcasted_iota(jnp.int32, (groups, narrow), 0) == device
    ).astype(jnp.float32)
    base_cos = jnp.dot(constant(base_cos.T), chooser, precision=highest)
    base_sin = jnp.dot(constant(base_sin.T), chooser, precision=highest)
    lane_index = np.arange(narrow, dtype=np.int64)
    lane_cos, lane_sin = exact_phases(lane_index[None, :] * (2 * half_index[:, None] + 1), limb_total)
    lane_cos = constant(lane_cos)
    lane_sin = constant(lane_sin)
    tables = (
        base_cos * lane_cos - base_sin * lane_sin,
        base_cos * lane_sin + base_sin * lane_cos,
    )

    send = row_stage(limbs, row_matrix, tables, groups)
    received = lax.all_to_all(send, ("row", "col"), 0, 0, tiled=True)

    outer_index = np.arange(groups, dtype=np.int64)
    inner_index = np.arange(narrow, dtype=np.int64)
    twist_cos, twist_sin = exact_phases(
        2 * (outer_index[:, None] * inner_index[None, :] % breadth), breadth
    )
    inner_cos, inner_sin = exact_phases(2 * (inner_index[:, None] * inner_index[None, :] % narrow), narrow)
    forward = np.block([[inner_cos, inner_sin], [-inner_sin, inner_cos]])
    inverse = np.block([[inner_cos, -inner_sin], [inner_sin, inner_cos]])
    outgoing = column_stage(
        received,
        constant(twist_cos),
        constant(twist_sin),
        jnp.asarray(split_bf16(forward)),
        jnp.asarray(split_bf16(inverse)),
    )
    pieces = lax.all_to_all(outgoing, ("row", "col"), 0, 0, tiled=True)

    scale_factor = 2.0 / (limb_total * math.sqrt(limb_total))
    return final_stage(pieces, final_matrix, tables, scale_factor)


def solution(mesh):
    in_specs = (P(None, "pair", ("row", "col")),)
    out_specs = P(None, "pair", ("row", "col"))
    return jax.shard_map(body, mesh=mesh, in_specs=in_specs, out_specs=out_specs, check_vma=False)
```

```python
import functools
import math

import jax
import jax.numpy as jnp
import ml_dtypes
import numpy as np
from jax import lax
from jax.experimental import pallas as pl
from jax.experimental.pallas import tpu as pltpu
from jax.sharding import PartitionSpec as P

highest = lax.Precision.HIGHEST


def phases(multiple, period):
    angles = multiple.astype(jnp.float32) * (math.pi / period)
    return (jnp.cos(angles), -jnp.sin(angles))


def exact_phases(multiple, period):
    angles = np.asarray(multiple, dtype=np.float64) * (math.pi / period)
    return np.cos(angles), -np.sin(angles)


def constant(table):
    return jnp.asarray(np.asarray(table, dtype=np.float32))


def dft_table(length):
    indices = np.arange(length, dtype=np.int64)
    table_cos, table_sin = exact_phases(2 * (indices[:, None] * indices[None, :] % length), length)
    return constant(table_cos), constant(table_sin)


def split_bf16(table):
    first = table.astype(ml_dtypes.bfloat16)
    second = (table - first.astype(np.float64)).astype(ml_dtypes.bfloat16)
    return np.concatenate((first, second), axis=0)


def mixing(former, latter, formula):
    return jnp.einsum(formula, former, latter, precision=highest)


def multiply_pair(ar, ai, br, bi):
    return ar * br - ai * bi, ar * bi + ai * br


def row_kernel(limbs_ref, matrix_ref, chooser_ref, base_cos_ref, base_sin_ref, lane_cos_ref, lane_sin_ref, out_ref):
    number = limbs_ref.shape[0]
    half = lane_cos_ref.shape[0]
    groups, _, _, local, narrow = out_ref.shape
    turn_cos, turn_sin = turn_tables(chooser_ref, base_cos_ref, base_sin_ref, lane_cos_ref, lane_sin_ref)
    centred = [limbs_ref[i] - jnp.int32(32768) for i in range(number)]
    upper = [lax.shift_right_arithmetic(value, jnp.int32(8)) for value in centred]
    lower = [value - top * jnp.int32(256) for value, top in zip(centred, upper)]
    pieces = jnp.concatenate(upper + lower, axis=1).astype(jnp.float32).astype(jnp.bfloat16)
    products = jnp.dot(matrix_ref[...], pieces, preferred_element_type=jnp.float32)
    count = 2 * half
    width = number * narrow
    upper_part = products[:count, :width] + products[count:, :width]
    lower_part = products[:count, width:] + products[count:, width:]
    rows = (upper_part * 256.0 + lower_part) * (1.0 / 32768.0)
    for i in range(number):
        real_rows = rows[:half, i * narrow : (i + 1) * narrow]
        imag_rows = rows[half:, i * narrow : (i + 1) * narrow]
        out_ref[:, 0, i] = (real_rows * turn_cos - imag_rows * turn_sin).reshape(groups, local, narrow)
        out_ref[:, 1, i] = (real_rows * turn_sin + imag_rows * turn_cos).reshape(groups, local, narrow)


def turn_tables(chooser_ref, base_cos_ref, base_sin_ref, lane_cos_ref, lane_sin_ref):
    pick = chooser_ref[...]
    base_cos = jnp.sum(base_cos_ref[...] * pick, axis=1, keepdims=True)
    base_sin = jnp.sum(base_sin_ref[...] * pick, axis=1, keepdims=True)
    lane_cos = lane_cos_ref[...]
    lane_sin = lane_sin_ref[...]
    return base_cos * lane_cos - base_sin * lane_sin, base_cos * lane_sin + base_sin * lane_cos


def row_stage(limbs, matrix, tables, groups):
    number, height, narrow = limbs.shape
    half = tables[3].shape[0]
    local = half // groups
    return pl.pallas_call(
        row_kernel,
        out_shape=jax.ShapeDtypeStruct((groups, 2, number, local, narrow), jnp.float32),
        cost_estimate=pl.CostEstimate(
            flops=2 * 4 * half * height * 2 * narrow * number,
            transcendentals=0,
            bytes_accessed=4 * 3 * number * height * narrow + 2 * 4 * half * height,
        ),
    )(limbs, matrix, *tables)


def final_kernel(pieces_ref, matrix_ref, chooser_ref, base_cos_ref, base_sin_ref, lane_cos_ref, lane_sin_ref, out_ref, *, scale):
    groups, _, outputs, local, narrow = pieces_ref.shape
    half = groups * local
    turn_cos, turn_sin = turn_tables(chooser_ref, base_cos_ref, base_sin_ref, lane_cos_ref, lane_sin_ref)
    turn_cos = turn_cos.reshape(groups, local, narrow)
    turn_sin = turn_sin.reshape(groups, local, narrow)
    columns = []
    for i in range(outputs):
        real = pieces_ref[:, 0, i]
        imag = pieces_ref[:, 1, i]
        untwisted = jnp.concatenate(
            (
                (real * turn_cos + imag * turn_sin).reshape(half, narrow),
                (imag * turn_cos - real * turn_sin).reshape(half, narrow),
            ),
            axis=0,
        )
        columns.append(untwisted)
    gathered = jnp.concatenate(columns, axis=1)
    first = gathered.astype(jnp.bfloat16)
    second = (gathered - first.astype(jnp.float32)).astype(jnp.bfloat16)
    products = jnp.dot(
        matrix_ref[...], jnp.concatenate((first, second), axis=1), preferred_element_type=jnp.float32
    )
    height = matrix_ref.shape[0] // 2
    width = outputs * narrow
    small = products[height:, width:] + products[height:, :width] + products[:height, width:]
    total = (small + products[:height, :width]) * scale
    for i in range(outputs):
        out_ref[i] = total[:, i * narrow : (i + 1) * narrow]


def final_stage(pieces, matrix, tables, scale):
    groups, _, outputs, local, narrow = pieces.shape
    height = matrix.shape[0] // 2
    return pl.pallas_call(
        functools.partial(final_kernel, scale=scale),
        out_shape=jax.ShapeDtypeStruct((outputs, height, narrow), jnp.float32),
        cost_estimate=pl.CostEstimate(
            flops=2 * 4 * height * height * 2 * outputs * narrow,
            transcendentals=0,
            bytes_accessed=4 * 3 * outputs * height * narrow + 2 * 2 * height * height,
        ),
    )(pieces, matrix, *tables)


def fft16(real, imag, sign):
    def dft4(a, b, c, d):
        sum_ac = (a[0] + c[0], a[1] + c[1])
        dif_ac = (a[0] - c[0], a[1] - c[1])
        sum_bd = (b[0] + d[0], b[1] + d[1])
        dif_bd = (b[0] - d[0], b[1] - d[1])
        return (
            (sum_ac[0] + sum_bd[0], sum_ac[1] + sum_bd[1]),
            (dif_ac[0] - sign * dif_bd[1], dif_ac[1] + sign * dif_bd[0]),
            (sum_ac[0] - sum_bd[0], sum_ac[1] - sum_bd[1]),
            (dif_ac[0] + sign * dif_bd[1], dif_ac[1] - sign * dif_bd[0]),
        )

    values = list(zip(real, imag))
    stage = []
    for first in range(4):
        outs = dft4(*(values[4 * second + first] for second in range(4)))
        turned = []
        for low, (re, im) in enumerate(outs):
            if first * low == 0:
                turned.append((re, im))
                continue
            angle = sign * 2.0 * math.pi * first * low / 16.0
            cos_v, sin_v = math.cos(angle), math.sin(angle)
            turned.append((re * cos_v - im * sin_v, re * sin_v + im * cos_v))
        stage.append(turned)
    result = [None] * 16
    for low in range(4):
        outs = dft4(*(stage[first][low] for first in range(4)))
        for high in range(4):
            result[low + 4 * high] = outs[high]
    return [v[0] for v in result], [v[1] for v in result]


def split_dot(values, matrix_ref):
    size = matrix_ref.shape[0] // 2
    first = values.astype(jnp.bfloat16)
    second = (values - first.astype(jnp.float32)).astype(jnp.bfloat16)
    major = matrix_ref[:size]
    minor = matrix_ref[size:]
    small = jnp.dot(second, major, preferred_element_type=jnp.float32) + jnp.dot(
        first, minor, preferred_element_type=jnp.float32
    )
    return small + jnp.dot(first, major, preferred_element_type=jnp.float32)


def column_kernel(in_ref, twist_cos_ref, twist_sin_ref, forward_ref, inverse_ref, out_ref, lifted_ref, mixed_ref):
    groups, _, number, local, narrow = in_ref.shape
    tile = 8
    for operand in range(number):
        for start in range(0, local, tile):
            rows = pl.ds(start, tile)
            real = [in_ref[p, 0, operand, rows, :] for p in range(groups)]
            imag = [in_ref[p, 1, operand, rows, :] for p in range(groups)]
            real, imag = fft16(real, imag, -1.0)
            for k in range(groups):
                cos_v = twist_cos_ref[k : k + 1, :]
                sin_v = twist_sin_ref[k : k + 1, :]
                lifted_ref[k, operand, rows, :narrow] = real[k] * cos_v - imag[k] * sin_v
                lifted_ref[k, operand, rows, narrow:] = real[k] * sin_v + imag[k] * cos_v
    spectra = split_dot(
        lifted_ref[...].reshape(groups * number * local, 2 * narrow), forward_ref
    ).reshape(groups, number, local, 2 * narrow)

    def spectrum(k):
        part = spectra[:, k]
        return part[..., :narrow], part[..., narrow:]

    first = multiply_pair(*spectrum(0), *spectrum(3))
    second = multiply_pair(*spectrum(1), *spectrum(4))
    third_a = multiply_pair(*spectrum(2), *spectrum(4))
    third_b = multiply_pair(*spectrum(0), *spectrum(5))
    combined = (first, second, (third_a[0] + third_b[0], third_a[1] + third_b[1]))
    for index, (re, im) in enumerate(combined):
        mixed_ref[:, index, :, :narrow] = re
        mixed_ref[:, index, :, narrow:] = im
    outputs = mixed_ref.shape[1]
    mixed_ref[...] = split_dot(
        mixed_ref[...].reshape(groups * outputs * local, 2 * narrow), inverse_ref
    ).reshape(groups, outputs, local, 2 * narrow)
    for operand in range(outputs):
        for start in range(0, local, tile):
            rows = pl.ds(start, tile)
            real = []
            imag = []
            for k in range(groups):
                re = mixed_ref[k, operand, rows, :narrow]
                im = mixed_ref[k, operand, rows, narrow:]
                cos_v = twist_cos_ref[k : k + 1, :]
                sin_v = twist_sin_ref[k : k + 1, :]
                real.append(re * cos_v + im * sin_v)
                imag.append(im * cos_v - re * sin_v)
            real, imag = fft16(real, imag, 1.0)
            for p in range(groups):
                out_ref[p, 0, operand, rows, :] = real[p]
                out_ref[p, 1, operand, rows, :] = imag[p]


def column_stage(received, twist_cos, twist_sin, forward, inverse):
    groups, _, number, local, narrow = received.shape
    outputs = 3
    rows = groups * local
    return pl.pallas_call(
        column_kernel,
        out_shape=jax.ShapeDtypeStruct((groups, 2, outputs, local, narrow), jnp.float32),
        scratch_shapes=[
            pltpu.VMEM((groups, number, local, 2 * narrow), jnp.float32),
            pltpu.VMEM((groups, outputs, local, 2 * narrow), jnp.float32),
        ],
        cost_estimate=pl.CostEstimate(
            flops=3 * 2 * rows * (number + outputs) * (2 * narrow) ** 2,
            transcendentals=0,
            bytes_accessed=4 * rows * narrow * 2 * (number + outputs),
        ),
    )(received, twist_cos, twist_sin, forward, inverse)


def body(limbs):
    groups = lax.axis_size(("row", "col"))
    number, height, narrow = limbs.shape
    breadth = narrow * groups
    limb_total = height * breadth
    half = height // 2
    local = half // groups
    device = lax.axis_index(("row", "col"))

    half_index = np.arange(half, dtype=np.int64)
    row_index = np.arange(height, dtype=np.int64)
    row_cos_exact, row_sin_exact = exact_phases(
        row_index[None, :] * (2 * half_index[:, None] + 1) % (2 * height), height
    )
    row_matrix = jnp.asarray(split_bf16(np.concatenate((row_cos_exact, row_sin_exact), axis=0)))
    final_matrix = jnp.asarray(split_bf16(np.concatenate((row_cos_exact, row_sin_exact), axis=0).T))
    device_index = np.arange(groups, dtype=np.int64)
    base_cos, base_sin = exact_phases(
        device_index[:, None] * narrow * (2 * half_index[None, :] + 1), limb_total
    )
    base_cos_table = np.zeros((half, narrow))
    base_sin_table = np.zeros((half, narrow))
    base_cos_table[:, :groups] = base_cos.T
    base_sin_table[:, :groups] = base_sin.T
    chooser = (lax.broadcasted_iota(jnp.int32, (1, narrow), 1) == device).astype(jnp.float32)
    lane_index = np.arange(narrow, dtype=np.int64)
    lane_cos, lane_sin = exact_phases(lane_index[None, :] * (2 * half_index[:, None] + 1), limb_total)
    tables = (
        chooser,
        constant(base_cos_table),
        constant(base_sin_table),
        constant(lane_cos),
        constant(lane_sin),
    )

    send = row_stage(limbs, row_matrix, tables, groups)
    received = lax.all_to_all(send, ("row", "col"), 0, 0, tiled=True)

    outer_index = np.arange(groups, dtype=np.int64)
    inner_index = np.arange(narrow, dtype=np.int64)
    twist_cos, twist_sin = exact_phases(
        2 * (outer_index[:, None] * inner_index[None, :] % breadth), breadth
    )
    inner_cos, inner_sin = exact_phases(2 * (inner_index[:, None] * inner_index[None, :] % narrow), narrow)
    forward = np.block([[inner_cos, inner_sin], [-inner_sin, inner_cos]])
    inverse = np.block([[inner_cos, -inner_sin], [inner_sin, inner_cos]])
    outgoing = column_stage(
        received,
        constant(twist_cos),
        constant(twist_sin),
        jnp.asarray(split_bf16(forward)),
        jnp.asarray(split_bf16(inverse)),
    )
    pieces = lax.all_to_all(outgoing, ("row", "col"), 0, 0, tiled=True)

    scale_factor = 2.0 / (limb_total * math.sqrt(limb_total))
    return final_stage(pieces, final_matrix, tables, scale_factor)


def solution(mesh):
    in_specs = (P(None, "pair", ("row", "col")),)
    out_specs = P(None, "pair", ("row", "col"))
    return jax.shard_map(body, mesh=mesh, in_specs=in_specs, out_specs=out_specs, check_vma=False)
```

```python
import functools
import math

import jax
import jax.numpy as jnp
import ml_dtypes
import numpy as np
from jax import lax
from jax.experimental import pallas as pl
from jax.experimental.pallas import tpu as pltpu
from jax.sharding import PartitionSpec as P

highest = lax.Precision.HIGHEST


def phases(multiple, period):
    angles = multiple.astype(jnp.float32) * (math.pi / period)
    return (jnp.cos(angles), -jnp.sin(angles))


def exact_phases(multiple, period):
    angles = np.asarray(multiple, dtype=np.float64) * (math.pi / period)
    return np.cos(angles), -np.sin(angles)


def constant(table):
    return jnp.asarray(np.asarray(table, dtype=np.float32))


def dft_table(length):
    indices = np.arange(length, dtype=np.int64)
    table_cos, table_sin = exact_phases(2 * (indices[:, None] * indices[None, :] % length), length)
    return constant(table_cos), constant(table_sin)


def split_bf16(table):
    first = table.astype(ml_dtypes.bfloat16)
    second = (table - first.astype(np.float64)).astype(ml_dtypes.bfloat16)
    return np.concatenate((first, second), axis=0)


def mixing(former, latter, formula):
    return jnp.einsum(formula, former, latter, precision=highest)


def multiply_pair(ar, ai, br, bi):
    return ar * br - ai * bi, ar * bi + ai * br


def row_kernel(limbs_ref, matrix_ref, chooser_ref, base_cos_ref, base_sin_ref, lane_cos_ref, lane_sin_ref, out_ref):
    number = limbs_ref.shape[0]
    half = lane_cos_ref.shape[0]
    groups, _, _, local, narrow = out_ref.shape
    turn_cos, turn_sin = turn_tables(chooser_ref, base_cos_ref, base_sin_ref, lane_cos_ref, lane_sin_ref)
    centred = [limbs_ref[i] - jnp.int32(32768) for i in range(number)]
    upper = [lax.shift_right_arithmetic(value, jnp.int32(8)) for value in centred]
    lower = [value - top * jnp.int32(256) for value, top in zip(centred, upper)]
    pieces = jnp.concatenate(upper + lower, axis=1).astype(jnp.float32).astype(jnp.bfloat16)
    products = jnp.dot(matrix_ref[...], pieces, preferred_element_type=jnp.float32)
    count = 2 * half
    width = number * narrow
    upper_part = products[:count, :width] + products[count:, :width]
    lower_part = products[:count, width:] + products[count:, width:]
    rows = (upper_part * 256.0 + lower_part) * (1.0 / 32768.0)
    for i in range(number):
        real_rows = rows[:half, i * narrow : (i + 1) * narrow]
        imag_rows = rows[half:, i * narrow : (i + 1) * narrow]
        out_ref[:, 0, i] = (real_rows * turn_cos - imag_rows * turn_sin).reshape(groups, local, narrow)
        out_ref[:, 1, i] = (real_rows * turn_sin + imag_rows * turn_cos).reshape(groups, local, narrow)


def turn_tables(chooser_ref, base_cos_ref, base_sin_ref, lane_cos_ref, lane_sin_ref):
    pick = chooser_ref[...]
    base_cos = jnp.sum(base_cos_ref[...] * pick, axis=1, keepdims=True)
    base_sin = jnp.sum(base_sin_ref[...] * pick, axis=1, keepdims=True)
    lane_cos = lane_cos_ref[...]
    lane_sin = lane_sin_ref[...]
    return base_cos * lane_cos - base_sin * lane_sin, base_cos * lane_sin + base_sin * lane_cos


def row_stage(limbs, matrix, tables, groups):
    number, height, narrow = limbs.shape
    half = tables[3].shape[0]
    local = half // groups
    steps = 2
    block = number // steps
    fixed = lambda shape: pl.BlockSpec(shape, lambda s: (0,) * len(shape))
    return pl.pallas_call(
        row_kernel,
        out_shape=jax.ShapeDtypeStruct((groups, 2, number, local, narrow), jnp.float32),
        grid=(steps,),
        in_specs=[pl.BlockSpec((block, height, narrow), lambda s: (s, 0, 0)), fixed(matrix.shape)]
        + [fixed(table.shape) for table in tables],
        out_specs=pl.BlockSpec((groups, 2, block, local, narrow), lambda s: (0, 0, s, 0, 0)),
        cost_estimate=pl.CostEstimate(
            flops=2 * 4 * half * height * 2 * narrow * number,
            transcendentals=0,
            bytes_accessed=4 * 3 * number * height * narrow + 2 * 4 * half * height,
        ),
    )(limbs, matrix, *tables)


def final_kernel(pieces_ref, matrix_ref, chooser_ref, base_cos_ref, base_sin_ref, lane_cos_ref, lane_sin_ref, out_ref, *, scale):
    groups, _, outputs, local, narrow = pieces_ref.shape
    half = groups * local
    turn_cos, turn_sin = turn_tables(chooser_ref, base_cos_ref, base_sin_ref, lane_cos_ref, lane_sin_ref)
    turn_cos = turn_cos.reshape(groups, local, narrow)
    turn_sin = turn_sin.reshape(groups, local, narrow)
    columns = []
    for i in range(outputs):
        real = pieces_ref[:, 0, i]
        imag = pieces_ref[:, 1, i]
        untwisted = jnp.concatenate(
            (
                (real * turn_cos + imag * turn_sin).reshape(half, narrow),
                (imag * turn_cos - real * turn_sin).reshape(half, narrow),
            ),
            axis=0,
        )
        columns.append(untwisted)
    gathered = jnp.concatenate(columns, axis=1)
    first = gathered.astype(jnp.bfloat16)
    second = (gathered - first.astype(jnp.float32)).astype(jnp.bfloat16)
    products = jnp.dot(
        matrix_ref[...], jnp.concatenate((first, second), axis=1), preferred_element_type=jnp.float32
    )
    height = matrix_ref.shape[0] // 2
    width = outputs * narrow
    small = products[height:, width:] + products[height:, :width] + products[:height, width:]
    total = (small + products[:height, :width]) * scale
    for i in range(outputs):
        out_ref[i] = total[:, i * narrow : (i + 1) * narrow]


def final_stage(pieces, matrix, tables, scale):
    groups, _, outputs, local, narrow = pieces.shape
    height = matrix.shape[0] // 2
    fixed = lambda shape: pl.BlockSpec(shape, lambda s: (0,) * len(shape))
    return pl.pallas_call(
        functools.partial(final_kernel, scale=scale),
        out_shape=jax.ShapeDtypeStruct((outputs, height, narrow), jnp.float32),
        grid=(outputs,),
        in_specs=[pl.BlockSpec((groups, 2, 1, local, narrow), lambda s: (0, 0, s, 0, 0)), fixed(matrix.shape)]
        + [fixed(table.shape) for table in tables],
        out_specs=pl.BlockSpec((1, height, narrow), lambda s: (s, 0, 0)),
        cost_estimate=pl.CostEstimate(
            flops=2 * 4 * height * height * 2 * outputs * narrow,
            transcendentals=0,
            bytes_accessed=4 * 3 * outputs * height * narrow + 2 * 2 * height * height,
        ),
    )(pieces, matrix, *tables)


def fft16(real, imag, sign):
    def dft4(a, b, c, d):
        sum_ac = (a[0] + c[0], a[1] + c[1])
        dif_ac = (a[0] - c[0], a[1] - c[1])
        sum_bd = (b[0] + d[0], b[1] + d[1])
        dif_bd = (b[0] - d[0], b[1] - d[1])
        return (
            (sum_ac[0] + sum_bd[0], sum_ac[1] + sum_bd[1]),
            (dif_ac[0] - sign * dif_bd[1], dif_ac[1] + sign * dif_bd[0]),
            (sum_ac[0] - sum_bd[0], sum_ac[1] - sum_bd[1]),
            (dif_ac[0] + sign * dif_bd[1], dif_ac[1] - sign * dif_bd[0]),
        )

    values = list(zip(real, imag))
    stage = []
    for first in range(4):
        outs = dft4(*(values[4 * second + first] for second in range(4)))
        turned = []
        for low, (re, im) in enumerate(outs):
            if first * low == 0:
                turned.append((re, im))
                continue
            angle = sign * 2.0 * math.pi * first * low / 16.0
            cos_v, sin_v = math.cos(angle), math.sin(angle)
            turned.append((re * cos_v - im * sin_v, re * sin_v + im * cos_v))
        stage.append(turned)
    result = [None] * 16
    for low in range(4):
        outs = dft4(*(stage[first][low] for first in range(4)))
        for high in range(4):
            result[low + 4 * high] = outs[high]
    return [v[0] for v in result], [v[1] for v in result]


def split_dot(values, matrix_ref):
    size = matrix_ref.shape[0] // 2
    first = values.astype(jnp.bfloat16)
    second = (values - first.astype(jnp.float32)).astype(jnp.bfloat16)
    major = matrix_ref[:size]
    minor = matrix_ref[size:]
    small = jnp.dot(second, major, preferred_element_type=jnp.float32) + jnp.dot(
        first, minor, preferred_element_type=jnp.float32
    )
    return small + jnp.dot(first, major, preferred_element_type=jnp.float32)


def column_kernel(in_ref, twist_cos_ref, twist_sin_ref, forward_ref, inverse_ref, out_ref, lifted_ref, mixed_ref):
    groups, _, number, local, narrow = in_ref.shape
    tile = 8
    for operand in range(number):
        for start in range(0, local, tile):
            rows = pl.ds(start, tile)
            real = [in_ref[p, 0, operand, rows, :] for p in range(groups)]
            imag = [in_ref[p, 1, operand, rows, :] for p in range(groups)]
            real, imag = fft16(real, imag, -1.0)
            for k in range(groups):
                cos_v = twist_cos_ref[k : k + 1, :]
                sin_v = twist_sin_ref[k : k + 1, :]
                lifted_ref[k, operand, rows, :narrow] = real[k] * cos_v - imag[k] * sin_v
                lifted_ref[k, operand, rows, narrow:] = real[k] * sin_v + imag[k] * cos_v
    spectra = split_dot(
        lifted_ref[...].reshape(groups * number * local, 2 * narrow), forward_ref
    ).reshape(groups, number, local, 2 * narrow)

    def spectrum(k):
        part = spectra[:, k]
        return part[..., :narrow], part[..., narrow:]

    first = multiply_pair(*spectrum(0), *spectrum(3))
    second = multiply_pair(*spectrum(1), *spectrum(4))
    third_a = multiply_pair(*spectrum(2), *spectrum(4))
    third_b = multiply_pair(*spectrum(0), *spectrum(5))
    combined = (first, second, (third_a[0] + third_b[0], third_a[1] + third_b[1]))
    for index, (re, im) in enumerate(combined):
        mixed_ref[:, index, :, :narrow] = re
        mixed_ref[:, index, :, narrow:] = im
    outputs = mixed_ref.shape[1]
    mixed_ref[...] = split_dot(
        mixed_ref[...].reshape(groups * outputs * local, 2 * narrow), inverse_ref
    ).reshape(groups, outputs, local, 2 * narrow)
    for operand in range(outputs):
        for start in range(0, local, tile):
            rows = pl.ds(start, tile)
            real = []
            imag = []
            for k in range(groups):
                re = mixed_ref[k, operand, rows, :narrow]
                im = mixed_ref[k, operand, rows, narrow:]
                cos_v = twist_cos_ref[k : k + 1, :]
                sin_v = twist_sin_ref[k : k + 1, :]
                real.append(re * cos_v + im * sin_v)
                imag.append(im * cos_v - re * sin_v)
            real, imag = fft16(real, imag, 1.0)
            for p in range(groups):
                out_ref[p, 0, operand, rows, :] = real[p]
                out_ref[p, 1, operand, rows, :] = imag[p]


def column_stage(received, twist_cos, twist_sin, forward, inverse):
    groups, _, number, local, narrow = received.shape
    outputs = 3
    rows = groups * local
    return pl.pallas_call(
        column_kernel,
        out_shape=jax.ShapeDtypeStruct((groups, 2, outputs, local, narrow), jnp.float32),
        scratch_shapes=[
            pltpu.VMEM((groups, number, local, 2 * narrow), jnp.float32),
            pltpu.VMEM((groups, outputs, local, 2 * narrow), jnp.float32),
        ],
        cost_estimate=pl.CostEstimate(
            flops=3 * 2 * rows * (number + outputs) * (2 * narrow) ** 2,
            transcendentals=0,
            bytes_accessed=4 * rows * narrow * 2 * (number + outputs),
        ),
    )(received, twist_cos, twist_sin, forward, inverse)


def body(limbs):
    groups = lax.axis_size(("row", "col"))
    number, height, narrow = limbs.shape
    breadth = narrow * groups
    limb_total = height * breadth
    half = height // 2
    local = half // groups
    device = lax.axis_index(("row", "col"))

    half_index = np.arange(half, dtype=np.int64)
    row_index = np.arange(height, dtype=np.int64)
    row_cos_exact, row_sin_exact = exact_phases(
        row_index[None, :] * (2 * half_index[:, None] + 1) % (2 * height), height
    )
    row_matrix = jnp.asarray(split_bf16(np.concatenate((row_cos_exact, row_sin_exact), axis=0)))
    final_matrix = jnp.asarray(split_bf16(np.concatenate((row_cos_exact, row_sin_exact), axis=0).T))
    device_index = np.arange(groups, dtype=np.int64)
    base_cos, base_sin = exact_phases(
        device_index[:, None] * narrow * (2 * half_index[None, :] + 1), limb_total
    )
    base_cos_table = np.zeros((half, narrow))
    base_sin_table = np.zeros((half, narrow))
    base_cos_table[:, :groups] = base_cos.T
    base_sin_table[:, :groups] = base_sin.T
    chooser = (lax.broadcasted_iota(jnp.int32, (1, narrow), 1) == device).astype(jnp.float32)
    lane_index = np.arange(narrow, dtype=np.int64)
    lane_cos, lane_sin = exact_phases(lane_index[None, :] * (2 * half_index[:, None] + 1), limb_total)
    tables = (
        chooser,
        constant(base_cos_table),
        constant(base_sin_table),
        constant(lane_cos),
        constant(lane_sin),
    )

    send = row_stage(limbs, row_matrix, tables, groups)
    received = lax.all_to_all(send, ("row", "col"), 0, 0, tiled=True)

    outer_index = np.arange(groups, dtype=np.int64)
    inner_index = np.arange(narrow, dtype=np.int64)
    twist_cos, twist_sin = exact_phases(
        2 * (outer_index[:, None] * inner_index[None, :] % breadth), breadth
    )
    inner_cos, inner_sin = exact_phases(2 * (inner_index[:, None] * inner_index[None, :] % narrow), narrow)
    forward = np.block([[inner_cos, inner_sin], [-inner_sin, inner_cos]])
    inverse = np.block([[inner_cos, -inner_sin], [inner_sin, inner_cos]])
    outgoing = column_stage(
        received,
        constant(twist_cos),
        constant(twist_sin),
        jnp.asarray(split_bf16(forward)),
        jnp.asarray(split_bf16(inverse)),
    )
    pieces = lax.all_to_all(outgoing, ("row", "col"), 0, 0, tiled=True)

    scale_factor = 2.0 / (limb_total * math.sqrt(limb_total))
    return final_stage(pieces, final_matrix, tables, scale_factor)


def solution(mesh):
    in_specs = (P(None, "pair", ("row", "col")),)
    out_specs = P(None, "pair", ("row", "col"))
    return jax.shard_map(body, mesh=mesh, in_specs=in_specs, out_specs=out_specs, check_vma=False)
```

```python
import functools
import math

import jax
import jax.numpy as jnp
import ml_dtypes
import numpy as np
from jax import lax
from jax.experimental import pallas as pl
from jax.experimental.pallas import tpu as pltpu
from jax.sharding import PartitionSpec as P

highest = lax.Precision.HIGHEST


def phases(multiple, period):
    angles = multiple.astype(jnp.float32) * (math.pi / period)
    return (jnp.cos(angles), -jnp.sin(angles))


def exact_phases(multiple, period):
    angles = np.asarray(multiple, dtype=np.float64) * (math.pi / period)
    return np.cos(angles), -np.sin(angles)


def constant(table):
    return jnp.asarray(np.asarray(table, dtype=np.float32))


def dft_table(length):
    indices = np.arange(length, dtype=np.int64)
    table_cos, table_sin = exact_phases(2 * (indices[:, None] * indices[None, :] % length), length)
    return constant(table_cos), constant(table_sin)


def split_bf16(table):
    first = table.astype(ml_dtypes.bfloat16)
    second = (table - first.astype(np.float64)).astype(ml_dtypes.bfloat16)
    return np.concatenate((first, second), axis=0)


def mixing(former, latter, formula):
    return jnp.einsum(formula, former, latter, precision=highest)


def multiply_pair(ar, ai, br, bi):
    return ar * br - ai * bi, ar * bi + ai * br


def row_kernel(limbs_ref, matrix_ref, base_cos_ref, base_sin_ref, lane_cos_ref, lane_sin_ref, out_ref):
    number = limbs_ref.shape[0]
    half = lane_cos_ref.shape[0]
    groups, _, _, local, narrow = out_ref.shape
    turn_cos, turn_sin = turn_tables(base_cos_ref, base_sin_ref, lane_cos_ref, lane_sin_ref)
    centred = [limbs_ref[i] - jnp.int32(32768) for i in range(number)]
    upper = [lax.shift_right_arithmetic(value, jnp.int32(8)) for value in centred]
    lower = [value - top * jnp.int32(256) for value, top in zip(centred, upper)]
    pieces = jnp.concatenate(upper + lower, axis=1).astype(jnp.float32).astype(jnp.bfloat16)
    products = jnp.dot(matrix_ref[...], pieces, preferred_element_type=jnp.float32)
    count = 2 * half
    width = number * narrow
    upper_part = products[:count, :width] + products[count:, :width]
    lower_part = products[:count, width:] + products[count:, width:]
    rows = (upper_part * 256.0 + lower_part) * (1.0 / 32768.0)
    for i in range(number):
        real_rows = rows[:half, i * narrow : (i + 1) * narrow]
        imag_rows = rows[half:, i * narrow : (i + 1) * narrow]
        out_ref[:, 0, i] = (real_rows * turn_cos - imag_rows * turn_sin).reshape(groups, local, narrow)
        out_ref[:, 1, i] = (real_rows * turn_sin + imag_rows * turn_cos).reshape(groups, local, narrow)


def turn_tables(base_cos_ref, base_sin_ref, lane_cos_ref, lane_sin_ref):
    device = lax.axis_index("row") * lax.axis_size("col") + lax.axis_index("col")
    pick = (lax.broadcasted_iota(jnp.int32, (1, base_cos_ref.shape[1]), 1) == device).astype(jnp.float32)
    base_cos = jnp.sum(base_cos_ref[...] * pick, axis=1, keepdims=True)
    base_sin = jnp.sum(base_sin_ref[...] * pick, axis=1, keepdims=True)
    lane_cos = lane_cos_ref[...]
    lane_sin = lane_sin_ref[...]
    return base_cos * lane_cos - base_sin * lane_sin, base_cos * lane_sin + base_sin * lane_cos


def row_stage(limbs, matrix, tables, groups):
    number, height, narrow = limbs.shape
    half = tables[2].shape[0]
    local = half // groups
    steps = 2
    block = number // steps
    fixed = lambda shape: pl.BlockSpec(shape, lambda s: (0,) * len(shape))
    return pl.pallas_call(
        row_kernel,
        out_shape=jax.ShapeDtypeStruct((groups, 2, number, local, narrow), jnp.float32),
        grid=(steps,),
        in_specs=[pl.BlockSpec((block, height, narrow), lambda s: (s, 0, 0)), fixed(matrix.shape)]
        + [fixed(table.shape) for table in tables],
        out_specs=pl.BlockSpec((groups, 2, block, local, narrow), lambda s: (0, 0, s, 0, 0)),
        cost_estimate=pl.CostEstimate(
            flops=2 * 4 * half * height * 2 * narrow * number,
            transcendentals=0,
            bytes_accessed=4 * 3 * number * height * narrow + 2 * 4 * half * height,
        ),
    )(limbs, matrix, *tables)


def final_kernel(pieces_ref, matrix_ref, base_cos_ref, base_sin_ref, lane_cos_ref, lane_sin_ref, out_ref, *, scale):
    groups, _, outputs, local, narrow = pieces_ref.shape
    half = groups * local
    turn_cos, turn_sin = turn_tables(base_cos_ref, base_sin_ref, lane_cos_ref, lane_sin_ref)
    turn_cos = turn_cos.reshape(groups, local, narrow)
    turn_sin = turn_sin.reshape(groups, local, narrow)
    columns = []
    for i in range(outputs):
        real = pieces_ref[:, 0, i]
        imag = pieces_ref[:, 1, i]
        untwisted = jnp.concatenate(
            (
                (real * turn_cos + imag * turn_sin).reshape(half, narrow),
                (imag * turn_cos - real * turn_sin).reshape(half, narrow),
            ),
            axis=0,
        )
        columns.append(untwisted)
    gathered = jnp.concatenate(columns, axis=1)
    first = gathered.astype(jnp.bfloat16)
    second = (gathered - first.astype(jnp.float32)).astype(jnp.bfloat16)
    products = jnp.dot(
        matrix_ref[...], jnp.concatenate((first, second), axis=1), preferred_element_type=jnp.float32
    )
    height = matrix_ref.shape[0] // 2
    width = outputs * narrow
    small = products[height:, width:] + products[height:, :width] + products[:height, width:]
    total = (small + products[:height, :width]) * scale
    for i in range(outputs):
        out_ref[i] = total[:, i * narrow : (i + 1) * narrow]


def final_stage(pieces, matrix, tables, scale):
    groups, _, outputs, local, narrow = pieces.shape
    height = matrix.shape[0] // 2
    return pl.pallas_call(
        functools.partial(final_kernel, scale=scale),
        out_shape=jax.ShapeDtypeStruct((outputs, height, narrow), jnp.float32),
        cost_estimate=pl.CostEstimate(
            flops=2 * 4 * height * height * 2 * outputs * narrow,
            transcendentals=0,
            bytes_accessed=4 * 3 * outputs * height * narrow + 2 * 2 * height * height,
        ),
    )(pieces, matrix, *tables)


def fft16(real, imag, sign):
    def dft4(a, b, c, d):
        sum_ac = (a[0] + c[0], a[1] + c[1])
        dif_ac = (a[0] - c[0], a[1] - c[1])
        sum_bd = (b[0] + d[0], b[1] + d[1])
        dif_bd = (b[0] - d[0], b[1] - d[1])
        return (
            (sum_ac[0] + sum_bd[0], sum_ac[1] + sum_bd[1]),
            (dif_ac[0] - sign * dif_bd[1], dif_ac[1] + sign * dif_bd[0]),
            (sum_ac[0] - sum_bd[0], sum_ac[1] - sum_bd[1]),
            (dif_ac[0] + sign * dif_bd[1], dif_ac[1] - sign * dif_bd[0]),
        )

    values = list(zip(real, imag))
    stage = []
    for first in range(4):
        outs = dft4(*(values[4 * second + first] for second in range(4)))
        turned = []
        for low, (re, im) in enumerate(outs):
            if first * low == 0:
                turned.append((re, im))
                continue
            angle = sign * 2.0 * math.pi * first * low / 16.0
            cos_v, sin_v = math.cos(angle), math.sin(angle)
            turned.append((re * cos_v - im * sin_v, re * sin_v + im * cos_v))
        stage.append(turned)
    result = [None] * 16
    for low in range(4):
        outs = dft4(*(stage[first][low] for first in range(4)))
        for high in range(4):
            result[low + 4 * high] = outs[high]
    return [v[0] for v in result], [v[1] for v in result]


def split_dot(values, matrix_ref):
    size = matrix_ref.shape[0] // 2
    first = values.astype(jnp.bfloat16)
    second = (values - first.astype(jnp.float32)).astype(jnp.bfloat16)
    major = matrix_ref[:size]
    minor = matrix_ref[size:]
    small = jnp.dot(second, major, preferred_element_type=jnp.float32) + jnp.dot(
        first, minor, preferred_element_type=jnp.float32
    )
    return small + jnp.dot(first, major, preferred_element_type=jnp.float32)


def column_kernel(in_ref, twist_cos_ref, twist_sin_ref, forward_ref, inverse_ref, out_ref, lifted_ref, mixed_ref):
    groups, _, number, local, narrow = in_ref.shape
    tile = 8
    for operand in range(number):
        for start in range(0, local, tile):
            rows = pl.ds(start, tile)
            real = [in_ref[p, 0, operand, rows, :] for p in range(groups)]
            imag = [in_ref[p, 1, operand, rows, :] for p in range(groups)]
            real, imag = fft16(real, imag, -1.0)
            for k in range(groups):
                cos_v = twist_cos_ref[k : k + 1, :]
                sin_v = twist_sin_ref[k : k + 1, :]
                lifted_ref[k, operand, rows, :narrow] = real[k] * cos_v - imag[k] * sin_v
                lifted_ref[k, operand, rows, narrow:] = real[k] * sin_v + imag[k] * cos_v
    spectra = split_dot(
        lifted_ref[...].reshape(groups * number * local, 2 * narrow), forward_ref
    ).reshape(groups, number, local, 2 * narrow)

    def spectrum(k):
        part = spectra[:, k]
        return part[..., :narrow], part[..., narrow:]

    first = multiply_pair(*spectrum(0), *spectrum(3))
    second = multiply_pair(*spectrum(1), *spectrum(4))
    third_a = multiply_pair(*spectrum(2), *spectrum(4))
    third_b = multiply_pair(*spectrum(0), *spectrum(5))
    combined = (first, second, (third_a[0] + third_b[0], third_a[1] + third_b[1]))
    for index, (re, im) in enumerate(combined):
        mixed_ref[:, index, :, :narrow] = re
        mixed_ref[:, index, :, narrow:] = im
    outputs = mixed_ref.shape[1]
    mixed_ref[...] = split_dot(
        mixed_ref[...].reshape(groups * outputs * local, 2 * narrow), inverse_ref
    ).reshape(groups, outputs, local, 2 * narrow)
    for operand in range(outputs):
        for start in range(0, local, tile):
            rows = pl.ds(start, tile)
            real = []
            imag = []
            for k in range(groups):
                re = mixed_ref[k, operand, rows, :narrow]
                im = mixed_ref[k, operand, rows, narrow:]
                cos_v = twist_cos_ref[k : k + 1, :]
                sin_v = twist_sin_ref[k : k + 1, :]
                real.append(re * cos_v + im * sin_v)
                imag.append(im * cos_v - re * sin_v)
            real, imag = fft16(real, imag, 1.0)
            for p in range(groups):
                out_ref[p, 0, operand, rows, :] = real[p]
                out_ref[p, 1, operand, rows, :] = imag[p]


def column_stage(received, twist_cos, twist_sin, forward, inverse):
    groups, _, number, local, narrow = received.shape
    outputs = 3
    rows = groups * local
    return pl.pallas_call(
        column_kernel,
        out_shape=jax.ShapeDtypeStruct((groups, 2, outputs, local, narrow), jnp.float32),
        scratch_shapes=[
            pltpu.VMEM((groups, number, local, 2 * narrow), jnp.float32),
            pltpu.VMEM((groups, outputs, local, 2 * narrow), jnp.float32),
        ],
        cost_estimate=pl.CostEstimate(
            flops=3 * 2 * rows * (number + outputs) * (2 * narrow) ** 2,
            transcendentals=0,
            bytes_accessed=4 * rows * narrow * 2 * (number + outputs),
        ),
    )(received, twist_cos, twist_sin, forward, inverse)


def body(limbs):
    groups = lax.axis_size(("row", "col"))
    number, height, narrow = limbs.shape
    breadth = narrow * groups
    limb_total = height * breadth
    half = height // 2
    local = half // groups
    device = lax.axis_index(("row", "col"))

    half_index = np.arange(half, dtype=np.int64)
    row_index = np.arange(height, dtype=np.int64)
    row_cos_exact, row_sin_exact = exact_phases(
        row_index[None, :] * (2 * half_index[:, None] + 1) % (2 * height), height
    )
    row_matrix = jnp.asarray(split_bf16(np.concatenate((row_cos_exact, row_sin_exact), axis=0)))
    final_matrix = jnp.asarray(split_bf16(np.concatenate((row_cos_exact, row_sin_exact), axis=0).T))
    device_index = np.arange(groups, dtype=np.int64)
    base_cos, base_sin = exact_phases(
        device_index[:, None] * narrow * (2 * half_index[None, :] + 1), limb_total
    )
    base_cos_table = np.zeros((half, narrow))
    base_sin_table = np.zeros((half, narrow))
    base_cos_table[:, :groups] = base_cos.T
    base_sin_table[:, :groups] = base_sin.T
    lane_index = np.arange(narrow, dtype=np.int64)
    lane_cos, lane_sin = exact_phases(lane_index[None, :] * (2 * half_index[:, None] + 1), limb_total)
    tables = (
        constant(base_cos_table),
        constant(base_sin_table),
        constant(lane_cos),
        constant(lane_sin),
    )

    send = row_stage(limbs, row_matrix, tables, groups)
    received = lax.all_to_all(send, ("row", "col"), 0, 0, tiled=True)

    outer_index = np.arange(groups, dtype=np.int64)
    inner_index = np.arange(narrow, dtype=np.int64)
    twist_cos, twist_sin = exact_phases(
        2 * (outer_index[:, None] * inner_index[None, :] % breadth), breadth
    )
    inner_cos, inner_sin = exact_phases(2 * (inner_index[:, None] * inner_index[None, :] % narrow), narrow)
    forward = np.block([[inner_cos, inner_sin], [-inner_sin, inner_cos]])
    inverse = np.block([[inner_cos, -inner_sin], [inner_sin, inner_cos]])
    outgoing = column_stage(
        received,
        constant(twist_cos),
        constant(twist_sin),
        jnp.asarray(split_bf16(forward)),
        jnp.asarray(split_bf16(inverse)),
    )
    pieces = lax.all_to_all(outgoing, ("row", "col"), 0, 0, tiled=True)

    scale_factor = 2.0 / (limb_total * math.sqrt(limb_total))
    return final_stage(pieces, final_matrix, tables, scale_factor)


def solution(mesh):
    in_specs = (P(None, "pair", ("row", "col")),)
    out_specs = P(None, "pair", ("row", "col"))
    return jax.shard_map(body, mesh=mesh, in_specs=in_specs, out_specs=out_specs, check_vma=False)
```

```python
import functools
import math

import jax
import jax.numpy as jnp
import ml_dtypes
import numpy as np
from jax import lax
from jax.experimental import pallas as pl
from jax.experimental.pallas import tpu as pltpu
from jax.sharding import PartitionSpec as P

highest = lax.Precision.HIGHEST


def phases(multiple, period):
    angles = multiple.astype(jnp.float32) * (math.pi / period)
    return (jnp.cos(angles), -jnp.sin(angles))


def exact_phases(multiple, period):
    angles = np.asarray(multiple, dtype=np.float64) * (math.pi / period)
    return np.cos(angles), -np.sin(angles)


def constant(table):
    return jnp.asarray(np.asarray(table, dtype=np.float32))


def dft_table(length):
    indices = np.arange(length, dtype=np.int64)
    table_cos, table_sin = exact_phases(2 * (indices[:, None] * indices[None, :] % length), length)
    return constant(table_cos), constant(table_sin)


def split_bf16_side(table):
    first = table.astype(ml_dtypes.bfloat16)
    second = (table - first.astype(np.float64)).astype(ml_dtypes.bfloat16)
    return np.concatenate((first, second), axis=1)


def split_bf16(table):
    first = table.astype(ml_dtypes.bfloat16)
    second = (table - first.astype(np.float64)).astype(ml_dtypes.bfloat16)
    return np.concatenate((first, second), axis=0)


def mixing(former, latter, formula):
    return jnp.einsum(formula, former, latter, precision=highest)


def multiply_pair(ar, ai, br, bi):
    return ar * br - ai * bi, ar * bi + ai * br


def row_kernel(limbs_ref, matrix_ref, base_cos_ref, base_sin_ref, lane_cos_ref, lane_sin_ref, out_ref):
    number = limbs_ref.shape[0]
    half = lane_cos_ref.shape[0]
    groups, _, _, local, narrow = out_ref.shape
    turn_cos, turn_sin = turn_tables(base_cos_ref, base_sin_ref, lane_cos_ref, lane_sin_ref)
    centred = [limbs_ref[i] - jnp.int32(32768) for i in range(number)]
    upper = [lax.shift_right_arithmetic(value, jnp.int32(8)) for value in centred]
    lower = [value - top * jnp.int32(256) for value, top in zip(centred, upper)]
    upper = jnp.concatenate(upper, axis=1).astype(jnp.float32) * 256.0
    lower = jnp.concatenate(lower, axis=1).astype(jnp.float32)
    upper = upper.astype(jnp.bfloat16)
    lower = lower.astype(jnp.bfloat16)
    matrix = matrix_ref[...]
    rows = jnp.dot(matrix, jnp.concatenate((upper, upper), axis=0), preferred_element_type=jnp.float32)
    rows = rows + jnp.dot(matrix, jnp.concatenate((lower, lower), axis=0), preferred_element_type=jnp.float32)
    rows = rows * (1.0 / 32768.0)
    for i in range(number):
        real_rows = rows[:half, i * narrow : (i + 1) * narrow]
        imag_rows = rows[half:, i * narrow : (i + 1) * narrow]
        out_ref[:, 0, i] = (real_rows * turn_cos - imag_rows * turn_sin).reshape(groups, local, narrow)
        out_ref[:, 1, i] = (real_rows * turn_sin + imag_rows * turn_cos).reshape(groups, local, narrow)


def turn_tables(base_cos_ref, base_sin_ref, lane_cos_ref, lane_sin_ref):
    device = lax.axis_index("row") * lax.axis_size("col") + lax.axis_index("col")
    pick = (lax.broadcasted_iota(jnp.int32, (1, base_cos_ref.shape[1]), 1) == device).astype(jnp.float32)
    base_cos = jnp.sum(base_cos_ref[...] * pick, axis=1, keepdims=True)
    base_sin = jnp.sum(base_sin_ref[...] * pick, axis=1, keepdims=True)
    lane_cos = lane_cos_ref[...]
    lane_sin = lane_sin_ref[...]
    return base_cos * lane_cos - base_sin * lane_sin, base_cos * lane_sin + base_sin * lane_cos


def row_stage(limbs, matrix, tables, groups):
    number, height, narrow = limbs.shape
    half = tables[2].shape[0]
    local = half // groups
    steps = 2
    block = number // steps
    fixed = lambda shape: pl.BlockSpec(shape, lambda s: (0,) * len(shape))
    return pl.pallas_call(
        row_kernel,
        out_shape=jax.ShapeDtypeStruct((groups, 2, number, local, narrow), jnp.float32),
        grid=(steps,),
        in_specs=[pl.BlockSpec((block, height, narrow), lambda s: (s, 0, 0)), fixed(matrix.shape)]
        + [fixed(table.shape) for table in tables],
        out_specs=pl.BlockSpec((groups, 2, block, local, narrow), lambda s: (0, 0, s, 0, 0)),
        cost_estimate=pl.CostEstimate(
            flops=2 * 4 * half * height * 2 * narrow * number,
            transcendentals=0,
            bytes_accessed=4 * 3 * number * height * narrow + 2 * 4 * half * height,
        ),
    )(limbs, matrix, *tables)


def final_kernel(pieces_ref, matrix_ref, base_cos_ref, base_sin_ref, lane_cos_ref, lane_sin_ref, out_ref, *, scale):
    groups, _, outputs, local, narrow = pieces_ref.shape
    half = groups * local
    turn_cos, turn_sin = turn_tables(base_cos_ref, base_sin_ref, lane_cos_ref, lane_sin_ref)
    turn_cos = turn_cos.reshape(groups, local, narrow)
    turn_sin = turn_sin.reshape(groups, local, narrow)
    columns = []
    for i in range(outputs):
        real = pieces_ref[:, 0, i]
        imag = pieces_ref[:, 1, i]
        untwisted = jnp.concatenate(
            (
                (real * turn_cos + imag * turn_sin).reshape(half, narrow),
                (imag * turn_cos - real * turn_sin).reshape(half, narrow),
            ),
            axis=0,
        )
        columns.append(untwisted)
    gathered = jnp.concatenate(columns, axis=1)
    first = gathered.astype(jnp.bfloat16)
    second = (gathered - first.astype(jnp.float32)).astype(jnp.bfloat16)
    matrix = matrix_ref[...]
    small = jnp.dot(matrix, jnp.concatenate((second, second), axis=0), preferred_element_type=jnp.float32)
    large = jnp.dot(matrix, jnp.concatenate((first, first), axis=0), preferred_element_type=jnp.float32)
    total = (small + large) * scale
    for i in range(outputs):
        out_ref[i] = total[:, i * narrow : (i + 1) * narrow]


def final_stage(pieces, matrix, tables, scale):
    groups, _, outputs, local, narrow = pieces.shape
    height = matrix.shape[0]
    return pl.pallas_call(
        functools.partial(final_kernel, scale=scale),
        out_shape=jax.ShapeDtypeStruct((outputs, height, narrow), jnp.float32),
        cost_estimate=pl.CostEstimate(
            flops=2 * 4 * height * height * 2 * outputs * narrow,
            transcendentals=0,
            bytes_accessed=4 * 3 * outputs * height * narrow + 2 * 2 * height * height,
        ),
    )(pieces, matrix, *tables)


def fft16(real, imag, sign):
    def dft4(a, b, c, d):
        sum_ac = (a[0] + c[0], a[1] + c[1])
        dif_ac = (a[0] - c[0], a[1] - c[1])
        sum_bd = (b[0] + d[0], b[1] + d[1])
        dif_bd = (b[0] - d[0], b[1] - d[1])
        return (
            (sum_ac[0] + sum_bd[0], sum_ac[1] + sum_bd[1]),
            (dif_ac[0] - sign * dif_bd[1], dif_ac[1] + sign * dif_bd[0]),
            (sum_ac[0] - sum_bd[0], sum_ac[1] - sum_bd[1]),
            (dif_ac[0] + sign * dif_bd[1], dif_ac[1] - sign * dif_bd[0]),
        )

    values = list(zip(real, imag))
    stage = []
    for first in range(4):
        outs = dft4(*(values[4 * second + first] for second in range(4)))
        turned = []
        for low, (re, im) in enumerate(outs):
            if first * low == 0:
                turned.append((re, im))
                continue
            angle = sign * 2.0 * math.pi * first * low / 16.0
            cos_v, sin_v = math.cos(angle), math.sin(angle)
            turned.append((re * cos_v - im * sin_v, re * sin_v + im * cos_v))
        stage.append(turned)
    result = [None] * 16
    for low in range(4):
        outs = dft4(*(stage[first][low] for first in range(4)))
        for high in range(4):
            result[low + 4 * high] = outs[high]
    return [v[0] for v in result], [v[1] for v in result]


def split_dot(values, matrix_ref):
    size = matrix_ref.shape[0] // 2
    first = values.astype(jnp.bfloat16)
    second = (values - first.astype(jnp.float32)).astype(jnp.bfloat16)
    major = matrix_ref[:size]
    minor = matrix_ref[size:]
    small = jnp.dot(second, major, preferred_element_type=jnp.float32) + jnp.dot(
        first, minor, preferred_element_type=jnp.float32
    )
    return small + jnp.dot(first, major, preferred_element_type=jnp.float32)


def column_kernel(in_ref, twist_cos_ref, twist_sin_ref, forward_ref, inverse_ref, out_ref, lifted_ref, mixed_ref):
    groups, _, number, local, narrow = in_ref.shape
    tile = 8
    for operand in range(number):
        for start in range(0, local, tile):
            rows = pl.ds(start, tile)
            real = [in_ref[p, 0, operand, rows, :] for p in range(groups)]
            imag = [in_ref[p, 1, operand, rows, :] for p in range(groups)]
            real, imag = fft16(real, imag, -1.0)
            for k in range(groups):
                cos_v = twist_cos_ref[k : k + 1, :]
                sin_v = twist_sin_ref[k : k + 1, :]
                lifted_ref[k, operand, rows, :narrow] = real[k] * cos_v - imag[k] * sin_v
                lifted_ref[k, operand, rows, narrow:] = real[k] * sin_v + imag[k] * cos_v
    spectra = split_dot(
        lifted_ref[...].reshape(groups * number * local, 2 * narrow), forward_ref
    ).reshape(groups, number, local, 2 * narrow)

    def spectrum(k):
        part = spectra[:, k]
        return part[..., :narrow], part[..., narrow:]

    first = multiply_pair(*spectrum(0), *spectrum(3))
    second = multiply_pair(*spectrum(1), *spectrum(4))
    third_a = multiply_pair(*spectrum(2), *spectrum(4))
    third_b = multiply_pair(*spectrum(0), *spectrum(5))
    combined = (first, second, (third_a[0] + third_b[0], third_a[1] + third_b[1]))
    for index, (re, im) in enumerate(combined):
        mixed_ref[:, index, :, :narrow] = re
        mixed_ref[:, index, :, narrow:] = im
    outputs = mixed_ref.shape[1]
    mixed_ref[...] = split_dot(
        mixed_ref[...].reshape(groups * outputs * local, 2 * narrow), inverse_ref
    ).reshape(groups, outputs, local, 2 * narrow)
    for operand in range(outputs):
        for start in range(0, local, tile):
            rows = pl.ds(start, tile)
            real = []
            imag = []
            for k in range(groups):
                re = mixed_ref[k, operand, rows, :narrow]
                im = mixed_ref[k, operand, rows, narrow:]
                cos_v = twist_cos_ref[k : k + 1, :]
                sin_v = twist_sin_ref[k : k + 1, :]
                real.append(re * cos_v + im * sin_v)
                imag.append(im * cos_v - re * sin_v)
            real, imag = fft16(real, imag, 1.0)
            for p in range(groups):
                out_ref[p, 0, operand, rows, :] = real[p]
                out_ref[p, 1, operand, rows, :] = imag[p]


def column_stage(received, twist_cos, twist_sin, forward, inverse):
    groups, _, number, local, narrow = received.shape
    outputs = 3
    rows = groups * local
    return pl.pallas_call(
        column_kernel,
        out_shape=jax.ShapeDtypeStruct((groups, 2, outputs, local, narrow), jnp.float32),
        scratch_shapes=[
            pltpu.VMEM((groups, number, local, 2 * narrow), jnp.float32),
            pltpu.VMEM((groups, outputs, local, 2 * narrow), jnp.float32),
        ],
        cost_estimate=pl.CostEstimate(
            flops=3 * 2 * rows * (number + outputs) * (2 * narrow) ** 2,
            transcendentals=0,
            bytes_accessed=4 * rows * narrow * 2 * (number + outputs),
        ),
    )(received, twist_cos, twist_sin, forward, inverse)


def body(limbs):
    groups = lax.axis_size(("row", "col"))
    number, height, narrow = limbs.shape
    breadth = narrow * groups
    limb_total = height * breadth
    half = height // 2
    local = half // groups
    device = lax.axis_index(("row", "col"))

    half_index = np.arange(half, dtype=np.int64)
    row_index = np.arange(height, dtype=np.int64)
    row_cos_exact, row_sin_exact = exact_phases(
        row_index[None, :] * (2 * half_index[:, None] + 1) % (2 * height), height
    )
    row_matrix = jnp.asarray(split_bf16_side(np.concatenate((row_cos_exact, row_sin_exact), axis=0)))
    final_matrix = jnp.asarray(split_bf16_side(np.concatenate((row_cos_exact, row_sin_exact), axis=0).T))
    device_index = np.arange(groups, dtype=np.int64)
    base_cos, base_sin = exact_phases(
        device_index[:, None] * narrow * (2 * half_index[None, :] + 1), limb_total
    )
    base_cos_table = np.zeros((half, narrow))
    base_sin_table = np.zeros((half, narrow))
    base_cos_table[:, :groups] = base_cos.T
    base_sin_table[:, :groups] = base_sin.T
    lane_index = np.arange(narrow, dtype=np.int64)
    lane_cos, lane_sin = exact_phases(lane_index[None, :] * (2 * half_index[:, None] + 1), limb_total)
    tables = (
        constant(base_cos_table),
        constant(base_sin_table),
        constant(lane_cos),
        constant(lane_sin),
    )

    send = row_stage(limbs, row_matrix, tables, groups)
    received = lax.all_to_all(send, ("row", "col"), 0, 0, tiled=True)

    outer_index = np.arange(groups, dtype=np.int64)
    inner_index = np.arange(narrow, dtype=np.int64)
    twist_cos, twist_sin = exact_phases(
        2 * (outer_index[:, None] * inner_index[None, :] % breadth), breadth
    )
    inner_cos, inner_sin = exact_phases(2 * (inner_index[:, None] * inner_index[None, :] % narrow), narrow)
    forward = np.block([[inner_cos, inner_sin], [-inner_sin, inner_cos]])
    inverse = np.block([[inner_cos, -inner_sin], [inner_sin, inner_cos]])
    outgoing = column_stage(
        received,
        constant(twist_cos),
        constant(twist_sin),
        jnp.asarray(split_bf16(forward)),
        jnp.asarray(split_bf16(inverse)),
    )
    pieces = lax.all_to_all(outgoing, ("row", "col"), 0, 0, tiled=True)

    scale_factor = 2.0 / (limb_total * math.sqrt(limb_total))
    return final_stage(pieces, final_matrix, tables, scale_factor)


def solution(mesh):
    in_specs = (P(None, "pair", ("row", "col")),)
    out_specs = P(None, "pair", ("row", "col"))
    return jax.shard_map(body, mesh=mesh, in_specs=in_specs, out_specs=out_specs, check_vma=False)
```

```python
import functools
import math

import jax
import jax.numpy as jnp
import ml_dtypes
import numpy as np
from jax import lax
from jax.experimental import pallas as pl
from jax.experimental.pallas import tpu as pltpu
from jax.sharding import PartitionSpec as P

highest = lax.Precision.HIGHEST


def phases(multiple, period):
    angles = multiple.astype(jnp.float32) * (math.pi / period)
    return (jnp.cos(angles), -jnp.sin(angles))


def exact_phases(multiple, period):
    angles = np.asarray(multiple, dtype=np.float64) * (math.pi / period)
    return np.cos(angles), -np.sin(angles)


def constant(table):
    return jnp.asarray(np.asarray(table, dtype=np.float32))


def dft_table(length):
    indices = np.arange(length, dtype=np.int64)
    table_cos, table_sin = exact_phases(2 * (indices[:, None] * indices[None, :] % length), length)
    return constant(table_cos), constant(table_sin)


def split_bf16(table):
    first = table.astype(ml_dtypes.bfloat16)
    second = (table - first.astype(np.float64)).astype(ml_dtypes.bfloat16)
    return np.concatenate((first, second), axis=0)


def mixing(former, latter, formula):
    return jnp.einsum(formula, former, latter, precision=highest)


def multiply_pair(ar, ai, br, bi):
    return ar * br - ai * bi, ar * bi + ai * br


def row_kernel(limbs_ref, matrix_ref, base_cos_ref, base_sin_ref, lane_cos_ref, lane_sin_ref, out_ref):
    number = limbs_ref.shape[0]
    half = lane_cos_ref.shape[0]
    groups, _, _, local, narrow = out_ref.shape
    turn_cos, turn_sin = turn_tables(base_cos_ref, base_sin_ref, lane_cos_ref, lane_sin_ref)
    centred = [limbs_ref[i] - jnp.int32(32768) for i in range(number)]
    upper = [lax.shift_right_arithmetic(value, jnp.int32(8)) for value in centred]
    lower = [value - top * jnp.int32(256) for value, top in zip(centred, upper)]
    pieces = jnp.concatenate(upper + lower, axis=1).astype(jnp.float32).astype(jnp.bfloat16)
    products = jnp.dot(matrix_ref[...], pieces, preferred_element_type=jnp.float32)
    count = 2 * half
    width = number * narrow
    upper_part = products[:count, :width] + products[count:, :width]
    lower_part = products[:count, width:] + products[count:, width:]
    rows = (upper_part * 256.0 + lower_part) * (1.0 / 32768.0)
    for i in range(number):
        real_rows = rows[:half, i * narrow : (i + 1) * narrow]
        imag_rows = rows[half:, i * narrow : (i + 1) * narrow]
        out_ref[:, 0, i] = (real_rows * turn_cos - imag_rows * turn_sin).reshape(groups, local, narrow)
        out_ref[:, 1, i] = (real_rows * turn_sin + imag_rows * turn_cos).reshape(groups, local, narrow)


def turn_tables(base_cos_ref, base_sin_ref, lane_cos_ref, lane_sin_ref):
    device = lax.axis_index("row") * lax.axis_size("col") + lax.axis_index("col")
    pick = (lax.broadcasted_iota(jnp.int32, (1, base_cos_ref.shape[1]), 1) == device).astype(jnp.float32)
    base_cos = jnp.sum(base_cos_ref[...] * pick, axis=1, keepdims=True)
    base_sin = jnp.sum(base_sin_ref[...] * pick, axis=1, keepdims=True)
    lane_cos = lane_cos_ref[...]
    lane_sin = lane_sin_ref[...]
    return base_cos * lane_cos - base_sin * lane_sin, base_cos * lane_sin + base_sin * lane_cos


def row_stage(limbs, matrix, tables, groups):
    number, height, narrow = limbs.shape
    half = tables[2].shape[0]
    local = half // groups
    steps = 3
    block = number // steps
    fixed = lambda shape: pl.BlockSpec(shape, lambda s: (0,) * len(shape))
    return pl.pallas_call(
        row_kernel,
        out_shape=jax.ShapeDtypeStruct((groups, 2, number, local, narrow), jnp.float32),
        grid=(steps,),
        in_specs=[pl.BlockSpec((block, height, narrow), lambda s: (s, 0, 0)), fixed(matrix.shape)]
        + [fixed(table.shape) for table in tables],
        out_specs=pl.BlockSpec((groups, 2, block, local, narrow), lambda s: (0, 0, s, 0, 0)),
        cost_estimate=pl.CostEstimate(
            flops=2 * 4 * half * height * 2 * narrow * number,
            transcendentals=0,
            bytes_accessed=4 * 3 * number * height * narrow + 2 * 4 * half * height,
        ),
    )(limbs, matrix, *tables)


def final_kernel(pieces_ref, matrix_ref, base_cos_ref, base_sin_ref, lane_cos_ref, lane_sin_ref, out_ref, *, scale):
    groups, _, outputs, local, narrow = pieces_ref.shape
    half = groups * local
    turn_cos, turn_sin = turn_tables(base_cos_ref, base_sin_ref, lane_cos_ref, lane_sin_ref)
    turn_cos = turn_cos.reshape(groups, local, narrow)
    turn_sin = turn_sin.reshape(groups, local, narrow)
    columns = []
    for i in range(outputs):
        real = pieces_ref[:, 0, i]
        imag = pieces_ref[:, 1, i]
        untwisted = jnp.concatenate(
            (
                (real * turn_cos + imag * turn_sin).reshape(half, narrow),
                (imag * turn_cos - real * turn_sin).reshape(half, narrow),
            ),
            axis=0,
        )
        columns.append(untwisted)
    gathered = jnp.concatenate(columns, axis=1)
    first = gathered.astype(jnp.bfloat16)
    second = (gathered - first.astype(jnp.float32)).astype(jnp.bfloat16)
    products = jnp.dot(
        matrix_ref[...], jnp.concatenate((first, second), axis=1), preferred_element_type=jnp.float32
    )
    height = matrix_ref.shape[0] // 2
    width = outputs * narrow
    small = products[height:, width:] + products[height:, :width] + products[:height, width:]
    total = (small + products[:height, :width]) * scale
    for i in range(outputs):
        out_ref[i] = total[:, i * narrow : (i + 1) * narrow]


def final_stage(pieces, matrix, tables, scale):
    groups, _, outputs, local, narrow = pieces.shape
    height = matrix.shape[0] // 2
    return pl.pallas_call(
        functools.partial(final_kernel, scale=scale),
        out_shape=jax.ShapeDtypeStruct((outputs, height, narrow), jnp.float32),
        cost_estimate=pl.CostEstimate(
            flops=2 * 4 * height * height * 2 * outputs * narrow,
            transcendentals=0,
            bytes_accessed=4 * 3 * outputs * height * narrow + 2 * 2 * height * height,
        ),
    )(pieces, matrix, *tables)


def fft16(real, imag, sign):
    def dft4(a, b, c, d):
        sum_ac = (a[0] + c[0], a[1] + c[1])
        dif_ac = (a[0] - c[0], a[1] - c[1])
        sum_bd = (b[0] + d[0], b[1] + d[1])
        dif_bd = (b[0] - d[0], b[1] - d[1])
        return (
            (sum_ac[0] + sum_bd[0], sum_ac[1] + sum_bd[1]),
            (dif_ac[0] - sign * dif_bd[1], dif_ac[1] + sign * dif_bd[0]),
            (sum_ac[0] - sum_bd[0], sum_ac[1] - sum_bd[1]),
            (dif_ac[0] + sign * dif_bd[1], dif_ac[1] - sign * dif_bd[0]),
        )

    values = list(zip(real, imag))
    stage = []
    for first in range(4):
        outs = dft4(*(values[4 * second + first] for second in range(4)))
        turned = []
        for low, (re, im) in enumerate(outs):
            if first * low == 0:
                turned.append((re, im))
                continue
            angle = sign * 2.0 * math.pi * first * low / 16.0
            cos_v, sin_v = math.cos(angle), math.sin(angle)
            turned.append((re * cos_v - im * sin_v, re * sin_v + im * cos_v))
        stage.append(turned)
    result = [None] * 16
    for low in range(4):
        outs = dft4(*(stage[first][low] for first in range(4)))
        for high in range(4):
            result[low + 4 * high] = outs[high]
    return [v[0] for v in result], [v[1] for v in result]


def split_dot(values, matrix_ref):
    size = matrix_ref.shape[0] // 2
    first = values.astype(jnp.bfloat16)
    second = (values - first.astype(jnp.float32)).astype(jnp.bfloat16)
    major = matrix_ref[:size]
    minor = matrix_ref[size:]
    small = jnp.dot(second, major, preferred_element_type=jnp.float32) + jnp.dot(
        first, minor, preferred_element_type=jnp.float32
    )
    return small + jnp.dot(first, major, preferred_element_type=jnp.float32)


def column_kernel(in_ref, twist_cos_ref, twist_sin_ref, forward_ref, inverse_ref, out_ref, lifted_ref, mixed_ref):
    groups, _, number, local, narrow = in_ref.shape
    tile = 8
    for operand in range(number):
        for start in range(0, local, tile):
            rows = pl.ds(start, tile)
            real = [in_ref[p, 0, operand, rows, :] for p in range(groups)]
            imag = [in_ref[p, 1, operand, rows, :] for p in range(groups)]
            real, imag = fft16(real, imag, -1.0)
            for k in range(groups):
                cos_v = twist_cos_ref[k : k + 1, :]
                sin_v = twist_sin_ref[k : k + 1, :]
                lifted_ref[k, operand, rows, :narrow] = real[k] * cos_v - imag[k] * sin_v
                lifted_ref[k, operand, rows, narrow:] = real[k] * sin_v + imag[k] * cos_v
    spectra = split_dot(
        lifted_ref[...].reshape(groups * number * local, 2 * narrow), forward_ref
    ).reshape(groups, number, local, 2 * narrow)

    def spectrum(k):
        part = spectra[:, k]
        return part[..., :narrow], part[..., narrow:]

    first = multiply_pair(*spectrum(0), *spectrum(3))
    second = multiply_pair(*spectrum(1), *spectrum(4))
    third_a = multiply_pair(*spectrum(2), *spectrum(4))
    third_b = multiply_pair(*spectrum(0), *spectrum(5))
    combined = (first, second, (third_a[0] + third_b[0], third_a[1] + third_b[1]))
    for index, (re, im) in enumerate(combined):
        mixed_ref[:, index, :, :narrow] = re
        mixed_ref[:, index, :, narrow:] = im
    outputs = mixed_ref.shape[1]
    mixed_ref[...] = split_dot(
        mixed_ref[...].reshape(groups * outputs * local, 2 * narrow), inverse_ref
    ).reshape(groups, outputs, local, 2 * narrow)
    for operand in range(outputs):
        for start in range(0, local, tile):
            rows = pl.ds(start, tile)
            real = []
            imag = []
            for k in range(groups):
                re = mixed_ref[k, operand, rows, :narrow]
                im = mixed_ref[k, operand, rows, narrow:]
                cos_v = twist_cos_ref[k : k + 1, :]
                sin_v = twist_sin_ref[k : k + 1, :]
                real.append(re * cos_v + im * sin_v)
                imag.append(im * cos_v - re * sin_v)
            real, imag = fft16(real, imag, 1.0)
            for p in range(groups):
                out_ref[p, 0, operand, rows, :] = real[p]
                out_ref[p, 1, operand, rows, :] = imag[p]


def column_stage(received, twist_cos, twist_sin, forward, inverse):
    groups, _, number, local, narrow = received.shape
    outputs = 3
    rows = groups * local
    return pl.pallas_call(
        column_kernel,
        out_shape=jax.ShapeDtypeStruct((groups, 2, outputs, local, narrow), jnp.float32),
        scratch_shapes=[
            pltpu.VMEM((groups, number, local, 2 * narrow), jnp.float32),
            pltpu.VMEM((groups, outputs, local, 2 * narrow), jnp.float32),
        ],
        cost_estimate=pl.CostEstimate(
            flops=3 * 2 * rows * (number + outputs) * (2 * narrow) ** 2,
            transcendentals=0,
            bytes_accessed=4 * rows * narrow * 2 * (number + outputs),
        ),
    )(received, twist_cos, twist_sin, forward, inverse)


def body(limbs):
    groups = lax.axis_size(("row", "col"))
    number, height, narrow = limbs.shape
    breadth = narrow * groups
    limb_total = height * breadth
    half = height // 2
    local = half // groups
    device = lax.axis_index(("row", "col"))

    half_index = np.arange(half, dtype=np.int64)
    row_index = np.arange(height, dtype=np.int64)
    row_cos_exact, row_sin_exact = exact_phases(
        row_index[None, :] * (2 * half_index[:, None] + 1) % (2 * height), height
    )
    row_matrix = jnp.asarray(split_bf16(np.concatenate((row_cos_exact, row_sin_exact), axis=0)))
    final_matrix = jnp.asarray(split_bf16(np.concatenate((row_cos_exact, row_sin_exact), axis=0).T))
    device_index = np.arange(groups, dtype=np.int64)
    base_cos, base_sin = exact_phases(
        device_index[:, None] * narrow * (2 * half_index[None, :] + 1), limb_total
    )
    base_cos_table = np.zeros((half, narrow))
    base_sin_table = np.zeros((half, narrow))
    base_cos_table[:, :groups] = base_cos.T
    base_sin_table[:, :groups] = base_sin.T
    lane_index = np.arange(narrow, dtype=np.int64)
    lane_cos, lane_sin = exact_phases(lane_index[None, :] * (2 * half_index[:, None] + 1), limb_total)
    tables = (
        constant(base_cos_table),
        constant(base_sin_table),
        constant(lane_cos),
        constant(lane_sin),
    )

    send = row_stage(limbs, row_matrix, tables, groups)
    received = lax.all_to_all(send, ("row", "col"), 0, 0, tiled=True)

    outer_index = np.arange(groups, dtype=np.int64)
    inner_index = np.arange(narrow, dtype=np.int64)
    twist_cos, twist_sin = exact_phases(
        2 * (outer_index[:, None] * inner_index[None, :] % breadth), breadth
    )
    inner_cos, inner_sin = exact_phases(2 * (inner_index[:, None] * inner_index[None, :] % narrow), narrow)
    forward = np.block([[inner_cos, inner_sin], [-inner_sin, inner_cos]])
    inverse = np.block([[inner_cos, -inner_sin], [inner_sin, inner_cos]])
    outgoing = column_stage(
        received,
        constant(twist_cos),
        constant(twist_sin),
        jnp.asarray(split_bf16(forward)),
        jnp.asarray(split_bf16(inverse)),
    )
    pieces = lax.all_to_all(outgoing, ("row", "col"), 0, 0, tiled=True)

    scale_factor = 2.0 / (limb_total * math.sqrt(limb_total))
    return final_stage(pieces, final_matrix, tables, scale_factor)


def solution(mesh):
    in_specs = (P(None, "pair", ("row", "col")),)
    out_specs = P(None, "pair", ("row", "col"))
    return jax.shard_map(body, mesh=mesh, in_specs=in_specs, out_specs=out_specs, check_vma=False)
```

```python
import functools
import math

import jax
import jax.numpy as jnp
import ml_dtypes
import numpy as np
from jax import lax
from jax.experimental import pallas as pl
from jax.experimental.pallas import tpu as pltpu
from jax.sharding import PartitionSpec as P

highest = lax.Precision.HIGHEST


def phases(multiple, period):
    angles = multiple.astype(jnp.float32) * (math.pi / period)
    return (jnp.cos(angles), -jnp.sin(angles))


def exact_phases(multiple, period):
    angles = np.asarray(multiple, dtype=np.float64) * (math.pi / period)
    return np.cos(angles), -np.sin(angles)


def constant(table):
    return jnp.asarray(np.asarray(table, dtype=np.float32))


def dft_table(length):
    indices = np.arange(length, dtype=np.int64)
    table_cos, table_sin = exact_phases(2 * (indices[:, None] * indices[None, :] % length), length)
    return constant(table_cos), constant(table_sin)


def split_bf16(table):
    first = table.astype(ml_dtypes.bfloat16)
    second = (table - first.astype(np.float64)).astype(ml_dtypes.bfloat16)
    return np.concatenate((first, second), axis=0)


def mixing(former, latter, formula):
    return jnp.einsum(formula, former, latter, precision=highest)


def multiply_pair(ar, ai, br, bi):
    return ar * br - ai * bi, ar * bi + ai * br


def row_kernel(limbs_ref, matrix_ref, base_cos_ref, base_sin_ref, lane_cos_ref, lane_sin_ref, out_ref):
    number = limbs_ref.shape[0]
    half = lane_cos_ref.shape[0]
    groups, _, _, local, narrow = out_ref.shape
    turn_cos, turn_sin = turn_tables(base_cos_ref, base_sin_ref, lane_cos_ref, lane_sin_ref)
    centred = [limbs_ref[i] - jnp.int32(32768) for i in range(number)]
    upper = [lax.shift_right_arithmetic(value, jnp.int32(8)) for value in centred]
    lower = [value - top * jnp.int32(256) for value, top in zip(centred, upper)]
    pieces = jnp.concatenate(upper + lower, axis=1).astype(jnp.float32).astype(jnp.bfloat16)
    products = jnp.dot(matrix_ref[...], pieces, preferred_element_type=jnp.float32)
    count = 2 * half
    width = number * narrow
    upper_part = products[:count, :width] + products[count:, :width]
    lower_part = products[:count, width:] + products[count:, width:]
    rows = (upper_part * 256.0 + lower_part) * (1.0 / 32768.0)
    for i in range(number):
        real_rows = rows[:half, i * narrow : (i + 1) * narrow]
        imag_rows = rows[half:, i * narrow : (i + 1) * narrow]
        out_ref[:, 0, i] = (real_rows * turn_cos - imag_rows * turn_sin).reshape(groups, local, narrow)
        out_ref[:, 1, i] = (real_rows * turn_sin + imag_rows * turn_cos).reshape(groups, local, narrow)


def turn_tables(base_cos_ref, base_sin_ref, lane_cos_ref, lane_sin_ref):
    device = lax.axis_index("row") * lax.axis_size("col") + lax.axis_index("col")
    pick = (lax.broadcasted_iota(jnp.int32, (1, base_cos_ref.shape[1]), 1) == device).astype(jnp.float32)
    base_cos = jnp.sum(base_cos_ref[...] * pick, axis=1, keepdims=True)
    base_sin = jnp.sum(base_sin_ref[...] * pick, axis=1, keepdims=True)
    lane_cos = lane_cos_ref[...]
    lane_sin = lane_sin_ref[...]
    return base_cos * lane_cos - base_sin * lane_sin, base_cos * lane_sin + base_sin * lane_cos


def row_stage(limbs, matrix, tables, groups):
    number, height, narrow = limbs.shape
    half = tables[2].shape[0]
    local = half // groups
    steps = 2
    block = number // steps
    fixed = lambda shape: pl.BlockSpec(shape, lambda s: (0,) * len(shape))
    return pl.pallas_call(
        row_kernel,
        out_shape=jax.ShapeDtypeStruct((groups, 2, number, local, narrow), jnp.float32),
        grid=(steps,),
        in_specs=[pl.BlockSpec((block, height, narrow), lambda s: (s, 0, 0)), fixed(matrix.shape)]
        + [fixed(table.shape) for table in tables],
        out_specs=pl.BlockSpec((groups, 2, block, local, narrow), lambda s: (0, 0, s, 0, 0)),
        cost_estimate=pl.CostEstimate(
            flops=2 * 4 * half * height * 2 * narrow * number,
            transcendentals=0,
            bytes_accessed=4 * 3 * number * height * narrow + 2 * 4 * half * height,
        ),
    )(limbs, matrix, *tables)


def final_kernel(pieces_ref, matrix_ref, base_cos_ref, base_sin_ref, lane_cos_ref, lane_sin_ref, out_ref, *, scale):
    groups, _, outputs, local, narrow = pieces_ref.shape
    half = groups * local
    turn_cos, turn_sin = turn_tables(base_cos_ref, base_sin_ref, lane_cos_ref, lane_sin_ref)
    turn_cos = turn_cos.reshape(groups, local, narrow)
    turn_sin = turn_sin.reshape(groups, local, narrow)
    columns = []
    for i in range(outputs):
        real = pieces_ref[:, 0, i]
        imag = pieces_ref[:, 1, i]
        untwisted = jnp.concatenate(
            (
                (real * turn_cos + imag * turn_sin).reshape(half, narrow),
                (imag * turn_cos - real * turn_sin).reshape(half, narrow),
            ),
            axis=0,
        )
        columns.append(untwisted)
    gathered = jnp.concatenate(columns, axis=1)
    first = gathered.astype(jnp.bfloat16)
    second = (gathered - first.astype(jnp.float32)).astype(jnp.bfloat16)
    height = matrix_ref.shape[0] // 2
    width = outputs * narrow
    leading = jnp.dot(
        matrix_ref[:height], jnp.concatenate((first, second), axis=1), preferred_element_type=jnp.float32
    )
    trailing = jnp.dot(matrix_ref[height:], first, preferred_element_type=jnp.float32)
    small = trailing + leading[:, width:]
    total = (small + leading[:, :width]) * scale
    for i in range(outputs):
        out_ref[i] = total[:, i * narrow : (i + 1) * narrow]


def final_stage(pieces, matrix, tables, scale):
    groups, _, outputs, local, narrow = pieces.shape
    height = matrix.shape[0] // 2
    return pl.pallas_call(
        functools.partial(final_kernel, scale=scale),
        out_shape=jax.ShapeDtypeStruct((outputs, height, narrow), jnp.float32),
        cost_estimate=pl.CostEstimate(
            flops=2 * 3 * height * height * 2 * outputs * narrow,
            transcendentals=0,
            bytes_accessed=4 * 3 * outputs * height * narrow + 2 * 2 * height * height,
        ),
    )(pieces, matrix, *tables)


def fft16(real, imag, sign):
    def dft4(a, b, c, d):
        sum_ac = (a[0] + c[0], a[1] + c[1])
        dif_ac = (a[0] - c[0], a[1] - c[1])
        sum_bd = (b[0] + d[0], b[1] + d[1])
        dif_bd = (b[0] - d[0], b[1] - d[1])
        return (
            (sum_ac[0] + sum_bd[0], sum_ac[1] + sum_bd[1]),
            (dif_ac[0] - sign * dif_bd[1], dif_ac[1] + sign * dif_bd[0]),
            (sum_ac[0] - sum_bd[0], sum_ac[1] - sum_bd[1]),
            (dif_ac[0] + sign * dif_bd[1], dif_ac[1] - sign * dif_bd[0]),
        )

    values = list(zip(real, imag))
    stage = []
    for first in range(4):
        outs = dft4(*(values[4 * second + first] for second in range(4)))
        turned = []
        for low, (re, im) in enumerate(outs):
            if first * low == 0:
                turned.append((re, im))
                continue
            angle = sign * 2.0 * math.pi * first * low / 16.0
            cos_v, sin_v = math.cos(angle), math.sin(angle)
            turned.append((re * cos_v - im * sin_v, re * sin_v + im * cos_v))
        stage.append(turned)
    result = [None] * 16
    for low in range(4):
        outs = dft4(*(stage[first][low] for first in range(4)))
        for high in range(4):
            result[low + 4 * high] = outs[high]
    return [v[0] for v in result], [v[1] for v in result]


def split_dot(values, matrix_ref):
    size = matrix_ref.shape[0] // 2
    first = values.astype(jnp.bfloat16)
    second = (values - first.astype(jnp.float32)).astype(jnp.bfloat16)
    major = matrix_ref[:size]
    minor = matrix_ref[size:]
    small = jnp.dot(second, major, preferred_element_type=jnp.float32) + jnp.dot(
        first, minor, preferred_element_type=jnp.float32
    )
    return small + jnp.dot(first, major, preferred_element_type=jnp.float32)


def column_kernel(in_ref, twist_cos_ref, twist_sin_ref, forward_ref, inverse_ref, out_ref, lifted_ref, mixed_ref):
    groups, _, number, local, narrow = in_ref.shape
    tile = 8
    for operand in range(number):
        for start in range(0, local, tile):
            rows = pl.ds(start, tile)
            real = [in_ref[p, 0, operand, rows, :] for p in range(groups)]
            imag = [in_ref[p, 1, operand, rows, :] for p in range(groups)]
            real, imag = fft16(real, imag, -1.0)
            for k in range(groups):
                cos_v = twist_cos_ref[k : k + 1, :]
                sin_v = twist_sin_ref[k : k + 1, :]
                lifted_ref[k, operand, rows, :narrow] = real[k] * cos_v - imag[k] * sin_v
                lifted_ref[k, operand, rows, narrow:] = real[k] * sin_v + imag[k] * cos_v
    spectra = split_dot(
        lifted_ref[...].reshape(groups * number * local, 2 * narrow), forward_ref
    ).reshape(groups, number, local, 2 * narrow)

    def spectrum(k):
        part = spectra[:, k]
        return part[..., :narrow], part[..., narrow:]

    first = multiply_pair(*spectrum(0), *spectrum(3))
    second = multiply_pair(*spectrum(1), *spectrum(4))
    third_a = multiply_pair(*spectrum(2), *spectrum(4))
    third_b = multiply_pair(*spectrum(0), *spectrum(5))
    combined = (first, second, (third_a[0] + third_b[0], third_a[1] + third_b[1]))
    for index, (re, im) in enumerate(combined):
        mixed_ref[:, index, :, :narrow] = re
        mixed_ref[:, index, :, narrow:] = im
    outputs = mixed_ref.shape[1]
    mixed_ref[...] = split_dot(
        mixed_ref[...].reshape(groups * outputs * local, 2 * narrow), inverse_ref
    ).reshape(groups, outputs, local, 2 * narrow)
    for operand in range(outputs):
        for start in range(0, local, tile):
            rows = pl.ds(start, tile)
            real = []
            imag = []
            for k in range(groups):
                re = mixed_ref[k, operand, rows, :narrow]
                im = mixed_ref[k, operand, rows, narrow:]
                cos_v = twist_cos_ref[k : k + 1, :]
                sin_v = twist_sin_ref[k : k + 1, :]
                real.append(re * cos_v + im * sin_v)
                imag.append(im * cos_v - re * sin_v)
            real, imag = fft16(real, imag, 1.0)
            for p in range(groups):
                out_ref[p, 0, operand, rows, :] = real[p]
                out_ref[p, 1, operand, rows, :] = imag[p]


def column_stage(received, twist_cos, twist_sin, forward, inverse):
    groups, _, number, local, narrow = received.shape
    outputs = 3
    rows = groups * local
    return pl.pallas_call(
        column_kernel,
        out_shape=jax.ShapeDtypeStruct((groups, 2, outputs, local, narrow), jnp.float32),
        scratch_shapes=[
            pltpu.VMEM((groups, number, local, 2 * narrow), jnp.float32),
            pltpu.VMEM((groups, outputs, local, 2 * narrow), jnp.float32),
        ],
        cost_estimate=pl.CostEstimate(
            flops=3 * 2 * rows * (number + outputs) * (2 * narrow) ** 2,
            transcendentals=0,
            bytes_accessed=4 * rows * narrow * 2 * (number + outputs),
        ),
    )(received, twist_cos, twist_sin, forward, inverse)


def body(limbs):
    groups = lax.axis_size(("row", "col"))
    number, height, narrow = limbs.shape
    breadth = narrow * groups
    limb_total = height * breadth
    half = height // 2
    local = half // groups
    device = lax.axis_index(("row", "col"))

    half_index = np.arange(half, dtype=np.int64)
    row_index = np.arange(height, dtype=np.int64)
    row_cos_exact, row_sin_exact = exact_phases(
        row_index[None, :] * (2 * half_index[:, None] + 1) % (2 * height), height
    )
    row_matrix = jnp.asarray(split_bf16(np.concatenate((row_cos_exact, row_sin_exact), axis=0)))
    final_matrix = jnp.asarray(split_bf16(np.concatenate((row_cos_exact, row_sin_exact), axis=0).T))
    device_index = np.arange(groups, dtype=np.int64)
    base_cos, base_sin = exact_phases(
        device_index[:, None] * narrow * (2 * half_index[None, :] + 1), limb_total
    )
    base_cos_table = np.zeros((half, narrow))
    base_sin_table = np.zeros((half, narrow))
    base_cos_table[:, :groups] = base_cos.T
    base_sin_table[:, :groups] = base_sin.T
    lane_index = np.arange(narrow, dtype=np.int64)
    lane_cos, lane_sin = exact_phases(lane_index[None, :] * (2 * half_index[:, None] + 1), limb_total)
    tables = (
        constant(base_cos_table),
        constant(base_sin_table),
        constant(lane_cos),
        constant(lane_sin),
    )

    send = row_stage(limbs, row_matrix, tables, groups)
    received = lax.all_to_all(send, ("row", "col"), 0, 0, tiled=True)

    outer_index = np.arange(groups, dtype=np.int64)
    inner_index = np.arange(narrow, dtype=np.int64)
    twist_cos, twist_sin = exact_phases(
        2 * (outer_index[:, None] * inner_index[None, :] % breadth), breadth
    )
    inner_cos, inner_sin = exact_phases(2 * (inner_index[:, None] * inner_index[None, :] % narrow), narrow)
    forward = np.block([[inner_cos, inner_sin], [-inner_sin, inner_cos]])
    inverse = np.block([[inner_cos, -inner_sin], [inner_sin, inner_cos]])
    outgoing = column_stage(
        received,
        constant(twist_cos),
        constant(twist_sin),
        jnp.asarray(split_bf16(forward)),
        jnp.asarray(split_bf16(inverse)),
    )
    pieces = lax.all_to_all(outgoing, ("row", "col"), 0, 0, tiled=True)

    scale_factor = 2.0 / (limb_total * math.sqrt(limb_total))
    return final_stage(pieces, final_matrix, tables, scale_factor)


def solution(mesh):
    in_specs = (P(None, "pair", ("row", "col")),)
    out_specs = P(None, "pair", ("row", "col"))
    return jax.shard_map(body, mesh=mesh, in_specs=in_specs, out_specs=out_specs, check_vma=False)
```

```python
import functools
import math

import jax
import jax.numpy as jnp
import ml_dtypes
import numpy as np
from jax import lax
from jax.experimental import pallas as pl
from jax.experimental.pallas import tpu as pltpu
from jax.sharding import PartitionSpec as P

highest = lax.Precision.HIGHEST


def phases(multiple, period):
    angles = multiple.astype(jnp.float32) * (math.pi / period)
    return (jnp.cos(angles), -jnp.sin(angles))


def exact_phases(multiple, period):
    angles = np.asarray(multiple, dtype=np.float64) * (math.pi / period)
    return np.cos(angles), -np.sin(angles)


def constant(table):
    return jnp.asarray(np.asarray(table, dtype=np.float32))


def dft_table(length):
    indices = np.arange(length, dtype=np.int64)
    table_cos, table_sin = exact_phases(2 * (indices[:, None] * indices[None, :] % length), length)
    return constant(table_cos), constant(table_sin)


def split_bf16(table):
    first = table.astype(ml_dtypes.bfloat16)
    second = (table - first.astype(np.float64)).astype(ml_dtypes.bfloat16)
    return np.concatenate((first, second), axis=0)


def mixing(former, latter, formula):
    return jnp.einsum(formula, former, latter, precision=highest)


def multiply_pair(ar, ai, br, bi):
    return ar * br - ai * bi, ar * bi + ai * br


def row_kernel(limbs_ref, matrix_ref, base_cos_ref, base_sin_ref, lane_cos_ref, lane_sin_ref, out_ref):
    number = limbs_ref.shape[0]
    half = lane_cos_ref.shape[0]
    groups, _, _, local, narrow = out_ref.shape
    turn_cos, turn_sin = turn_tables(base_cos_ref, base_sin_ref, lane_cos_ref, lane_sin_ref)
    centred = [limbs_ref[i] - jnp.int32(32768) for i in range(number)]
    upper = [lax.shift_right_arithmetic(value, jnp.int32(8)) for value in centred]
    lower = [value - top * jnp.int32(256) for value, top in zip(centred, upper)]
    pieces = jnp.concatenate(upper + lower, axis=1).astype(jnp.float32).astype(jnp.bfloat16)
    products = jnp.dot(matrix_ref[...], pieces, preferred_element_type=jnp.float32)
    count = 2 * half
    width = number * narrow
    upper_part = products[:count, :width] + products[count:, :width]
    lower_part = products[:count, width:] + products[count:, width:]
    rows = (upper_part * 256.0 + lower_part) * (1.0 / 32768.0)
    for i in range(number):
        real_rows = rows[:half, i * narrow : (i + 1) * narrow]
        imag_rows = rows[half:, i * narrow : (i + 1) * narrow]
        out_ref[:, 0, i] = (real_rows * turn_cos - imag_rows * turn_sin).reshape(groups, local, narrow)
        out_ref[:, 1, i] = (real_rows * turn_sin + imag_rows * turn_cos).reshape(groups, local, narrow)


def turn_tables(base_cos_ref, base_sin_ref, lane_cos_ref, lane_sin_ref):
    device = lax.axis_index("row") * lax.axis_size("col") + lax.axis_index("col")
    pick = (lax.broadcasted_iota(jnp.int32, (1, base_cos_ref.shape[1]), 1) == device).astype(jnp.float32)
    base_cos = jnp.sum(base_cos_ref[...] * pick, axis=1, keepdims=True)
    base_sin = jnp.sum(base_sin_ref[...] * pick, axis=1, keepdims=True)
    lane_cos = lane_cos_ref[...]
    lane_sin = lane_sin_ref[...]
    return base_cos * lane_cos - base_sin * lane_sin, base_cos * lane_sin + base_sin * lane_cos


def row_stage(limbs, matrix, tables, groups):
    number, height, narrow = limbs.shape
    half = tables[2].shape[0]
    local = half // groups
    steps = 2
    block = number // steps
    fixed = lambda shape: pl.BlockSpec(shape, lambda s: (0,) * len(shape))
    return pl.pallas_call(
        row_kernel,
        out_shape=jax.ShapeDtypeStruct((groups, 2, number, local, narrow), jnp.float32),
        grid=(steps,),
        in_specs=[pl.BlockSpec((block, height, narrow), lambda s: (s, 0, 0)), fixed(matrix.shape)]
        + [fixed(table.shape) for table in tables],
        out_specs=pl.BlockSpec((groups, 2, block, local, narrow), lambda s: (0, 0, s, 0, 0)),
        cost_estimate=pl.CostEstimate(
            flops=2 * 4 * half * height * 2 * narrow * number,
            transcendentals=0,
            bytes_accessed=4 * 3 * number * height * narrow + 2 * 4 * half * height,
        ),
    )(limbs, matrix, *tables)


def final_kernel(pieces_ref, matrix_ref, base_cos_ref, base_sin_ref, lane_cos_ref, lane_sin_ref, out_ref, *, scale):
    groups, _, outputs, local, narrow = pieces_ref.shape
    half = groups * local
    turn_cos, turn_sin = turn_tables(base_cos_ref, base_sin_ref, lane_cos_ref, lane_sin_ref)
    turn_cos = turn_cos.reshape(groups, local, narrow)
    turn_sin = turn_sin.reshape(groups, local, narrow)
    columns = []
    for i in range(outputs):
        real = pieces_ref[:, 0, i]
        imag = pieces_ref[:, 1, i]
        untwisted = jnp.concatenate(
            (
                (real * turn_cos + imag * turn_sin).reshape(half, narrow),
                (imag * turn_cos - real * turn_sin).reshape(half, narrow),
            ),
            axis=0,
        )
        columns.append(untwisted)
    gathered = jnp.concatenate(columns, axis=1)
    first = gathered.astype(jnp.bfloat16)
    second = (gathered - first.astype(jnp.float32)).astype(jnp.bfloat16)
    height = matrix_ref.shape[0] // 2
    width = outputs * narrow
    leading = jnp.dot(
        matrix_ref[:height], jnp.concatenate((first, second), axis=1), preferred_element_type=jnp.float32
    )
    trailing = jnp.dot(matrix_ref[height:], first, preferred_element_type=jnp.float32)
    small = trailing + leading[:, width:]
    total = (small + leading[:, :width]) * scale
    for i in range(outputs):
        out_ref[i] = total[:, i * narrow : (i + 1) * narrow]


def final_stage(pieces, matrix, tables, scale):
    groups, _, outputs, local, narrow = pieces.shape
    height = matrix.shape[0] // 2
    return pl.pallas_call(
        functools.partial(final_kernel, scale=scale),
        out_shape=jax.ShapeDtypeStruct((outputs, height, narrow), jnp.float32),
        cost_estimate=pl.CostEstimate(
            flops=2 * 3 * height * height * 2 * outputs * narrow,
            transcendentals=0,
            bytes_accessed=4 * 3 * outputs * height * narrow + 2 * 2 * height * height,
        ),
    )(pieces, matrix, *tables)


def fft16(real, imag, sign):
    def dft4(a, b, c, d):
        sum_ac = (a[0] + c[0], a[1] + c[1])
        dif_ac = (a[0] - c[0], a[1] - c[1])
        sum_bd = (b[0] + d[0], b[1] + d[1])
        dif_bd = (b[0] - d[0], b[1] - d[1])
        return (
            (sum_ac[0] + sum_bd[0], sum_ac[1] + sum_bd[1]),
            (dif_ac[0] - sign * dif_bd[1], dif_ac[1] + sign * dif_bd[0]),
            (sum_ac[0] - sum_bd[0], sum_ac[1] - sum_bd[1]),
            (dif_ac[0] + sign * dif_bd[1], dif_ac[1] - sign * dif_bd[0]),
        )

    values = list(zip(real, imag))
    stage = []
    for first in range(4):
        outs = dft4(*(values[4 * second + first] for second in range(4)))
        turned = []
        for low, (re, im) in enumerate(outs):
            if first * low == 0:
                turned.append((re, im))
                continue
            angle = sign * 2.0 * math.pi * first * low / 16.0
            cos_v, sin_v = math.cos(angle), math.sin(angle)
            turned.append((re * cos_v - im * sin_v, re * sin_v + im * cos_v))
        stage.append(turned)
    result = [None] * 16
    for low in range(4):
        outs = dft4(*(stage[first][low] for first in range(4)))
        for high in range(4):
            result[low + 4 * high] = outs[high]
    return [v[0] for v in result], [v[1] for v in result]


def split_dot(values, matrix_ref):
    size = matrix_ref.shape[0] // 2
    first = values.astype(jnp.bfloat16)
    second = (values - first.astype(jnp.float32)).astype(jnp.bfloat16)
    major = matrix_ref[:size]
    minor = matrix_ref[size:]
    small = jnp.dot(second, major, preferred_element_type=jnp.float32) + jnp.dot(
        first, minor, preferred_element_type=jnp.float32
    )
    return small + jnp.dot(first, major, preferred_element_type=jnp.float32)


def column_kernel(in_ref, twist_cos_ref, twist_sin_ref, forward_ref, inverse_ref, out_ref, lifted_ref, mixed_ref):
    groups, _, number, local, narrow = in_ref.shape
    tile = 8
    for operand in range(number):
        for start in range(0, local, tile):
            rows = pl.ds(start, tile)
            real = [in_ref[p, 0, operand, rows, :] for p in range(groups)]
            imag = [in_ref[p, 1, operand, rows, :] for p in range(groups)]
            real, imag = fft16(real, imag, -1.0)
            for k in range(groups):
                cos_v = twist_cos_ref[k : k + 1, :]
                sin_v = twist_sin_ref[k : k + 1, :]
                lifted_ref[k, operand, rows, :narrow] = real[k] * cos_v - imag[k] * sin_v
                lifted_ref[k, operand, rows, narrow:] = real[k] * sin_v + imag[k] * cos_v
    spectra = split_dot(
        lifted_ref[...].reshape(groups * number * local, 2 * narrow), forward_ref
    ).reshape(groups, number, local, 2 * narrow)

    def spectrum(k):
        part = spectra[:, k]
        return part[..., :narrow], part[..., narrow:]

    first = multiply_pair(*spectrum(0), *spectrum(3))
    second = multiply_pair(*spectrum(1), *spectrum(4))
    third_a = multiply_pair(*spectrum(2), *spectrum(4))
    third_b = multiply_pair(*spectrum(0), *spectrum(5))
    combined = (first, second, (third_a[0] + third_b[0], third_a[1] + third_b[1]))
    for index, (re, im) in enumerate(combined):
        mixed_ref[:, index, :, :narrow] = re
        mixed_ref[:, index, :, narrow:] = im
    outputs = mixed_ref.shape[1]
    mixed_ref[...] = split_dot(
        mixed_ref[...].reshape(groups * outputs * local, 2 * narrow), inverse_ref
    ).reshape(groups, outputs, local, 2 * narrow)
    for operand in range(outputs):
        for start in range(0, local, tile):
            rows = pl.ds(start, tile)
            real = []
            imag = []
            for k in range(groups):
                re = mixed_ref[k, operand, rows, :narrow]
                im = mixed_ref[k, operand, rows, narrow:]
                cos_v = twist_cos_ref[k : k + 1, :]
                sin_v = twist_sin_ref[k : k + 1, :]
                real.append(re * cos_v + im * sin_v)
                imag.append(im * cos_v - re * sin_v)
            real, imag = fft16(real, imag, 1.0)
            for p in range(groups):
                out_ref[p, 0, operand, rows, :] = real[p]
                out_ref[p, 1, operand, rows, :] = imag[p]


def column_stage(received, twist_cos, twist_sin, forward, inverse):
    groups, _, number, local, narrow = received.shape
    outputs = 3
    rows = groups * local
    steps = 2
    block = local // steps
    fixed = lambda shape: pl.BlockSpec(shape, lambda s: (0,) * len(shape))
    return pl.pallas_call(
        column_kernel,
        out_shape=jax.ShapeDtypeStruct((groups, 2, outputs, local, narrow), jnp.float32),
        grid=(steps,),
        in_specs=[pl.BlockSpec((groups, 2, number, block, narrow), lambda s: (0, 0, 0, s, 0))]
        + [fixed(table.shape) for table in (twist_cos, twist_sin, forward, inverse)],
        out_specs=pl.BlockSpec((groups, 2, outputs, block, narrow), lambda s: (0, 0, 0, s, 0)),
        scratch_shapes=[
            pltpu.VMEM((groups, number, block, 2 * narrow), jnp.float32),
            pltpu.VMEM((groups, outputs, block, 2 * narrow), jnp.float32),
        ],
        cost_estimate=pl.CostEstimate(
            flops=3 * 2 * rows * (number + outputs) * (2 * narrow) ** 2,
            transcendentals=0,
            bytes_accessed=4 * rows * narrow * 2 * (number + outputs),
        ),
    )(received, twist_cos, twist_sin, forward, inverse)


def body(limbs):
    groups = lax.axis_size(("row", "col"))
    number, height, narrow = limbs.shape
    breadth = narrow * groups
    limb_total = height * breadth
    half = height // 2
    local = half // groups
    device = lax.axis_index(("row", "col"))

    half_index = np.arange(half, dtype=np.int64)
    row_index = np.arange(height, dtype=np.int64)
    row_cos_exact, row_sin_exact = exact_phases(
        row_index[None, :] * (2 * half_index[:, None] + 1) % (2 * height), height
    )
    row_matrix = jnp.asarray(split_bf16(np.concatenate((row_cos_exact, row_sin_exact), axis=0)))
    final_matrix = jnp.asarray(split_bf16(np.concatenate((row_cos_exact, row_sin_exact), axis=0).T))
    device_index = np.arange(groups, dtype=np.int64)
    base_cos, base_sin = exact_phases(
        device_index[:, None] * narrow * (2 * half_index[None, :] + 1), limb_total
    )
    base_cos_table = np.zeros((half, narrow))
    base_sin_table = np.zeros((half, narrow))
    base_cos_table[:, :groups] = base_cos.T
    base_sin_table[:, :groups] = base_sin.T
    lane_index = np.arange(narrow, dtype=np.int64)
    lane_cos, lane_sin = exact_phases(lane_index[None, :] * (2 * half_index[:, None] + 1), limb_total)
    tables = (
        constant(base_cos_table),
        constant(base_sin_table),
        constant(lane_cos),
        constant(lane_sin),
    )

    send = row_stage(limbs, row_matrix, tables, groups)
    received = lax.all_to_all(send, ("row", "col"), 0, 0, tiled=True)

    outer_index = np.arange(groups, dtype=np.int64)
    inner_index = np.arange(narrow, dtype=np.int64)
    twist_cos, twist_sin = exact_phases(
        2 * (outer_index[:, None] * inner_index[None, :] % breadth), breadth
    )
    inner_cos, inner_sin = exact_phases(2 * (inner_index[:, None] * inner_index[None, :] % narrow), narrow)
    forward = np.block([[inner_cos, inner_sin], [-inner_sin, inner_cos]])
    inverse = np.block([[inner_cos, -inner_sin], [inner_sin, inner_cos]])
    outgoing = column_stage(
        received,
        constant(twist_cos),
        constant(twist_sin),
        jnp.asarray(split_bf16(forward)),
        jnp.asarray(split_bf16(inverse)),
    )
    pieces = lax.all_to_all(outgoing, ("row", "col"), 0, 0, tiled=True)

    scale_factor = 2.0 / (limb_total * math.sqrt(limb_total))
    return final_stage(pieces, final_matrix, tables, scale_factor)


def solution(mesh):
    in_specs = (P(None, "pair", ("row", "col")),)
    out_specs = P(None, "pair", ("row", "col"))
    return jax.shard_map(body, mesh=mesh, in_specs=in_specs, out_specs=out_specs, check_vma=False)
```

```python
import functools
import math

import jax
import jax.numpy as jnp
import ml_dtypes
import numpy as np
from jax import lax
from jax.experimental import pallas as pl
from jax.experimental.pallas import tpu as pltpu
from jax.sharding import PartitionSpec as P

highest = lax.Precision.HIGHEST


def phases(multiple, period):
    angles = multiple.astype(jnp.float32) * (math.pi / period)
    return (jnp.cos(angles), -jnp.sin(angles))


def exact_phases(multiple, period):
    angles = np.asarray(multiple, dtype=np.float64) * (math.pi / period)
    return np.cos(angles), -np.sin(angles)


def constant(table):
    return jnp.asarray(np.asarray(table, dtype=np.float32))


def dft_table(length):
    indices = np.arange(length, dtype=np.int64)
    table_cos, table_sin = exact_phases(2 * (indices[:, None] * indices[None, :] % length), length)
    return constant(table_cos), constant(table_sin)


def split_bf16(table):
    first = table.astype(ml_dtypes.bfloat16)
    second = (table - first.astype(np.float64)).astype(ml_dtypes.bfloat16)
    return np.concatenate((first, second), axis=0)


def mixing(former, latter, formula):
    return jnp.einsum(formula, former, latter, precision=highest)


def multiply_pair(ar, ai, br, bi):
    return ar * br - ai * bi, ar * bi + ai * br


def row_kernel(limbs_ref, matrix_ref, base_cos_ref, base_sin_ref, lane_cos_ref, lane_sin_ref, out_ref):
    number = limbs_ref.shape[0]
    half = lane_cos_ref.shape[0]
    groups, _, _, local, narrow = out_ref.shape
    turn_cos, turn_sin = turn_tables(base_cos_ref, base_sin_ref, lane_cos_ref, lane_sin_ref)
    centred = [limbs_ref[i] - jnp.int32(32768) for i in range(number)]
    upper = [lax.shift_right_arithmetic(value, jnp.int32(8)) for value in centred]
    lower = [value - top * jnp.int32(256) for value, top in zip(centred, upper)]
    pieces = jnp.concatenate(upper + lower, axis=1).astype(jnp.float32).astype(jnp.bfloat16)
    products = jnp.dot(matrix_ref[...], pieces, preferred_element_type=jnp.float32)
    count = 2 * half
    width = number * narrow
    upper_part = products[:count, :width] + products[count:, :width]
    lower_part = products[:count, width:] + products[count:, width:]
    rows = (upper_part * 256.0 + lower_part) * (1.0 / 32768.0)
    for i in range(number):
        real_rows = rows[:half, i * narrow : (i + 1) * narrow]
        imag_rows = rows[half:, i * narrow : (i + 1) * narrow]
        out_ref[:, 0, i] = (real_rows * turn_cos - imag_rows * turn_sin).reshape(groups, local, narrow)
        out_ref[:, 1, i] = (real_rows * turn_sin + imag_rows * turn_cos).reshape(groups, local, narrow)


def turn_tables(base_cos_ref, base_sin_ref, lane_cos_ref, lane_sin_ref):
    device = lax.axis_index("row") * lax.axis_size("col") + lax.axis_index("col")
    pick = (lax.broadcasted_iota(jnp.int32, (1, base_cos_ref.shape[1]), 1) == device).astype(jnp.float32)
    base_cos = jnp.sum(base_cos_ref[...] * pick, axis=1, keepdims=True)
    base_sin = jnp.sum(base_sin_ref[...] * pick, axis=1, keepdims=True)
    lane_cos = lane_cos_ref[...]
    lane_sin = lane_sin_ref[...]
    return base_cos * lane_cos - base_sin * lane_sin, base_cos * lane_sin + base_sin * lane_cos


def row_stage(limbs, matrix, tables, groups):
    number, height, narrow = limbs.shape
    half = tables[2].shape[0]
    local = half // groups
    steps = 2
    block = number // steps
    fixed = lambda shape: pl.BlockSpec(shape, lambda s: (0,) * len(shape))
    return pl.pallas_call(
        row_kernel,
        out_shape=jax.ShapeDtypeStruct((groups, 2, number, local, narrow), jnp.float32),
        grid=(steps,),
        in_specs=[pl.BlockSpec((block, height, narrow), lambda s: (s, 0, 0)), fixed(matrix.shape)]
        + [fixed(table.shape) for table in tables],
        out_specs=pl.BlockSpec((groups, 2, block, local, narrow), lambda s: (0, 0, s, 0, 0)),
        cost_estimate=pl.CostEstimate(
            flops=2 * 4 * half * height * 2 * narrow * number,
            transcendentals=0,
            bytes_accessed=4 * 3 * number * height * narrow + 2 * 4 * half * height,
        ),
    )(limbs, matrix, *tables)


def final_kernel(pieces_ref, leading_ref, trailing_ref, base_cos_ref, base_sin_ref, lane_cos_ref, lane_sin_ref, out_ref, data_ref, *, scale):
    groups, _, outputs, local, narrow = pieces_ref.shape
    half = groups * local
    width = outputs * narrow

    @pl.when(pl.program_id(0) == 0)
    def _():
        turn_cos, turn_sin = turn_tables(base_cos_ref, base_sin_ref, lane_cos_ref, lane_sin_ref)
        turn_cos = turn_cos.reshape(groups, local, narrow)
        turn_sin = turn_sin.reshape(groups, local, narrow)
        columns = []
        for i in range(outputs):
            real = pieces_ref[:, 0, i]
            imag = pieces_ref[:, 1, i]
            untwisted = jnp.concatenate(
                (
                    (real * turn_cos + imag * turn_sin).reshape(half, narrow),
                    (imag * turn_cos - real * turn_sin).reshape(half, narrow),
                ),
                axis=0,
            )
            columns.append(untwisted)
        gathered = jnp.concatenate(columns, axis=1)
        first = gathered.astype(jnp.bfloat16)
        second = (gathered - first.astype(jnp.float32)).astype(jnp.bfloat16)
        data_ref[...] = jnp.concatenate((first, second), axis=1)

    data = data_ref[...]
    leading = jnp.dot(leading_ref[...], data, preferred_element_type=jnp.float32)
    trailing = jnp.dot(trailing_ref[...], data[:, :width], preferred_element_type=jnp.float32)
    small = trailing + leading[:, width:]
    total = (small + leading[:, :width]) * scale
    for i in range(outputs):
        out_ref[i] = total[:, i * narrow : (i + 1) * narrow]


def final_stage(pieces, matrix, tables, scale):
    groups, _, outputs, local, narrow = pieces.shape
    height = matrix.shape[0] // 2
    steps = 2
    block = height // steps
    fixed = lambda shape: pl.BlockSpec(shape, lambda s: (0,) * len(shape))
    return pl.pallas_call(
        functools.partial(final_kernel, scale=scale),
        out_shape=jax.ShapeDtypeStruct((outputs, height, narrow), jnp.float32),
        grid=(steps,),
        in_specs=[
            fixed(pieces.shape),
            pl.BlockSpec((block, matrix.shape[1]), lambda s: (s, 0)),
            pl.BlockSpec((block, matrix.shape[1]), lambda s: (s, 0)),
        ]
        + [fixed(table.shape) for table in tables],
        out_specs=pl.BlockSpec((outputs, block, narrow), lambda s: (0, s, 0)),
        scratch_shapes=[pltpu.VMEM((2 * groups * local, 2 * outputs * narrow), jnp.bfloat16)],
        compiler_params=pltpu.CompilerParams(dimension_semantics=("arbitrary",)),
        cost_estimate=pl.CostEstimate(
            flops=2 * 3 * height * height * 2 * outputs * narrow,
            transcendentals=0,
            bytes_accessed=4 * 3 * outputs * height * narrow + 2 * 2 * height * height,
        ),
    )(pieces, matrix[:height], matrix[height:], *tables)


def fft16(real, imag, sign):
    def dft4(a, b, c, d):
        sum_ac = (a[0] + c[0], a[1] + c[1])
        dif_ac = (a[0] - c[0], a[1] - c[1])
        sum_bd = (b[0] + d[0], b[1] + d[1])
        dif_bd = (b[0] - d[0], b[1] - d[1])
        return (
            (sum_ac[0] + sum_bd[0], sum_ac[1] + sum_bd[1]),
            (dif_ac[0] - sign * dif_bd[1], dif_ac[1] + sign * dif_bd[0]),
            (sum_ac[0] - sum_bd[0], sum_ac[1] - sum_bd[1]),
            (dif_ac[0] + sign * dif_bd[1], dif_ac[1] - sign * dif_bd[0]),
        )

    values = list(zip(real, imag))
    stage = []
    for first in range(4):
        outs = dft4(*(values[4 * second + first] for second in range(4)))
        turned = []
        for low, (re, im) in enumerate(outs):
            if first * low == 0:
                turned.append((re, im))
                continue
            angle = sign * 2.0 * math.pi * first * low / 16.0
            cos_v, sin_v = math.cos(angle), math.sin(angle)
            turned.append((re * cos_v - im * sin_v, re * sin_v + im * cos_v))
        stage.append(turned)
    result = [None] * 16
    for low in range(4):
        outs = dft4(*(stage[first][low] for first in range(4)))
        for high in range(4):
            result[low + 4 * high] = outs[high]
    return [v[0] for v in result], [v[1] for v in result]


def split_dot(values, matrix_ref):
    size = matrix_ref.shape[0] // 2
    first = values.astype(jnp.bfloat16)
    second = (values - first.astype(jnp.float32)).astype(jnp.bfloat16)
    major = matrix_ref[:size]
    minor = matrix_ref[size:]
    small = jnp.dot(second, major, preferred_element_type=jnp.float32) + jnp.dot(
        first, minor, preferred_element_type=jnp.float32
    )
    return small + jnp.dot(first, major, preferred_element_type=jnp.float32)


def column_kernel(in_ref, twist_cos_ref, twist_sin_ref, forward_ref, inverse_ref, out_ref, lifted_ref, mixed_ref):
    groups, _, number, local, narrow = in_ref.shape
    tile = 8
    for operand in range(number):
        for start in range(0, local, tile):
            rows = pl.ds(start, tile)
            real = [in_ref[p, 0, operand, rows, :] for p in range(groups)]
            imag = [in_ref[p, 1, operand, rows, :] for p in range(groups)]
            real, imag = fft16(real, imag, -1.0)
            for k in range(groups):
                cos_v = twist_cos_ref[k : k + 1, :]
                sin_v = twist_sin_ref[k : k + 1, :]
                lifted_ref[k, operand, rows, :narrow] = real[k] * cos_v - imag[k] * sin_v
                lifted_ref[k, operand, rows, narrow:] = real[k] * sin_v + imag[k] * cos_v
    spectra = split_dot(
        lifted_ref[...].reshape(groups * number * local, 2 * narrow), forward_ref
    ).reshape(groups, number, local, 2 * narrow)

    def spectrum(k):
        part = spectra[:, k]
        return part[..., :narrow], part[..., narrow:]

    first = multiply_pair(*spectrum(0), *spectrum(3))
    second = multiply_pair(*spectrum(1), *spectrum(4))
    third_a = multiply_pair(*spectrum(2), *spectrum(4))
    third_b = multiply_pair(*spectrum(0), *spectrum(5))
    combined = (first, second, (third_a[0] + third_b[0], third_a[1] + third_b[1]))
    for index, (re, im) in enumerate(combined):
        mixed_ref[:, index, :, :narrow] = re
        mixed_ref[:, index, :, narrow:] = im
    outputs = mixed_ref.shape[1]
    mixed_ref[...] = split_dot(
        mixed_ref[...].reshape(groups * outputs * local, 2 * narrow), inverse_ref
    ).reshape(groups, outputs, local, 2 * narrow)
    for operand in range(outputs):
        for start in range(0, local, tile):
            rows = pl.ds(start, tile)
            real = []
            imag = []
            for k in range(groups):
                re = mixed_ref[k, operand, rows, :narrow]
                im = mixed_ref[k, operand, rows, narrow:]
                cos_v = twist_cos_ref[k : k + 1, :]
                sin_v = twist_sin_ref[k : k + 1, :]
                real.append(re * cos_v + im * sin_v)
                imag.append(im * cos_v - re * sin_v)
            real, imag = fft16(real, imag, 1.0)
            for p in range(groups):
                out_ref[p, 0, operand, rows, :] = real[p]
                out_ref[p, 1, operand, rows, :] = imag[p]


def column_stage(received, twist_cos, twist_sin, forward, inverse):
    groups, _, number, local, narrow = received.shape
    outputs = 3
    rows = groups * local
    steps = 2
    block = local // steps
    fixed = lambda shape: pl.BlockSpec(shape, lambda s: (0,) * len(shape))
    return pl.pallas_call(
        column_kernel,
        out_shape=jax.ShapeDtypeStruct((groups, 2, outputs, local, narrow), jnp.float32),
        grid=(steps,),
        in_specs=[pl.BlockSpec((groups, 2, number, block, narrow), lambda s: (0, 0, 0, s, 0))]
        + [fixed(table.shape) for table in (twist_cos, twist_sin, forward, inverse)],
        out_specs=pl.BlockSpec((groups, 2, outputs, block, narrow), lambda s: (0, 0, 0, s, 0)),
        scratch_shapes=[
            pltpu.VMEM((groups, number, block, 2 * narrow), jnp.float32),
            pltpu.VMEM((groups, outputs, block, 2 * narrow), jnp.float32),
        ],
        cost_estimate=pl.CostEstimate(
            flops=3 * 2 * rows * (number + outputs) * (2 * narrow) ** 2,
            transcendentals=0,
            bytes_accessed=4 * rows * narrow * 2 * (number + outputs),
        ),
    )(received, twist_cos, twist_sin, forward, inverse)


def body(limbs):
    groups = lax.axis_size(("row", "col"))
    number, height, narrow = limbs.shape
    breadth = narrow * groups
    limb_total = height * breadth
    half = height // 2
    local = half // groups
    device = lax.axis_index(("row", "col"))

    half_index = np.arange(half, dtype=np.int64)
    row_index = np.arange(height, dtype=np.int64)
    row_cos_exact, row_sin_exact = exact_phases(
        row_index[None, :] * (2 * half_index[:, None] + 1) % (2 * height), height
    )
    row_matrix = jnp.asarray(split_bf16(np.concatenate((row_cos_exact, row_sin_exact), axis=0)))
    final_matrix = jnp.asarray(split_bf16(np.concatenate((row_cos_exact, row_sin_exact), axis=0).T))
    device_index = np.arange(groups, dtype=np.int64)
    base_cos, base_sin = exact_phases(
        device_index[:, None] * narrow * (2 * half_index[None, :] + 1), limb_total
    )
    base_cos_table = np.zeros((half, narrow))
    base_sin_table = np.zeros((half, narrow))
    base_cos_table[:, :groups] = base_cos.T
    base_sin_table[:, :groups] = base_sin.T
    lane_index = np.arange(narrow, dtype=np.int64)
    lane_cos, lane_sin = exact_phases(lane_index[None, :] * (2 * half_index[:, None] + 1), limb_total)
    tables = (
        constant(base_cos_table),
        constant(base_sin_table),
        constant(lane_cos),
        constant(lane_sin),
    )

    send = row_stage(limbs, row_matrix, tables, groups)
    received = lax.all_to_all(send, ("row", "col"), 0, 0, tiled=True)

    outer_index = np.arange(groups, dtype=np.int64)
    inner_index = np.arange(narrow, dtype=np.int64)
    twist_cos, twist_sin = exact_phases(
        2 * (outer_index[:, None] * inner_index[None, :] % breadth), breadth
    )
    inner_cos, inner_sin = exact_phases(2 * (inner_index[:, None] * inner_index[None, :] % narrow), narrow)
    forward = np.block([[inner_cos, inner_sin], [-inner_sin, inner_cos]])
    inverse = np.block([[inner_cos, -inner_sin], [inner_sin, inner_cos]])
    outgoing = column_stage(
        received,
        constant(twist_cos),
        constant(twist_sin),
        jnp.asarray(split_bf16(forward)),
        jnp.asarray(split_bf16(inverse)),
    )
    pieces = lax.all_to_all(outgoing, ("row", "col"), 0, 0, tiled=True)

    scale_factor = 2.0 / (limb_total * math.sqrt(limb_total))
    return final_stage(pieces, final_matrix, tables, scale_factor)


def solution(mesh):
    in_specs = (P(None, "pair", ("row", "col")),)
    out_specs = P(None, "pair", ("row", "col"))
    return jax.shard_map(body, mesh=mesh, in_specs=in_specs, out_specs=out_specs, check_vma=False)
```

```python
import functools
import math

import jax
import jax.numpy as jnp
import ml_dtypes
import numpy as np
from jax import lax
from jax.experimental import pallas as pl
from jax.experimental.pallas import tpu as pltpu
from jax.sharding import PartitionSpec as P

highest = lax.Precision.HIGHEST


def phases(multiple, period):
    angles = multiple.astype(jnp.float32) * (math.pi / period)
    return (jnp.cos(angles), -jnp.sin(angles))


def exact_phases(multiple, period):
    angles = np.asarray(multiple, dtype=np.float64) * (math.pi / period)
    return np.cos(angles), -np.sin(angles)


def constant(table):
    return jnp.asarray(np.asarray(table, dtype=np.float32))


def dft_table(length):
    indices = np.arange(length, dtype=np.int64)
    table_cos, table_sin = exact_phases(2 * (indices[:, None] * indices[None, :] % length), length)
    return constant(table_cos), constant(table_sin)


def split_bf16(table):
    first = table.astype(ml_dtypes.bfloat16)
    second = (table - first.astype(np.float64)).astype(ml_dtypes.bfloat16)
    return np.concatenate((first, second), axis=0)


def mixing(former, latter, formula):
    return jnp.einsum(formula, former, latter, precision=highest)


def multiply_pair(ar, ai, br, bi):
    return ar * br - ai * bi, ar * bi + ai * br


def row_kernel(limbs_ref, matrix_ref, base_cos_ref, base_sin_ref, lane_cos_ref, lane_sin_ref, out_ref):
    number = limbs_ref.shape[0]
    half = lane_cos_ref.shape[0]
    groups, _, _, local, narrow = out_ref.shape
    turn_cos, turn_sin = turn_tables(base_cos_ref, base_sin_ref, lane_cos_ref, lane_sin_ref)
    centred = [limbs_ref[i] - jnp.int32(32768) for i in range(number)]
    upper = [lax.shift_right_arithmetic(value, jnp.int32(8)) for value in centred]
    lower = [value - top * jnp.int32(256) for value, top in zip(centred, upper)]
    pieces = jnp.concatenate(upper + lower, axis=1).astype(jnp.float32).astype(jnp.bfloat16)
    products = jnp.dot(matrix_ref[...], pieces, preferred_element_type=jnp.float32)
    count = 2 * half
    width = number * narrow
    upper_part = products[:count, :width] + products[count:, :width]
    lower_part = products[:count, width:] + products[count:, width:]
    rows = (upper_part * 256.0 + lower_part) * (1.0 / 32768.0)
    for i in range(number):
        real_rows = rows[:half, i * narrow : (i + 1) * narrow]
        imag_rows = rows[half:, i * narrow : (i + 1) * narrow]
        out_ref[:, 0, i] = (real_rows * turn_cos - imag_rows * turn_sin).reshape(groups, local, narrow)
        out_ref[:, 1, i] = (real_rows * turn_sin + imag_rows * turn_cos).reshape(groups, local, narrow)


def turn_tables(base_cos_ref, base_sin_ref, lane_cos_ref, lane_sin_ref):
    device = lax.axis_index("row") * lax.axis_size("col") + lax.axis_index("col")
    pick = (lax.broadcasted_iota(jnp.int32, (1, base_cos_ref.shape[1]), 1) == device).astype(jnp.float32)
    base_cos = jnp.sum(base_cos_ref[...] * pick, axis=1, keepdims=True)
    base_sin = jnp.sum(base_sin_ref[...] * pick, axis=1, keepdims=True)
    lane_cos = lane_cos_ref[...]
    lane_sin = lane_sin_ref[...]
    return base_cos * lane_cos - base_sin * lane_sin, base_cos * lane_sin + base_sin * lane_cos


def row_stage(limbs, matrix, tables, groups):
    number, height, narrow = limbs.shape
    half = tables[2].shape[0]
    local = half // groups
    steps = 2
    block = number // steps
    fixed = lambda shape: pl.BlockSpec(shape, lambda s: (0,) * len(shape))
    return pl.pallas_call(
        row_kernel,
        out_shape=jax.ShapeDtypeStruct((groups, 2, number, local, narrow), jnp.float32),
        grid=(steps,),
        in_specs=[pl.BlockSpec((block, height, narrow), lambda s: (s, 0, 0)), fixed(matrix.shape)]
        + [fixed(table.shape) for table in tables],
        out_specs=pl.BlockSpec((groups, 2, block, local, narrow), lambda s: (0, 0, s, 0, 0)),
        cost_estimate=pl.CostEstimate(
            flops=2 * 4 * half * height * 2 * narrow * number,
            transcendentals=0,
            bytes_accessed=4 * 3 * number * height * narrow + 2 * 4 * half * height,
        ),
    )(limbs, matrix, *tables)


def final_kernel(pieces_ref, matrix_ref, base_cos_ref, base_sin_ref, lane_cos_ref, lane_sin_ref, out_ref, *, scale):
    groups, _, outputs, local, narrow = pieces_ref.shape
    half = groups * local
    turn_cos, turn_sin = turn_tables(base_cos_ref, base_sin_ref, lane_cos_ref, lane_sin_ref)
    turn_cos = turn_cos.reshape(groups, local, narrow)
    turn_sin = turn_sin.reshape(groups, local, narrow)
    columns = []
    for i in range(outputs):
        real = pieces_ref[:, 0, i]
        imag = pieces_ref[:, 1, i]
        untwisted = jnp.concatenate(
            (
                (real * turn_cos + imag * turn_sin).reshape(half, narrow),
                (imag * turn_cos - real * turn_sin).reshape(half, narrow),
            ),
            axis=0,
        )
        columns.append(untwisted)
    gathered = jnp.concatenate(columns, axis=1)
    first = gathered.astype(jnp.bfloat16)
    second = (gathered - first.astype(jnp.float32)).astype(jnp.bfloat16)
    height = matrix_ref.shape[0] // 2
    width = outputs * narrow
    leading = jnp.dot(
        matrix_ref[:height], jnp.concatenate((first, second), axis=1), preferred_element_type=jnp.float32
    )
    trailing = jnp.dot(matrix_ref[height:], first, preferred_element_type=jnp.float32)
    small = trailing + leading[:, width:]
    total = (small + leading[:, :width]) * scale
    for i in range(outputs):
        out_ref[i] = total[:, i * narrow : (i + 1) * narrow]


def final_stage(pieces, matrix, tables, scale):
    groups, _, outputs, local, narrow = pieces.shape
    height = matrix.shape[0] // 2
    return pl.pallas_call(
        functools.partial(final_kernel, scale=scale),
        out_shape=jax.ShapeDtypeStruct((outputs, height, narrow), jnp.float32),
        cost_estimate=pl.CostEstimate(
            flops=2 * 3 * height * height * 2 * outputs * narrow,
            transcendentals=0,
            bytes_accessed=4 * 3 * outputs * height * narrow + 2 * 2 * height * height,
        ),
    )(pieces, matrix, *tables)


def fft16(real, imag, sign):
    def dft4(a, b, c, d):
        sum_ac = (a[0] + c[0], a[1] + c[1])
        dif_ac = (a[0] - c[0], a[1] - c[1])
        sum_bd = (b[0] + d[0], b[1] + d[1])
        dif_bd = (b[0] - d[0], b[1] - d[1])
        return (
            (sum_ac[0] + sum_bd[0], sum_ac[1] + sum_bd[1]),
            (dif_ac[0] - sign * dif_bd[1], dif_ac[1] + sign * dif_bd[0]),
            (sum_ac[0] - sum_bd[0], sum_ac[1] - sum_bd[1]),
            (dif_ac[0] + sign * dif_bd[1], dif_ac[1] - sign * dif_bd[0]),
        )

    values = list(zip(real, imag))
    stage = []
    for first in range(4):
        outs = dft4(*(values[4 * second + first] for second in range(4)))
        turned = []
        for low, (re, im) in enumerate(outs):
            if first * low == 0:
                turned.append((re, im))
                continue
            angle = sign * 2.0 * math.pi * first * low / 16.0
            cos_v, sin_v = math.cos(angle), math.sin(angle)
            turned.append((re * cos_v - im * sin_v, re * sin_v + im * cos_v))
        stage.append(turned)
    result = [None] * 16
    for low in range(4):
        outs = dft4(*(stage[first][low] for first in range(4)))
        for high in range(4):
            result[low + 4 * high] = outs[high]
    return [v[0] for v in result], [v[1] for v in result]


def split_dot(values, matrix_ref):
    size = matrix_ref.shape[0] // 2
    first = values.astype(jnp.bfloat16)
    second = (values - first.astype(jnp.float32)).astype(jnp.bfloat16)
    major = matrix_ref[:size]
    small = jnp.dot(
        jnp.concatenate((second, first), axis=1), matrix_ref[...], preferred_element_type=jnp.float32
    )
    return small + jnp.dot(first, major, preferred_element_type=jnp.float32)


def column_kernel(in_ref, twist_cos_ref, twist_sin_ref, forward_ref, inverse_ref, out_ref, lifted_ref, mixed_ref):
    groups, _, number, local, narrow = in_ref.shape
    tile = 8
    for operand in range(number):
        for start in range(0, local, tile):
            rows = pl.ds(start, tile)
            real = [in_ref[p, 0, operand, rows, :] for p in range(groups)]
            imag = [in_ref[p, 1, operand, rows, :] for p in range(groups)]
            real, imag = fft16(real, imag, -1.0)
            for k in range(groups):
                cos_v = twist_cos_ref[k : k + 1, :]
                sin_v = twist_sin_ref[k : k + 1, :]
                lifted_ref[k, operand, rows, :narrow] = real[k] * cos_v - imag[k] * sin_v
                lifted_ref[k, operand, rows, narrow:] = real[k] * sin_v + imag[k] * cos_v
    spectra = split_dot(
        lifted_ref[...].reshape(groups * number * local, 2 * narrow), forward_ref
    ).reshape(groups, number, local, 2 * narrow)

    def spectrum(k):
        part = spectra[:, k]
        return part[..., :narrow], part[..., narrow:]

    first = multiply_pair(*spectrum(0), *spectrum(3))
    second = multiply_pair(*spectrum(1), *spectrum(4))
    third_a = multiply_pair(*spectrum(2), *spectrum(4))
    third_b = multiply_pair(*spectrum(0), *spectrum(5))
    combined = (first, second, (third_a[0] + third_b[0], third_a[1] + third_b[1]))
    for index, (re, im) in enumerate(combined):
        mixed_ref[:, index, :, :narrow] = re
        mixed_ref[:, index, :, narrow:] = im
    outputs = mixed_ref.shape[1]
    mixed_ref[...] = split_dot(
        mixed_ref[...].reshape(groups * outputs * local, 2 * narrow), inverse_ref
    ).reshape(groups, outputs, local, 2 * narrow)
    for operand in range(outputs):
        for start in range(0, local, tile):
            rows = pl.ds(start, tile)
            real = []
            imag = []
            for k in range(groups):
                re = mixed_ref[k, operand, rows, :narrow]
                im = mixed_ref[k, operand, rows, narrow:]
                cos_v = twist_cos_ref[k : k + 1, :]
                sin_v = twist_sin_ref[k : k + 1, :]
                real.append(re * cos_v + im * sin_v)
                imag.append(im * cos_v - re * sin_v)
            real, imag = fft16(real, imag, 1.0)
            for p in range(groups):
                out_ref[p, 0, operand, rows, :] = real[p]
                out_ref[p, 1, operand, rows, :] = imag[p]


def column_stage(received, twist_cos, twist_sin, forward, inverse):
    groups, _, number, local, narrow = received.shape
    outputs = 3
    rows = groups * local
    steps = 2
    block = local // steps
    fixed = lambda shape: pl.BlockSpec(shape, lambda s: (0,) * len(shape))
    return pl.pallas_call(
        column_kernel,
        out_shape=jax.ShapeDtypeStruct((groups, 2, outputs, local, narrow), jnp.float32),
        grid=(steps,),
        in_specs=[pl.BlockSpec((groups, 2, number, block, narrow), lambda s: (0, 0, 0, s, 0))]
        + [fixed(table.shape) for table in (twist_cos, twist_sin, forward, inverse)],
        out_specs=pl.BlockSpec((groups, 2, outputs, block, narrow), lambda s: (0, 0, 0, s, 0)),
        scratch_shapes=[
            pltpu.VMEM((groups, number, block, 2 * narrow), jnp.float32),
            pltpu.VMEM((groups, outputs, block, 2 * narrow), jnp.float32),
        ],
        cost_estimate=pl.CostEstimate(
            flops=3 * 2 * rows * (number + outputs) * (2 * narrow) ** 2,
            transcendentals=0,
            bytes_accessed=4 * rows * narrow * 2 * (number + outputs),
        ),
    )(received, twist_cos, twist_sin, forward, inverse)


def body(limbs):
    groups = lax.axis_size(("row", "col"))
    number, height, narrow = limbs.shape
    breadth = narrow * groups
    limb_total = height * breadth
    half = height // 2
    local = half // groups
    device = lax.axis_index(("row", "col"))

    half_index = np.arange(half, dtype=np.int64)
    row_index = np.arange(height, dtype=np.int64)
    row_cos_exact, row_sin_exact = exact_phases(
        row_index[None, :] * (2 * half_index[:, None] + 1) % (2 * height), height
    )
    row_matrix = jnp.asarray(split_bf16(np.concatenate((row_cos_exact, row_sin_exact), axis=0)))
    final_matrix = jnp.asarray(split_bf16(np.concatenate((row_cos_exact, row_sin_exact), axis=0).T))
    device_index = np.arange(groups, dtype=np.int64)
    base_cos, base_sin = exact_phases(
        device_index[:, None] * narrow * (2 * half_index[None, :] + 1), limb_total
    )
    base_cos_table = np.zeros((half, narrow))
    base_sin_table = np.zeros((half, narrow))
    base_cos_table[:, :groups] = base_cos.T
    base_sin_table[:, :groups] = base_sin.T
    lane_index = np.arange(narrow, dtype=np.int64)
    lane_cos, lane_sin = exact_phases(lane_index[None, :] * (2 * half_index[:, None] + 1), limb_total)
    tables = (
        constant(base_cos_table),
        constant(base_sin_table),
        constant(lane_cos),
        constant(lane_sin),
    )

    send = row_stage(limbs, row_matrix, tables, groups)
    received = lax.all_to_all(send, ("row", "col"), 0, 0, tiled=True)

    outer_index = np.arange(groups, dtype=np.int64)
    inner_index = np.arange(narrow, dtype=np.int64)
    twist_cos, twist_sin = exact_phases(
        2 * (outer_index[:, None] * inner_index[None, :] % breadth), breadth
    )
    inner_cos, inner_sin = exact_phases(2 * (inner_index[:, None] * inner_index[None, :] % narrow), narrow)
    forward = np.block([[inner_cos, inner_sin], [-inner_sin, inner_cos]])
    inverse = np.block([[inner_cos, -inner_sin], [inner_sin, inner_cos]])
    outgoing = column_stage(
        received,
        constant(twist_cos),
        constant(twist_sin),
        jnp.asarray(split_bf16(forward)),
        jnp.asarray(split_bf16(inverse)),
    )
    pieces = lax.all_to_all(outgoing, ("row", "col"), 0, 0, tiled=True)

    scale_factor = 2.0 / (limb_total * math.sqrt(limb_total))
    return final_stage(pieces, final_matrix, tables, scale_factor)


def solution(mesh):
    in_specs = (P(None, "pair", ("row", "col")),)
    out_specs = P(None, "pair", ("row", "col"))
    return jax.shard_map(body, mesh=mesh, in_specs=in_specs, out_specs=out_specs, check_vma=False)
```

```python
import functools
import math

import jax
import jax.numpy as jnp
import ml_dtypes
import numpy as np
from jax import lax
from jax.experimental import pallas as pl
from jax.experimental.pallas import tpu as pltpu
from jax.sharding import PartitionSpec as P

highest = lax.Precision.HIGHEST


def phases(multiple, period):
    angles = multiple.astype(jnp.float32) * (math.pi / period)
    return (jnp.cos(angles), -jnp.sin(angles))


def exact_phases(multiple, period):
    angles = np.asarray(multiple, dtype=np.float64) * (math.pi / period)
    return np.cos(angles), -np.sin(angles)


def constant(table):
    return jnp.asarray(np.asarray(table, dtype=np.float32))


def dft_table(length):
    indices = np.arange(length, dtype=np.int64)
    table_cos, table_sin = exact_phases(2 * (indices[:, None] * indices[None, :] % length), length)
    return constant(table_cos), constant(table_sin)


def split_bf16(table):
    first = table.astype(ml_dtypes.bfloat16)
    second = (table - first.astype(np.float64)).astype(ml_dtypes.bfloat16)
    return np.concatenate((first, second), axis=0)


def mixing(former, latter, formula):
    return jnp.einsum(formula, former, latter, precision=highest)


def multiply_pair(ar, ai, br, bi):
    return ar * br - ai * bi, ar * bi + ai * br


def row_kernel(limbs_ref, matrix_ref, base_cos_ref, base_sin_ref, lane_cos_ref, lane_sin_ref, out_ref):
    number = limbs_ref.shape[0]
    half = lane_cos_ref.shape[0]
    groups, _, _, local, narrow = out_ref.shape
    turn_cos, turn_sin = turn_tables(base_cos_ref, base_sin_ref, lane_cos_ref, lane_sin_ref)
    centred = [limbs_ref[i] - jnp.int32(32768) for i in range(number)]
    upper = [lax.shift_right_arithmetic(value, jnp.int32(8)) for value in centred]
    lower = [value - top * jnp.int32(256) for value, top in zip(centred, upper)]
    upper = [value - low for value, low in zip(centred, lower)]
    pieces = jnp.concatenate(upper + lower, axis=1).astype(jnp.float32).astype(jnp.bfloat16)
    products = jnp.dot(matrix_ref[...], pieces, preferred_element_type=jnp.float32)
    count = 2 * half
    width = number * narrow
    upper_part = products[:count, :width] + products[count:, :width]
    lower_part = products[:count, width:] + products[count:, width:]
    rows = upper_part + lower_part
    for i in range(number):
        real_rows = rows[:half, i * narrow : (i + 1) * narrow]
        imag_rows = rows[half:, i * narrow : (i + 1) * narrow]
        out_ref[:, 0, i] = (real_rows * turn_cos - imag_rows * turn_sin).reshape(groups, local, narrow)
        out_ref[:, 1, i] = (real_rows * turn_sin + imag_rows * turn_cos).reshape(groups, local, narrow)


def turn_tables(base_cos_ref, base_sin_ref, lane_cos_ref, lane_sin_ref):
    device = lax.axis_index("row") * lax.axis_size("col") + lax.axis_index("col")
    pick = (lax.broadcasted_iota(jnp.int32, (1, base_cos_ref.shape[1]), 1) == device).astype(jnp.float32)
    base_cos = jnp.sum(base_cos_ref[...] * pick, axis=1, keepdims=True)
    base_sin = jnp.sum(base_sin_ref[...] * pick, axis=1, keepdims=True)
    lane_cos = lane_cos_ref[...]
    lane_sin = lane_sin_ref[...]
    return base_cos * lane_cos - base_sin * lane_sin, base_cos * lane_sin + base_sin * lane_cos


def row_stage(limbs, matrix, tables, groups):
    number, height, narrow = limbs.shape
    half = tables[2].shape[0]
    local = half // groups
    steps = 2
    block = number // steps
    fixed = lambda shape: pl.BlockSpec(shape, lambda s: (0,) * len(shape))
    return pl.pallas_call(
        row_kernel,
        out_shape=jax.ShapeDtypeStruct((groups, 2, number, local, narrow), jnp.float32),
        grid=(steps,),
        in_specs=[pl.BlockSpec((block, height, narrow), lambda s: (s, 0, 0)), fixed(matrix.shape)]
        + [fixed(table.shape) for table in tables],
        out_specs=pl.BlockSpec((groups, 2, block, local, narrow), lambda s: (0, 0, s, 0, 0)),
        cost_estimate=pl.CostEstimate(
            flops=2 * 4 * half * height * 2 * narrow * number,
            transcendentals=0,
            bytes_accessed=4 * 3 * number * height * narrow + 2 * 4 * half * height,
        ),
    )(limbs, matrix, *tables)


def final_kernel(pieces_ref, matrix_ref, base_cos_ref, base_sin_ref, lane_cos_ref, lane_sin_ref, out_ref, *, scale):
    groups, _, outputs, local, narrow = pieces_ref.shape
    half = groups * local
    turn_cos, turn_sin = turn_tables(base_cos_ref, base_sin_ref, lane_cos_ref, lane_sin_ref)
    turn_cos = turn_cos.reshape(groups, local, narrow)
    turn_sin = turn_sin.reshape(groups, local, narrow)
    columns = []
    for i in range(outputs):
        real = pieces_ref[:, 0, i]
        imag = pieces_ref[:, 1, i]
        untwisted = jnp.concatenate(
            (
                (real * turn_cos + imag * turn_sin).reshape(half, narrow),
                (imag * turn_cos - real * turn_sin).reshape(half, narrow),
            ),
            axis=0,
        )
        columns.append(untwisted)
    gathered = jnp.concatenate(columns, axis=1)
    first = gathered.astype(jnp.bfloat16)
    second = (gathered - first.astype(jnp.float32)).astype(jnp.bfloat16)
    height = matrix_ref.shape[0] // 2
    width = outputs * narrow
    leading = jnp.dot(
        matrix_ref[:height], jnp.concatenate((first, second), axis=1), preferred_element_type=jnp.float32
    )
    trailing = jnp.dot(matrix_ref[height:], first, preferred_element_type=jnp.float32)
    small = trailing + leading[:, width:]
    total = (small + leading[:, :width]) * scale
    for i in range(outputs):
        out_ref[i] = total[:, i * narrow : (i + 1) * narrow]


def final_stage(pieces, matrix, tables, scale):
    groups, _, outputs, local, narrow = pieces.shape
    height = matrix.shape[0] // 2
    return pl.pallas_call(
        functools.partial(final_kernel, scale=scale),
        out_shape=jax.ShapeDtypeStruct((outputs, height, narrow), jnp.float32),
        cost_estimate=pl.CostEstimate(
            flops=2 * 3 * height * height * 2 * outputs * narrow,
            transcendentals=0,
            bytes_accessed=4 * 3 * outputs * height * narrow + 2 * 2 * height * height,
        ),
    )(pieces, matrix, *tables)


def fft16(real, imag, sign):
    def dft4(a, b, c, d):
        sum_ac = (a[0] + c[0], a[1] + c[1])
        dif_ac = (a[0] - c[0], a[1] - c[1])
        sum_bd = (b[0] + d[0], b[1] + d[1])
        dif_bd = (b[0] - d[0], b[1] - d[1])
        return (
            (sum_ac[0] + sum_bd[0], sum_ac[1] + sum_bd[1]),
            (dif_ac[0] - sign * dif_bd[1], dif_ac[1] + sign * dif_bd[0]),
            (sum_ac[0] - sum_bd[0], sum_ac[1] - sum_bd[1]),
            (dif_ac[0] + sign * dif_bd[1], dif_ac[1] - sign * dif_bd[0]),
        )

    values = list(zip(real, imag))
    stage = []
    for first in range(4):
        outs = dft4(*(values[4 * second + first] for second in range(4)))
        turned = []
        for low, (re, im) in enumerate(outs):
            if first * low == 0:
                turned.append((re, im))
                continue
            angle = sign * 2.0 * math.pi * first * low / 16.0
            cos_v, sin_v = math.cos(angle), math.sin(angle)
            turned.append((re * cos_v - im * sin_v, re * sin_v + im * cos_v))
        stage.append(turned)
    result = [None] * 16
    for low in range(4):
        outs = dft4(*(stage[first][low] for first in range(4)))
        for high in range(4):
            result[low + 4 * high] = outs[high]
    return [v[0] for v in result], [v[1] for v in result]


def split_dot(values, matrix_ref):
    size = matrix_ref.shape[0] // 2
    first = values.astype(jnp.bfloat16)
    second = (values - first.astype(jnp.float32)).astype(jnp.bfloat16)
    major = matrix_ref[:size]
    small = jnp.dot(
        jnp.concatenate((second, first), axis=1), matrix_ref[...], preferred_element_type=jnp.float32
    )
    return small + jnp.dot(first, major, preferred_element_type=jnp.float32)


def column_kernel(in_ref, twist_cos_ref, twist_sin_ref, forward_ref, inverse_ref, out_ref, lifted_ref, mixed_ref):
    groups, _, number, local, narrow = in_ref.shape
    tile = 8
    for operand in range(number):
        for start in range(0, local, tile):
            rows = pl.ds(start, tile)
            real = [in_ref[p, 0, operand, rows, :] for p in range(groups)]
            imag = [in_ref[p, 1, operand, rows, :] for p in range(groups)]
            real, imag = fft16(real, imag, -1.0)
            for k in range(groups):
                cos_v = twist_cos_ref[k : k + 1, :]
                sin_v = twist_sin_ref[k : k + 1, :]
                lifted_ref[k, operand, rows, :narrow] = real[k] * cos_v - imag[k] * sin_v
                lifted_ref[k, operand, rows, narrow:] = real[k] * sin_v + imag[k] * cos_v
    spectra = split_dot(
        lifted_ref[...].reshape(groups * number * local, 2 * narrow), forward_ref
    ).reshape(groups, number, local, 2 * narrow)

    def spectrum(k):
        part = spectra[:, k]
        return part[..., :narrow], part[..., narrow:]

    first = multiply_pair(*spectrum(0), *spectrum(3))
    second = multiply_pair(*spectrum(1), *spectrum(4))
    third_a = multiply_pair(*spectrum(2), *spectrum(4))
    third_b = multiply_pair(*spectrum(0), *spectrum(5))
    combined = (first, second, (third_a[0] + third_b[0], third_a[1] + third_b[1]))
    for index, (re, im) in enumerate(combined):
        mixed_ref[:, index, :, :narrow] = re
        mixed_ref[:, index, :, narrow:] = im
    outputs = mixed_ref.shape[1]
    mixed_ref[...] = split_dot(
        mixed_ref[...].reshape(groups * outputs * local, 2 * narrow), inverse_ref
    ).reshape(groups, outputs, local, 2 * narrow)
    for operand in range(outputs):
        for start in range(0, local, tile):
            rows = pl.ds(start, tile)
            real = []
            imag = []
            for k in range(groups):
                re = mixed_ref[k, operand, rows, :narrow]
                im = mixed_ref[k, operand, rows, narrow:]
                cos_v = twist_cos_ref[k : k + 1, :]
                sin_v = twist_sin_ref[k : k + 1, :]
                real.append(re * cos_v + im * sin_v)
                imag.append(im * cos_v - re * sin_v)
            real, imag = fft16(real, imag, 1.0)
            for p in range(groups):
                out_ref[p, 0, operand, rows, :] = real[p]
                out_ref[p, 1, operand, rows, :] = imag[p]


def column_stage(received, twist_cos, twist_sin, forward, inverse):
    groups, _, number, local, narrow = received.shape
    outputs = 3
    rows = groups * local
    steps = 2
    block = local // steps
    fixed = lambda shape: pl.BlockSpec(shape, lambda s: (0,) * len(shape))
    return pl.pallas_call(
        column_kernel,
        out_shape=jax.ShapeDtypeStruct((groups, 2, outputs, local, narrow), jnp.float32),
        grid=(steps,),
        in_specs=[pl.BlockSpec((groups, 2, number, block, narrow), lambda s: (0, 0, 0, s, 0))]
        + [fixed(table.shape) for table in (twist_cos, twist_sin, forward, inverse)],
        out_specs=pl.BlockSpec((groups, 2, outputs, block, narrow), lambda s: (0, 0, 0, s, 0)),
        scratch_shapes=[
            pltpu.VMEM((groups, number, block, 2 * narrow), jnp.float32),
            pltpu.VMEM((groups, outputs, block, 2 * narrow), jnp.float32),
        ],
        cost_estimate=pl.CostEstimate(
            flops=3 * 2 * rows * (number + outputs) * (2 * narrow) ** 2,
            transcendentals=0,
            bytes_accessed=4 * rows * narrow * 2 * (number + outputs),
        ),
    )(received, twist_cos, twist_sin, forward, inverse)


def body(limbs):
    groups = lax.axis_size(("row", "col"))
    number, height, narrow = limbs.shape
    breadth = narrow * groups
    limb_total = height * breadth
    half = height // 2
    local = half // groups
    device = lax.axis_index(("row", "col"))

    half_index = np.arange(half, dtype=np.int64)
    row_index = np.arange(height, dtype=np.int64)
    row_cos_exact, row_sin_exact = exact_phases(
        row_index[None, :] * (2 * half_index[:, None] + 1) % (2 * height), height
    )
    row_matrix = jnp.asarray(split_bf16(np.concatenate((row_cos_exact, row_sin_exact), axis=0) / 32768.0))
    final_matrix = jnp.asarray(split_bf16(np.concatenate((row_cos_exact, row_sin_exact), axis=0).T))
    device_index = np.arange(groups, dtype=np.int64)
    base_cos, base_sin = exact_phases(
        device_index[:, None] * narrow * (2 * half_index[None, :] + 1), limb_total
    )
    base_cos_table = np.zeros((half, narrow))
    base_sin_table = np.zeros((half, narrow))
    base_cos_table[:, :groups] = base_cos.T
    base_sin_table[:, :groups] = base_sin.T
    lane_index = np.arange(narrow, dtype=np.int64)
    lane_cos, lane_sin = exact_phases(lane_index[None, :] * (2 * half_index[:, None] + 1), limb_total)
    tables = (
        constant(base_cos_table),
        constant(base_sin_table),
        constant(lane_cos),
        constant(lane_sin),
    )

    send = row_stage(limbs, row_matrix, tables, groups)
    received = lax.all_to_all(send, ("row", "col"), 0, 0, tiled=True)

    outer_index = np.arange(groups, dtype=np.int64)
    inner_index = np.arange(narrow, dtype=np.int64)
    twist_cos, twist_sin = exact_phases(
        2 * (outer_index[:, None] * inner_index[None, :] % breadth), breadth
    )
    inner_cos, inner_sin = exact_phases(2 * (inner_index[:, None] * inner_index[None, :] % narrow), narrow)
    forward = np.block([[inner_cos, inner_sin], [-inner_sin, inner_cos]])
    inverse = np.block([[inner_cos, -inner_sin], [inner_sin, inner_cos]])
    outgoing = column_stage(
        received,
        constant(twist_cos),
        constant(twist_sin),
        jnp.asarray(split_bf16(forward)),
        jnp.asarray(split_bf16(inverse)),
    )
    pieces = lax.all_to_all(outgoing, ("row", "col"), 0, 0, tiled=True)

    scale_factor = 2.0 / (limb_total * math.sqrt(limb_total))
    return final_stage(pieces, final_matrix, tables, scale_factor)


def solution(mesh):
    in_specs = (P(None, "pair", ("row", "col")),)
    out_specs = P(None, "pair", ("row", "col"))
    return jax.shard_map(body, mesh=mesh, in_specs=in_specs, out_specs=out_specs, check_vma=False)
```

```python
import functools
import math

import jax
import jax.numpy as jnp
import ml_dtypes
import numpy as np
from jax import lax
from jax.experimental import pallas as pl
from jax.experimental.pallas import tpu as pltpu
from jax.sharding import PartitionSpec as P

highest = lax.Precision.HIGHEST


def phases(multiple, period):
    angles = multiple.astype(jnp.float32) * (math.pi / period)
    return (jnp.cos(angles), -jnp.sin(angles))


def exact_phases(multiple, period):
    angles = np.asarray(multiple, dtype=np.float64) * (math.pi / period)
    return np.cos(angles), -np.sin(angles)


def constant(table):
    return jnp.asarray(np.asarray(table, dtype=np.float32))


def dft_table(length):
    indices = np.arange(length, dtype=np.int64)
    table_cos, table_sin = exact_phases(2 * (indices[:, None] * indices[None, :] % length), length)
    return constant(table_cos), constant(table_sin)


def split_bf16(table):
    first = table.astype(ml_dtypes.bfloat16)
    second = (table - first.astype(np.float64)).astype(ml_dtypes.bfloat16)
    return np.concatenate((first, second), axis=0)


def mixing(former, latter, formula):
    return jnp.einsum(formula, former, latter, precision=highest)


def multiply_pair(ar, ai, br, bi):
    return ar * br - ai * bi, ar * bi + ai * br


def row_kernel(limbs_ref, matrix_ref, base_cos_ref, base_sin_ref, lane_cos_ref, lane_sin_ref, out_ref):
    number = limbs_ref.shape[0]
    half = lane_cos_ref.shape[0]
    groups, _, _, local, narrow = out_ref.shape
    turn_cos, turn_sin = turn_tables(base_cos_ref, base_sin_ref, lane_cos_ref, lane_sin_ref)
    centred = [limbs_ref[i] - jnp.int32(32768) for i in range(number)]
    upper = [lax.shift_right_arithmetic(value, jnp.int32(8)) for value in centred]
    lower = [value - top * jnp.int32(256) for value, top in zip(centred, upper)]
    upper = [value - low for value, low in zip(centred, lower)]
    pieces = jnp.concatenate(upper + lower, axis=1).astype(jnp.float32).astype(jnp.bfloat16)
    products = jnp.dot(matrix_ref[...], pieces, preferred_element_type=jnp.float32)
    count = 2 * half
    width = number * narrow
    upper_part = products[:count, :width] + products[count:, :width]
    lower_part = products[:count, width:] + products[count:, width:]
    rows = upper_part + lower_part
    for i in range(number):
        real_rows = rows[:half, i * narrow : (i + 1) * narrow]
        imag_rows = rows[half:, i * narrow : (i + 1) * narrow]
        out_ref[:, 0, i] = (real_rows * turn_cos - imag_rows * turn_sin).reshape(groups, local, narrow)
        out_ref[:, 1, i] = (real_rows * turn_sin + imag_rows * turn_cos).reshape(groups, local, narrow)


def turn_tables(base_cos_ref, base_sin_ref, lane_cos_ref, lane_sin_ref):
    device = lax.axis_index("row") * lax.axis_size("col") + lax.axis_index("col")
    pick = (lax.broadcasted_iota(jnp.int32, (1, base_cos_ref.shape[1]), 1) == device).astype(jnp.float32)
    base_cos = jnp.sum(base_cos_ref[...] * pick, axis=1, keepdims=True)
    base_sin = jnp.sum(base_sin_ref[...] * pick, axis=1, keepdims=True)
    lane_cos = lane_cos_ref[...]
    lane_sin = lane_sin_ref[...]
    return base_cos * lane_cos - base_sin * lane_sin, base_cos * lane_sin + base_sin * lane_cos


def row_stage(limbs, matrix, tables, groups):
    number, height, narrow = limbs.shape
    half = tables[2].shape[0]
    local = half // groups
    steps = 2
    block = number // steps
    fixed = lambda shape: pl.BlockSpec(shape, lambda s: (0,) * len(shape))
    return pl.pallas_call(
        row_kernel,
        out_shape=jax.ShapeDtypeStruct((groups, 2, number, local, narrow), jnp.float32),
        grid=(steps,),
        in_specs=[pl.BlockSpec((block, height, narrow), lambda s: (s, 0, 0)), fixed(matrix.shape)]
        + [fixed(table.shape) for table in tables],
        out_specs=pl.BlockSpec((groups, 2, block, local, narrow), lambda s: (0, 0, s, 0, 0)),
        cost_estimate=pl.CostEstimate(
            flops=2 * 4 * half * height * 2 * narrow * number,
            transcendentals=0,
            bytes_accessed=4 * 3 * number * height * narrow + 2 * 4 * half * height,
        ),
    )(limbs, matrix, *tables)


def final_kernel(pieces_ref, matrix_ref, base_cos_ref, base_sin_ref, lane_cos_ref, lane_sin_ref, out_ref, *, scale):
    groups, _, outputs, local, narrow = pieces_ref.shape
    half = groups * local
    turn_cos, turn_sin = turn_tables(base_cos_ref, base_sin_ref, lane_cos_ref, lane_sin_ref)
    turn_cos = turn_cos.reshape(groups, local, narrow)
    turn_sin = turn_sin.reshape(groups, local, narrow)
    columns = []
    for i in range(outputs):
        real = pieces_ref[:, 0, i]
        imag = pieces_ref[:, 1, i]
        untwisted = jnp.concatenate(
            (
                (real * turn_cos + imag * turn_sin).reshape(half, narrow),
                (imag * turn_cos - real * turn_sin).reshape(half, narrow),
            ),
            axis=0,
        )
        columns.append(untwisted)
    gathered = jnp.concatenate(columns, axis=1)
    first = gathered.astype(jnp.bfloat16)
    second = (gathered - first.astype(jnp.float32)).astype(jnp.bfloat16)
    height = matrix_ref.shape[0] // 2
    width = outputs * narrow
    leading = jnp.dot(
        matrix_ref[:height], jnp.concatenate((first, second), axis=1), preferred_element_type=jnp.float32
    )
    trailing = jnp.dot(matrix_ref[height:], first, preferred_element_type=jnp.float32)
    small = trailing + leading[:, width:]
    total = small + leading[:, :width]
    for i in range(outputs):
        out_ref[i] = total[:, i * narrow : (i + 1) * narrow]


def final_stage(pieces, matrix, tables, scale):
    groups, _, outputs, local, narrow = pieces.shape
    height = matrix.shape[0] // 2
    return pl.pallas_call(
        functools.partial(final_kernel, scale=scale),
        out_shape=jax.ShapeDtypeStruct((outputs, height, narrow), jnp.float32),
        cost_estimate=pl.CostEstimate(
            flops=2 * 3 * height * height * 2 * outputs * narrow,
            transcendentals=0,
            bytes_accessed=4 * 3 * outputs * height * narrow + 2 * 2 * height * height,
        ),
    )(pieces, matrix, *tables)


def fft16(real, imag, sign):
    def dft4(a, b, c, d):
        sum_ac = (a[0] + c[0], a[1] + c[1])
        dif_ac = (a[0] - c[0], a[1] - c[1])
        sum_bd = (b[0] + d[0], b[1] + d[1])
        dif_bd = (b[0] - d[0], b[1] - d[1])
        return (
            (sum_ac[0] + sum_bd[0], sum_ac[1] + sum_bd[1]),
            (dif_ac[0] - sign * dif_bd[1], dif_ac[1] + sign * dif_bd[0]),
            (sum_ac[0] - sum_bd[0], sum_ac[1] - sum_bd[1]),
            (dif_ac[0] + sign * dif_bd[1], dif_ac[1] - sign * dif_bd[0]),
        )

    values = list(zip(real, imag))
    stage = []
    for first in range(4):
        outs = dft4(*(values[4 * second + first] for second in range(4)))
        turned = []
        for low, (re, im) in enumerate(outs):
            if first * low == 0:
                turned.append((re, im))
                continue
            angle = sign * 2.0 * math.pi * first * low / 16.0
            cos_v, sin_v = math.cos(angle), math.sin(angle)
            turned.append((re * cos_v - im * sin_v, re * sin_v + im * cos_v))
        stage.append(turned)
    result = [None] * 16
    for low in range(4):
        outs = dft4(*(stage[first][low] for first in range(4)))
        for high in range(4):
            result[low + 4 * high] = outs[high]
    return [v[0] for v in result], [v[1] for v in result]


def split_dot(values, matrix_ref):
    size = matrix_ref.shape[0] // 2
    first = values.astype(jnp.bfloat16)
    second = (values - first.astype(jnp.float32)).astype(jnp.bfloat16)
    major = matrix_ref[:size]
    small = jnp.dot(
        jnp.concatenate((second, first), axis=1), matrix_ref[...], preferred_element_type=jnp.float32
    )
    return small + jnp.dot(first, major, preferred_element_type=jnp.float32)


def column_kernel(in_ref, twist_cos_ref, twist_sin_ref, forward_ref, inverse_ref, out_ref, lifted_ref, mixed_ref):
    groups, _, number, local, narrow = in_ref.shape
    tile = 8
    for operand in range(number):
        for start in range(0, local, tile):
            rows = pl.ds(start, tile)
            real = [in_ref[p, 0, operand, rows, :] for p in range(groups)]
            imag = [in_ref[p, 1, operand, rows, :] for p in range(groups)]
            real, imag = fft16(real, imag, -1.0)
            for k in range(groups):
                cos_v = twist_cos_ref[k : k + 1, :]
                sin_v = twist_sin_ref[k : k + 1, :]
                lifted_ref[k, operand, rows, :narrow] = real[k] * cos_v - imag[k] * sin_v
                lifted_ref[k, operand, rows, narrow:] = real[k] * sin_v + imag[k] * cos_v
    spectra = split_dot(
        lifted_ref[...].reshape(groups * number * local, 2 * narrow), forward_ref
    ).reshape(groups, number, local, 2 * narrow)

    def spectrum(k):
        part = spectra[:, k]
        return part[..., :narrow], part[..., narrow:]

    first = multiply_pair(*spectrum(0), *spectrum(3))
    second = multiply_pair(*spectrum(1), *spectrum(4))
    third_a = multiply_pair(*spectrum(2), *spectrum(4))
    third_b = multiply_pair(*spectrum(0), *spectrum(5))
    combined = (first, second, (third_a[0] + third_b[0], third_a[1] + third_b[1]))
    for index, (re, im) in enumerate(combined):
        mixed_ref[:, index, :, :narrow] = re
        mixed_ref[:, index, :, narrow:] = im
    outputs = mixed_ref.shape[1]
    mixed_ref[...] = split_dot(
        mixed_ref[...].reshape(groups * outputs * local, 2 * narrow), inverse_ref
    ).reshape(groups, outputs, local, 2 * narrow)
    for operand in range(outputs):
        for start in range(0, local, tile):
            rows = pl.ds(start, tile)
            real = []
            imag = []
            for k in range(groups):
                re = mixed_ref[k, operand, rows, :narrow]
                im = mixed_ref[k, operand, rows, narrow:]
                cos_v = twist_cos_ref[k : k + 1, :]
                sin_v = twist_sin_ref[k : k + 1, :]
                real.append(re * cos_v + im * sin_v)
                imag.append(im * cos_v - re * sin_v)
            real, imag = fft16(real, imag, 1.0)
            for p in range(groups):
                out_ref[p, 0, operand, rows, :] = real[p]
                out_ref[p, 1, operand, rows, :] = imag[p]


def column_stage(received, twist_cos, twist_sin, forward, inverse):
    groups, _, number, local, narrow = received.shape
    outputs = 3
    rows = groups * local
    steps = 2
    block = local // steps
    fixed = lambda shape: pl.BlockSpec(shape, lambda s: (0,) * len(shape))
    return pl.pallas_call(
        column_kernel,
        out_shape=jax.ShapeDtypeStruct((groups, 2, outputs, local, narrow), jnp.float32),
        grid=(steps,),
        in_specs=[pl.BlockSpec((groups, 2, number, block, narrow), lambda s: (0, 0, 0, s, 0))]
        + [fixed(table.shape) for table in (twist_cos, twist_sin, forward, inverse)],
        out_specs=pl.BlockSpec((groups, 2, outputs, block, narrow), lambda s: (0, 0, 0, s, 0)),
        scratch_shapes=[
            pltpu.VMEM((groups, number, block, 2 * narrow), jnp.float32),
            pltpu.VMEM((groups, outputs, block, 2 * narrow), jnp.float32),
        ],
        cost_estimate=pl.CostEstimate(
            flops=3 * 2 * rows * (number + outputs) * (2 * narrow) ** 2,
            transcendentals=0,
            bytes_accessed=4 * rows * narrow * 2 * (number + outputs),
        ),
    )(received, twist_cos, twist_sin, forward, inverse)


def body(limbs):
    groups = lax.axis_size(("row", "col"))
    number, height, narrow = limbs.shape
    breadth = narrow * groups
    limb_total = height * breadth
    half = height // 2
    local = half // groups
    device = lax.axis_index(("row", "col"))

    half_index = np.arange(half, dtype=np.int64)
    row_index = np.arange(height, dtype=np.int64)
    row_cos_exact, row_sin_exact = exact_phases(
        row_index[None, :] * (2 * half_index[:, None] + 1) % (2 * height), height
    )
    row_matrix = jnp.asarray(split_bf16(np.concatenate((row_cos_exact, row_sin_exact), axis=0) / 32768.0))
    final_matrix = jnp.asarray(
        split_bf16(np.concatenate((row_cos_exact, row_sin_exact), axis=0).T * (2.0 / (limb_total * math.sqrt(limb_total))))
    )
    device_index = np.arange(groups, dtype=np.int64)
    base_cos, base_sin = exact_phases(
        device_index[:, None] * narrow * (2 * half_index[None, :] + 1), limb_total
    )
    base_cos_table = np.zeros((half, narrow))
    base_sin_table = np.zeros((half, narrow))
    base_cos_table[:, :groups] = base_cos.T
    base_sin_table[:, :groups] = base_sin.T
    lane_index = np.arange(narrow, dtype=np.int64)
    lane_cos, lane_sin = exact_phases(lane_index[None, :] * (2 * half_index[:, None] + 1), limb_total)
    tables = (
        constant(base_cos_table),
        constant(base_sin_table),
        constant(lane_cos),
        constant(lane_sin),
    )

    send = row_stage(limbs, row_matrix, tables, groups)
    received = lax.all_to_all(send, ("row", "col"), 0, 0, tiled=True)

    outer_index = np.arange(groups, dtype=np.int64)
    inner_index = np.arange(narrow, dtype=np.int64)
    twist_cos, twist_sin = exact_phases(
        2 * (outer_index[:, None] * inner_index[None, :] % breadth), breadth
    )
    inner_cos, inner_sin = exact_phases(2 * (inner_index[:, None] * inner_index[None, :] % narrow), narrow)
    forward = np.block([[inner_cos, inner_sin], [-inner_sin, inner_cos]])
    inverse = np.block([[inner_cos, -inner_sin], [inner_sin, inner_cos]])
    outgoing = column_stage(
        received,
        constant(twist_cos),
        constant(twist_sin),
        jnp.asarray(split_bf16(forward)),
        jnp.asarray(split_bf16(inverse)),
    )
    pieces = lax.all_to_all(outgoing, ("row", "col"), 0, 0, tiled=True)

    scale_factor = 2.0 / (limb_total * math.sqrt(limb_total))
    return final_stage(pieces, final_matrix, tables, scale_factor)


def solution(mesh):
    in_specs = (P(None, "pair", ("row", "col")),)
    out_specs = P(None, "pair", ("row", "col"))
    return jax.shard_map(body, mesh=mesh, in_specs=in_specs, out_specs=out_specs, check_vma=False)
```
